256 devices in a mesh: freq: 32 (over y_hi, z, core), tm: 4 (over x), grp: 2 (over y_lo).
Axes of the slice: x: 4, y: 4 (y_hi: 2, y_lo: 2; y = y_hi * 2 + y_lo), z: 8, core: 2. Of those that a mesh axis runs over, the one named last changes fastest.
Arguments:
- voltages: bfloat16 [32, 2, 1024, 4096], P(None, None, ('freq', 'grp'), 'tm'), may hold values from -6 to 6
- prior_gains: float32 [32, 2, 1024], P('freq'), may hold values from -4.2 to 4.2
- station_flags: int32 [512], replicated, may hold values 0 or 1
- ingest_map: int32 [512], replicated, may hold values from 0 to 511, each once
- station_coords: float32 [2, 512], replicated, may hold values from -40 to 40
- pointing: int32 [2, 256], replicated, may hold values from 0 to 63
- corr_channels: int32 [32], replicated, may hold values from 0 to 31, each once
- beam_channels: int32 [32], replicated, may hold values from 0 to 31, each once
Outputs:
- visibilities: float32 [32, 2, 1024, 1024], P('freq', None, 'grp', 'tm')
- solved_gains: float32 [32, 2, 1024], P('freq')
- tied_beams: bfloat16 [32, 2, 2, 256, 4096], P('freq', None, None, 'grp', 'tm')
The draws below stay inside these ranges and needn't reach their ends.
Inputs may be any that keep to these rules, and one draw needn't show every extreme that they name: `ingest_map`: each station appears in exactly one ingest slot. `corr_channels`: each channel is handled by exactly one correlator slot. `beam_channels`: each channel is handled by exactly one beamformer slot.
All inputs are finite; a program needn't handle non-finite values.
Results may differ from the reference program's by a relative error of at most 0.0049.
Values may be sent and summed in bfloat16 or wider, within the bound.
No kernel may reach another device: no remote copies, remote signals or barrier semaphores. Data moves between devices by JAX's collectives and lax.ppermute only.
A program may use at most 64 MiB of HBM per device.

```python
import math
import jax
import jax.numpy as jnp
from jax import lax

S = 512
NBEAM = 256
ITERS = 4
NIN = 1024
C = 32
TIME = 4096


def plant(drawn, rng, least, top_value):
    spot = [jax.random.randint(jax.random.fold_in(rng, axis), (), 0, length) for axis, length in enumerate(drawn.shape)]
    longest = drawn.shape.index(max(drawn.shape))
    beside = spot[:longest] + [(spot[longest] + 1) % drawn.shape[longest]] + spot[longest + 1:]
    return drawn.at[tuple(spot)].set(least).at[tuple(beside)].set(top_value)


def block_levels(stream_key, dims, pieces, low, top_value):
    gain, own = 1.0, jax.random.fold_in(stream_key, 6)
    for position, parts in pieces:
        heights = jnp.exp(jax.random.uniform(jax.random.fold_in(own, position), (parts,), jnp.float32, low / len(pieces), top_value / len(pieces)))
        gain = gain * jnp.repeat(heights, dims[position] // parts).reshape([-1 if axis == position else 1 for axis in range(len(dims))])
    return gain


def gaussian(stream_key, dims, spread, most, shards=(), held_as=jnp.bfloat16):
    array = spread * jax.random.normal(stream_key, dims, jnp.float32)
    if shards:
        array = array * block_levels(stream_key, dims, shards, -0.22, 0.18)
    return jnp.clip(array, -most, most).astype(held_as)


def setup_inputs(seed: int = 0) -> dict:
    keys = jax.random.split(jax.random.key(seed), 9)
    return {
        "voltages": gaussian(keys[0], (C, 2, NIN, TIME), 1.0, 6.0, ((2, 64), (3, 4))),
        "prior_gains": gaussian(keys[1], (C, 2, NIN), 0.7, 4.2, ((0, 32),), jnp.float32),
        "station_flags": plant((jax.random.randint(keys[2], (S,), 0, 16) < 1).astype(jnp.int32), jax.random.fold_in(keys[2], 1), 0, 1),
        "ingest_map": jax.random.permutation(keys[3], S).astype(jnp.int32),
        "station_coords": jnp.clip(jax.random.uniform(keys[4], (2, S), jnp.float32, -40.0, 40.0), -40.0, 40.0),
        "pointing": plant(jax.random.randint(keys[5], (2, NBEAM), 0, 64), jax.random.fold_in(keys[5], 1), 0, 63).astype(jnp.int32),
        "corr_channels": jax.random.permutation(keys[6], C).astype(jnp.int32),
        "beam_channels": jax.random.permutation(keys[7], C).astype(jnp.int32),
    }


grid_cells = 64.0

def keep_inputs(station_flags, ingest_map):
    slot_keep = 1 - jnp.take(station_flags, ingest_map)
    return jnp.concatenate([slot_keep, slot_keep]).astype(jnp.bfloat16)

def correlate(block):
    left_real = jnp.concatenate([block[0], block[1]], axis=1)
    left_imag = jnp.concatenate([block[1], -block[0]], axis=1)
    real_part = jnp.dot(left_real, left_real.T, preferred_element_type=jnp.float32)
    imag_part = jnp.dot(left_imag, left_real.T, preferred_element_type=jnp.float32)
    return jnp.stack([real_part, imag_part]) * (1.0 / TIME)

def solve(visibilities, prior_gains):
    gains = prior_gains
    highest = lax.Precision.HIGHEST
    for iteration in range(ITERS):
        power = lax.optimization_barrier(jnp.sum(gains * gains, axis=(1, 2))) + 1e-06
        real_real = jnp.einsum('cij,cj->ci', visibilities[:, 0], gains[:, 0], precision=highest)
        imag_imag = jnp.einsum('cij,cj->ci', visibilities[:, 1], gains[:, 1], precision=highest)
        real_imag = jnp.einsum('cij,cj->ci', visibilities[:, 0], gains[:, 1], precision=highest)
        imag_real = jnp.einsum('cij,cj->ci', visibilities[:, 1], gains[:, 0], precision=highest)
        update = jnp.stack([real_real - imag_imag, imag_real + real_imag], axis=1)
        gains = 0.5 * (gains + 2 * S * update / power[:, None, None])
    return gains

def weights_for(gains_sel, ratio, pointing_part, slot_coords):
    east_dir = (pointing_part[0].astype(jnp.float32) + 0.5) / grid_cells - 0.5
    north_dir = (pointing_part[1].astype(jnp.float32) + 0.5) / grid_cells - 0.5
    phase = 2.0 * math.pi * ratio * (east_dir[:, None] * slot_coords[0][None, :] + north_dir[:, None] * slot_coords[1][None, :])
    cosine = jnp.cos(phase)
    sine = jnp.sin(phase)
    gain_real = gains_sel[0].reshape(2, S)
    gain_imag = gains_sel[1].reshape(2, S)
    denom = jnp.maximum(gain_real * gain_real + gain_imag * gain_imag, 0.5)
    along_real = gain_real / denom
    along_imag = gain_imag / denom
    factor = 1.0 / math.sqrt(S)
    w_real = (cosine[None] * along_real[:, None, :] - sine[None] * along_imag[:, None, :]) * factor
    w_imag = -(cosine[None] * along_imag[:, None, :] + sine[None] * along_real[:, None, :]) * factor
    upper = jnp.stack([w_real, -w_imag], axis=2)
    lower = jnp.stack([w_imag, w_real], axis=2)
    return jnp.stack([upper, lower], axis=1).astype(jnp.bfloat16)

def reference(voltages, prior_gains, station_flags, ingest_map, station_coords, pointing, corr_channels, beam_channels):
    keep = keep_inputs(station_flags, ingest_map)

    def corr_slot(channel):
        block = voltages[channel] * keep[None, :, None]
        return correlate(block)
    visibilities = lax.map(corr_slot, corr_channels)
    solved = solve(visibilities, prior_gains)
    slot_coords = jnp.take(station_coords, ingest_map, axis=1)

    def beam_slot(channel):
        onehot = (corr_channels == channel).astype(jnp.float32)
        gains_sel = jnp.einsum('k,kri->ri', onehot, solved, precision=lax.Precision.HIGHEST)
        ratio = 0.875 + 0.25 * (channel.astype(jnp.float32) + 0.5) / C
        weights = weights_for(gains_sel, ratio, pointing, slot_coords)
        block = (voltages[channel] * keep[None, :, None]).reshape(2, 2, S, TIME)
        beams = jnp.einsum('pobrq,rpqt->pobt', weights.astype(jnp.float32), block.astype(jnp.float32))
        return beams.astype(jnp.bfloat16)
    tied_beams = lax.map(beam_slot, beam_channels)
    return (visibilities, solved, tied_beams)
```

```python
import functools
import math

import jax
import jax.numpy as jnp
from jax import lax
from jax.experimental import pallas as pl
from jax.experimental.pallas import tpu as pltpu
from jax.sharding import PartitionSpec as P

ITERS = 4
GRID_CELLS = 64.0
F32 = jnp.float32
BF16 = jnp.bfloat16
WIDE = ("freq", "grp")
TEAM = ("tm", "grp")
VMEM = pltpu.VMEM
SMEM = pltpu.SMEM


def whole(space=VMEM):
    return pl.BlockSpec(memory_space=space)


def params(mib=48):
    return pltpu.CompilerParams(vmem_limit_bytes=mib << 20)


def ingest_kernel(stations, chan_ref, map_ref, flag_ref, base_ref, volts_ref, out_ref):
    step = pl.program_id(0)
    per_step = out_ref.shape[0]
    rows, half = out_ref.shape[3], out_ref.shape[4]
    line = lax.broadcasted_iota(jnp.int32, (rows, half), 0)
    keep = jnp.zeros((rows, half), F32)
    for row in range(rows):
        slot = lax.rem(base_ref[0] + row, stations)
        good = (1 - flag_ref[map_ref[slot]]).astype(F32)
        keep = jnp.where(line == row, good, keep)
    keep = keep.astype(BF16)
    for i in range(per_step):
        channel = chan_ref[step * per_step + i]
        for part in range(2):
            for g in range(out_ref.shape[1]):
                piece = volts_ref[channel, part, :, g * half : (g + 1) * half]
                out_ref[i, g, part] = piece * keep


def ingest(voltages, channels, ingest_map, station_flags, base, groups):
    slots, parts, rows, samples = voltages.shape
    stations = ingest_map.shape[0]
    per_step = 8
    half = samples // groups
    out = pl.pallas_call(
        functools.partial(ingest_kernel, stations),
        grid=(slots // per_step,),
        in_specs=[whole(SMEM)] * 4 + [whole(VMEM)],
        out_specs=pl.BlockSpec(
            (per_step, groups, parts, rows, half), lambda s: (s, 0, 0, 0, 0)
        ),
        out_shape=jax.ShapeDtypeStruct((slots, groups, parts, rows, half), BF16),
        compiler_params=params(),
        name="ingest",
    )(channels, ingest_map, station_flags, base, voltages)
    return out.reshape(slots * groups, parts, rows, half)


def load_part(ref, part):
    blocks, _, rows, samples = ref.shape
    return ref[:, part].reshape(blocks * rows, samples)


def nt_dot(a, b):
    return lax.dot_general(a, b, (((1,), (1,)), ((), ())), preferred_element_type=F32)


def correlate_kernel(scale, row_blocks, y_ref, out_ref, real_ref, imag_ref):
    col, row = pl.program_id(0), pl.program_id(1)

    @pl.when((col == 0) & (row == 0))
    def _():
        real_ref[...] = load_part(y_ref, 0)
        imag_ref[...] = load_part(y_ref, 1)

    height, width = out_ref.shape[1], out_ref.shape[2]
    rows = pl.ds(pl.multiple_of(row * height, height), height)
    cols = pl.ds(pl.multiple_of(col * width, width), width)
    left_r, left_i = real_ref[rows, :], imag_ref[rows, :]
    right_r, right_i = real_ref[cols, :], imag_ref[cols, :]
    out_ref[0] = ((nt_dot(left_r, right_r) + nt_dot(left_i, right_i)) * scale).astype(BF16)
    out_ref[1] = ((nt_dot(left_i, right_r) - nt_dot(left_r, right_i)) * scale).astype(BF16)


def correlate(y, scale, n_time, n_group):
    blocks, _, rows, samples = y.shape
    inputs = blocks * rows
    height, width = inputs // n_group, inputs // n_time
    return pl.pallas_call(
        functools.partial(correlate_kernel, scale, n_group),
        grid=(n_time, n_group),
        in_specs=[whole(VMEM)],
        out_specs=pl.BlockSpec((2, height, width), lambda t, g: (0, g, t)),
        out_shape=jax.ShapeDtypeStruct((2, inputs, inputs), BF16),
        scratch_shapes=[VMEM((inputs, samples), BF16)] * 2,
        compiler_params=params(),
        name="correlate",
    )(y)


def in_terms(x):
    high = x.astype(BF16).astype(F32)
    rest = x - high
    mid = rest.astype(BF16).astype(F32)
    low = rest - mid
    pad = jnp.zeros_like(x)
    return jnp.concatenate([high, mid, low, pad], axis=0).astype(BF16)


def add_terms(x):
    return x[0:2] + x[2:4] + x[4:6]


def advance(scale, z, partials):
    power = jnp.sum(z * z) + 1e-06
    update = partials[0]
    for i in range(1, partials.shape[0]):
        update = update + partials[i]
    return 0.5 * (z + scale * update / power)


def apply_kernel(scale, first, y_ref, z_ref, *refs):
    z = z_ref[...]
    if first:
        (out_ref,) = refs
    else:
        sums_ref, out_ref, fresh_ref = refs
        z = advance(scale, z, sums_ref[...])
        fresh_ref[...] = z
    real, imag = load_part(y_ref, 0), load_part(y_ref, 1)
    terms = in_terms(z)
    a = add_terms(jnp.dot(terms, real, preferred_element_type=F32))
    b = add_terms(jnp.dot(terms, imag, preferred_element_type=F32))
    w = jnp.concatenate([a[0:1] + b[1:2], a[1:2] - b[0:1]], axis=0)
    terms = in_terms(w)
    c = add_terms(nt_dot(terms, real))
    d = add_terms(nt_dot(terms, imag))
    u = jnp.concatenate([c[0:1] - d[1:2], c[1:2] + d[0:1]], axis=0)
    for i in range(out_ref.shape[0]):
        out_ref[i] = u


def apply_visibilities(y, z, sums, scale, team):
    first = sums is None
    part = jax.ShapeDtypeStruct((team,) + z.shape, F32)
    return pl.pallas_call(
        functools.partial(apply_kernel, scale, first),
        in_specs=[whole(VMEM)] * (2 if first else 3),
        out_specs=whole(VMEM) if first else [whole(VMEM)] * 2,
        out_shape=part if first else [part, jax.ShapeDtypeStruct(z.shape, F32)],
        compiler_params=params(),
        name="apply",
    )(*((y, z) if first else (y, z, sums)))


def finish_kernel(scale, z_ref, sums_ref, fresh_ref, copies_ref):
    z = advance(scale, z_ref[...], sums_ref[...])
    fresh_ref[...] = z
    for i in range(copies_ref.shape[0]):
        copies_ref[i] = z


def finish(z, sums, scale, copies):
    return pl.pallas_call(
        functools.partial(finish_kernel, scale),
        in_specs=[whole(VMEM)] * 2,
        out_specs=[whole(VMEM)] * 2,
        out_shape=[
            jax.ShapeDtypeStruct(z.shape, F32),
            jax.ShapeDtypeStruct((copies,) + z.shape, F32),
        ],
        compiler_params=params(),
        name="finish",
    )(z, sums)


def beam_kernel(corr_ref, beam_ref, me_ref, gains_ref, cos_ref, sin_ref, y_ref, out_ref):
    slots = gains_ref.shape[0]
    mine = beam_ref[me_ref[0]]
    source = jnp.int32(0)
    for k in range(slots):
        source = jnp.where(corr_ref[k] == mine, k, source)
    blocks, _, rows, samples = y_ref.shape
    stations = blocks // 2 * rows
    beams = out_ref.shape[3]
    factor = 1.0 / math.sqrt(stations)
    for pol in range(2):
        chunk = pl.ds(pol * stations, stations)
        gain_r = gains_ref[source, 0:1, chunk]
        gain_i = gains_ref[source, 1:2, chunk]
        denom = jnp.maximum(gain_r * gain_r + gain_i * gain_i, 0.5)
        along_r, along_i = gain_r / denom, gain_i / denom
        y_r = y_ref[pol * blocks // 2 : (pol + 1) * blocks // 2, 0].reshape(stations, samples)
        y_i = y_ref[pol * blocks // 2 : (pol + 1) * blocks // 2, 1].reshape(stations, samples)
        for g in range(out_ref.shape[0]):
            cosine = cos_ref[g * beams : (g + 1) * beams]
            sine = sin_ref[g * beams : (g + 1) * beams]
            w_r = ((cosine * along_r - sine * along_i) * factor).astype(BF16)
            w_i = (-(cosine * along_i + sine * along_r) * factor).astype(BF16)
            dot = functools.partial(jnp.dot, preferred_element_type=F32)
            out_ref[g, pol, 0] = (dot(w_r, y_r) - dot(w_i, y_i)).astype(BF16)
            out_ref[g, pol, 1] = (dot(w_i, y_r) + dot(w_r, y_i)).astype(BF16)


def beamform(corr_channels, beam_channels, me, gains, cosine, sine, y, groups):
    samples = y.shape[3]
    beams = cosine.shape[0] // groups
    return pl.pallas_call(
        beam_kernel,
        in_specs=[whole(SMEM)] * 3 + [whole(VMEM)] * 4,
        out_specs=whole(VMEM),
        out_shape=jax.ShapeDtypeStruct((groups, 2, 2, beams, samples), BF16),
        compiler_params=params(),
        name="beamform",
    )(corr_channels, beam_channels, me, gains, cosine, sine, y)


def swap(x, axis, mask):
    n = lax.axis_size(axis)
    return lax.ppermute(x, axis, [(i, i ^ mask) for i in range(n)])


def exchange(part):
    part = part[0]
    part = part + swap(part, "grp", 1)
    part = part + swap(part, "tm", 1)
    part = part + swap(part, "tm", 2)
    return part[None]


def body(
    voltages,
    prior_gains,
    station_flags,
    ingest_map,
    station_coords,
    pointing,
    corr_channels,
    beam_channels,
):
    n_freq = lax.axis_size("freq")
    n_time = lax.axis_size("tm")
    n_group = lax.axis_size("grp")
    freq_index = lax.axis_index("freq")
    group_index = lax.axis_index("grp")
    slots, _, rows, samples = voltages.shape
    stations = ingest_map.shape[0]
    inputs = 2 * stations
    team = n_time * n_group
    total = samples * n_time

    me = freq_index.astype(jnp.int32).reshape(1)
    base = ((freq_index * n_group + group_index) * rows).astype(jnp.int32).reshape(1)

    corr_send = ingest(voltages, corr_channels, ingest_map, station_flags, base, n_group)
    corr_y = lax.all_to_all(corr_send, WIDE, split_axis=0, concat_axis=0, tiled=True)
    beam_send = ingest(voltages, beam_channels, ingest_map, station_flags, base, n_group)
    beam_send, corr_y = lax.optimization_barrier((beam_send, corr_y))
    beam_y = lax.all_to_all(beam_send, WIDE, split_axis=0, concat_axis=0, tiled=True)

    my_beam = lax.dynamic_slice_in_dim(beam_channels, freq_index, 1, 0)[0]
    ratio = 0.875 + 0.25 * (my_beam.astype(F32) + 0.5) / slots
    slot_coords = jnp.take(station_coords, ingest_map, axis=1, mode="clip")
    east = (pointing[0].astype(F32) + 0.5) / GRID_CELLS - 0.5
    north = (pointing[1].astype(F32) + 0.5) / GRID_CELLS - 0.5
    phase = (2.0 * math.pi * ratio) * (
        east[:, None] * slot_coords[0][None, :] + north[:, None] * slot_coords[1][None, :]
    )
    cosine, sine = jnp.cos(phase), jnp.sin(phase)

    parts = correlate(corr_y, 1.0 / total, n_time, n_group)
    parts = lax.psum_scatter(parts, "tm", scatter_dimension=2, tiled=True)
    parts = lax.psum_scatter(parts, "grp", scatter_dimension=1, tiled=True)
    visibilities = parts.astype(F32)[None]

    z = prior_gains[0]
    scale = float(inputs) / total
    sums = None
    for _ in range(ITERS):
        if sums is None:
            part = apply_visibilities(corr_y, z, None, scale, team)
        else:
            part, z = apply_visibilities(corr_y, z, sums, scale, team)
        sums = exchange(part)
    z, copies = finish(z, sums, scale, n_freq)
    copies, beam_y = lax.optimization_barrier((copies, beam_y))
    all_gains = lax.all_to_all(copies, "freq", split_axis=0, concat_axis=0, tiled=True)

    beams = beamform(
        corr_channels, beam_channels, me, all_gains, cosine, sine, beam_y, n_group
    )
    own = lax.dynamic_index_in_dim(beams, group_index, 0, keepdims=False)
    away = lax.dynamic_index_in_dim(beams, 1 - group_index, 0, keepdims=False)
    other = swap(away, "grp", 1)
    first = jnp.where(group_index == 0, own, other)
    second = jnp.where(group_index == 0, other, own)
    return visibilities, z[None], jnp.concatenate([first, second], axis=3)[None]


def solution(mesh):
    return jax.shard_map(
        body,
        mesh=mesh,
        in_specs=(
            P(None, None, ("freq", "grp"), "tm"),
            P("freq", None, None),
            P(),
            P(),
            P(),
            P(),
            P(),
            P(),
        ),
        out_specs=(
            P("freq", None, "grp", "tm"),
            P("freq", None, None),
            P("freq", None, None, "grp", "tm"),
        ),
        check_vma=False,
    )
```

```python
import functools
import math

import jax
import jax.numpy as jnp
from jax import lax
from jax.experimental import pallas as pl
from jax.experimental.pallas import tpu as pltpu
from jax.sharding import PartitionSpec as P

ITERS = 4
GRID_CELLS = 64.0
F32 = jnp.float32
BF16 = jnp.bfloat16
WIDE = ("freq", "grp")
TEAM = ("tm", "grp")
VMEM = pltpu.VMEM
SMEM = pltpu.SMEM


def whole(space=VMEM):
    return pl.BlockSpec(memory_space=space)


def params(mib=48):
    return pltpu.CompilerParams(vmem_limit_bytes=mib << 20)


def ingest_kernel(
    stations,
    pick,
    base_ref,
    chan_hbm,
    map_hbm,
    flag_hbm,
    volts_hbm,
    out_hbm,
    chan_ref,
    map_ref,
    flag_ref,
    volts_ref,
    out_ref,
    table_sem,
    volts_sem,
    out_sem,
):
    slots, groups, _, rows, half = out_ref.shape
    steps = out_sem.shape[0]
    per_step = slots // steps
    load = pltpu.make_async_copy(volts_hbm, volts_ref, volts_sem)
    load.start()
    tables = [
        pltpu.make_async_copy(source, target, table_sem.at[i])
        for i, (source, target) in enumerate(
            ((chan_hbm, chan_ref), (map_hbm, map_ref), (flag_hbm, flag_ref))
        )
    ]
    for copy in tables:
        copy.start()
    for copy in tables:
        copy.wait()
    line = lax.broadcasted_iota(jnp.int32, (rows, half), 0)
    keep = jnp.zeros((rows, half), F32)
    for row in range(rows):
        slot = lax.rem(base_ref[0] + row, stations)
        good = (1 - flag_ref[map_ref[slot]]).astype(F32)
        keep = jnp.where(line == row, good, keep)
    keep = keep.astype(BF16)
    load.wait()
    stores = []
    for step in range(steps):
        for slot in range(step * per_step, (step + 1) * per_step):
            for g in range(groups):
                index, cut = pick(slot, g)
                channel = chan_ref[index]
                for part in range(2):
                    piece = volts_ref[channel, part, :, cut * half : (cut + 1) * half]
                    out_ref[slot, g, part] = piece * keep
        span = pl.ds(step * per_step, per_step)
        store = pltpu.make_async_copy(out_ref.at[span], out_hbm.at[span], out_sem.at[step])
        store.start()
        stores.append(store)
    for store in stores:
        store.wait()


def ingest(voltages, channels, ingest_map, station_flags, base, groups, pick):
    slots, parts, rows, samples = voltages.shape
    stations = ingest_map.shape[0]
    half = samples // 2
    shape = (slots, groups, parts, rows, half)
    steps = 8
    out = pl.pallas_call(
        functools.partial(ingest_kernel, stations, pick),
        in_specs=[whole(SMEM)] + [whole(pltpu.HBM)] * 4,
        out_specs=whole(pltpu.HBM),
        out_shape=jax.ShapeDtypeStruct(shape, BF16),
        scratch_shapes=[
            SMEM(channels.shape, jnp.int32),
            SMEM(ingest_map.shape, jnp.int32),
            SMEM(station_flags.shape, jnp.int32),
            VMEM(voltages.shape, BF16),
            VMEM(shape, BF16),
            pltpu.SemaphoreType.DMA((3,)),
            pltpu.SemaphoreType.DMA,
            pltpu.SemaphoreType.DMA((steps,)),
        ],
        compiler_params=params(62),
        name="ingest",
    )(base, channels, ingest_map, station_flags, voltages)
    return out.reshape(slots * groups, parts, rows, half)


def load_part(ref, part):
    blocks, _, rows, samples = ref.shape
    return ref[:, part].reshape(blocks * rows, samples)


def nt_dot(a, b):
    return lax.dot_general(a, b, (((1,), (1,)), ((), ())), preferred_element_type=F32)


def correlate_kernel(scale, y_ref, out_ref, left_ref, turn_ref):
    row, col = pl.program_id(0), pl.program_id(1)
    samples = y_ref.shape[3]

    @pl.when((col == 0) & (row == 0))
    def _():
        real, imag = load_part(y_ref, 0), load_part(y_ref, 1)
        left_ref[:, :samples] = real
        left_ref[:, samples:] = imag
        turn_ref[:, :samples] = imag
        turn_ref[:, samples:] = -real

    height, width = out_ref.shape[1], out_ref.shape[2]
    rows = pl.ds(pl.multiple_of(row * height, height), height)
    cols = pl.ds(pl.multiple_of(col * width, width), width)
    right = left_ref[cols, :]
    out_ref[0] = (nt_dot(left_ref[rows, :], right) * scale).astype(BF16)
    out_ref[1] = (nt_dot(turn_ref[rows, :], right) * scale).astype(BF16)


def correlate(y, scale):
    blocks, _, rows, samples = y.shape
    inputs = blocks * rows
    height, width = inputs // 2, inputs // 4
    return pl.pallas_call(
        functools.partial(correlate_kernel, scale),
        grid=(inputs // height, inputs // width),
        in_specs=[whole(VMEM)],
        out_specs=pl.BlockSpec((2, height, width), lambda i, j: (0, i, j)),
        out_shape=jax.ShapeDtypeStruct((2, inputs, inputs), BF16),
        scratch_shapes=[VMEM((inputs, 2 * samples), BF16)] * 2,
        compiler_params=params(60),
        name="correlate",
    )(y)


def in_terms(x):
    high = x.astype(BF16).astype(F32)
    rest = x - high
    mid = rest.astype(BF16).astype(F32)
    low = rest - mid
    pad = jnp.zeros_like(x)
    return jnp.concatenate([high, mid, low, pad], axis=0).astype(BF16)


def add_terms(x):
    return x[0:2] + x[2:4] + x[4:6]


def advance(scale, z, update):
    power = jnp.sum(z * z) + 1e-06
    return 0.5 * (z + scale * update / power)


def apply_kernel(scale, first, y_ref, z_ref, *refs):
    z = z_ref[...]
    if first:
        (out_ref,) = refs
    else:
        near_ref, far_ref, out_ref, fresh_ref = refs
        z = advance(scale, z, near_ref[...] + far_ref[...])
        fresh_ref[...] = z
    real, imag = load_part(y_ref, 0), load_part(y_ref, 1)
    terms = in_terms(z)
    a = add_terms(jnp.dot(terms, real, preferred_element_type=F32))
    b = add_terms(jnp.dot(terms, imag, preferred_element_type=F32))
    w = jnp.concatenate([a[0:1] + b[1:2], a[1:2] - b[0:1]], axis=0)
    terms = in_terms(w)
    c = add_terms(nt_dot(terms, real))
    d = add_terms(nt_dot(terms, imag))
    out_ref[...] = jnp.concatenate([c[0:1] - d[1:2], c[1:2] + d[0:1]], axis=0)


def apply_visibilities(y, z, sums, scale):
    first = sums is None
    vector = jax.ShapeDtypeStruct(z.shape, F32)
    return pl.pallas_call(
        functools.partial(apply_kernel, scale, first),
        in_specs=[whole(VMEM)] * (2 if first else 4),
        out_specs=whole(VMEM) if first else [whole(VMEM)] * 2,
        out_shape=vector if first else [vector] * 2,
        compiler_params=params(16),
        name="apply",
    )(y, z, *(sums or ()))


def finish_kernel(scale, z_ref, near_ref, far_ref, fresh_ref, copies_ref):
    z = advance(scale, z_ref[...], near_ref[...] + far_ref[...])
    fresh_ref[...] = z
    for i in range(copies_ref.shape[0]):
        copies_ref[i] = z


def finish(z, sums, scale, copies):
    return pl.pallas_call(
        functools.partial(finish_kernel, scale),
        in_specs=[whole(VMEM)] * 3,
        out_specs=[whole(VMEM)] * 2,
        out_shape=[
            jax.ShapeDtypeStruct(z.shape, F32),
            jax.ShapeDtypeStruct((copies,) + z.shape, F32),
        ],
        compiler_params=params(8),
        name="finish",
    )(z, *sums)


def find_slot(corr_ref, channel):
    slot = jnp.int32(0)
    for k in range(corr_ref.shape[0]):
        slot = jnp.where(corr_ref[k] == channel, k, slot)
    return slot


def choose_kernel(reach, corr_ref, beam_ref, me_ref, line_ref, *out_refs):
    column, chip = me_ref[0] // 2, me_ref[0]
    for (high, _), out_ref in zip(reach, out_refs):
        peer = chip ^ (high * 2 * line_ref.shape[0])
        slot = find_slot(corr_ref, beam_ref[peer])
        out_ref[...] = line_ref[(slot // 2) % line_ref.shape[0]]


def choose(corr_channels, beam_channels, me, line, reach):
    vector = jax.ShapeDtypeStruct(line.shape[1:], F32)
    return pl.pallas_call(
        functools.partial(choose_kernel, reach),
        in_specs=[whole(SMEM)] * 3 + [whole(VMEM)],
        out_specs=[whole(VMEM)] * len(reach),
        out_shape=[vector] * len(reach),
        compiler_params=params(8),
        name="choose",
    )(corr_channels, beam_channels, me, line)


def beam_kernel(
    reach, corr_ref, beam_ref, me_ref, *refs
):
    gain_refs, (cos_ref, sin_ref, y_ref, out_ref) = refs[: len(reach)], refs[len(reach) :]
    slot = find_slot(corr_ref, beam_ref[me_ref[0]])
    half_ring = corr_ref.shape[0] // 2
    far = (slot // half_ring) ^ (me_ref[0] // half_ring)
    side = (slot % 2) ^ me_ref[1]
    gains = gain_refs[0][...]
    for (high, low), ref in zip(reach[1:], gain_refs[1:]):
        hit = ((far == high) & (side == low)).astype(jnp.int32)
        gains = jnp.where(jnp.full(gains.shape, hit) == 1, ref[...], gains)
    blocks, _, rows, samples = y_ref.shape
    stations = blocks // 2 * rows
    beams = out_ref.shape[3]
    factor = 1.0 / math.sqrt(stations)
    for pol in range(2):
        gain_r = gains[0:1, pol * stations : (pol + 1) * stations]
        gain_i = gains[1:2, pol * stations : (pol + 1) * stations]
        denom = jnp.maximum(gain_r * gain_r + gain_i * gain_i, 0.5)
        along_r, along_i = gain_r / denom, gain_i / denom
        y_r = y_ref[pol * blocks // 2 : (pol + 1) * blocks // 2, 0].reshape(stations, samples)
        y_i = y_ref[pol * blocks // 2 : (pol + 1) * blocks // 2, 1].reshape(stations, samples)
        for g in range(out_ref.shape[0]):
            cosine = cos_ref[g * beams : (g + 1) * beams]
            sine = sin_ref[g * beams : (g + 1) * beams]
            w_r = ((cosine * along_r - sine * along_i) * factor).astype(BF16)
            w_i = (-(cosine * along_i + sine * along_r) * factor).astype(BF16)
            dot = functools.partial(jnp.dot, preferred_element_type=F32)
            out_ref[g, pol, 0] = (dot(w_r, y_r) - dot(w_i, y_i)).astype(BF16)
            out_ref[g, pol, 1] = (dot(w_i, y_r) + dot(w_r, y_i)).astype(BF16)


def beamform(reach, corr_channels, beam_channels, me, gains, cosine, sine, y, groups):
    samples = y.shape[3]
    beams = cosine.shape[0] // groups
    return pl.pallas_call(
        functools.partial(beam_kernel, reach),
        in_specs=[whole(SMEM)] * 3 + [whole(VMEM)] * (3 + len(reach)),
        out_specs=whole(VMEM),
        out_shape=jax.ShapeDtypeStruct((groups, 2, 2, beams, samples), BF16),
        compiler_params=params(24),
        name="beamform",
    )(corr_channels, beam_channels, me, *gains, cosine, sine, y)


def swap(x, axis, mask):
    n = lax.axis_size(axis)
    return lax.ppermute(x, axis, [(i, i ^ mask) for i in range(n)])


def exchange(part):
    part = part + swap(part, "freq", 1)
    part = part + swap(part, "tm", 1)
    return part, swap(part, "tm", 3)


def cross(x, turn):
    pairs = []
    for i in range(lax.axis_size("freq") // 2):
        for core in range(2):
            for g in range(2):
                pairs.append(((2 * i + core) * 2 + g, (2 * i + g) * 2 + (core ^ turn)))
    return lax.ppermute(x, WIDE, pairs)


def body(
    voltages,
    prior_gains,
    station_flags,
    ingest_map,
    station_coords,
    pointing,
    corr_channels,
    beam_channels,
):
    n_freq = lax.axis_size("freq")
    n_time = lax.axis_size("tm")
    n_group = lax.axis_size("grp")
    freq_index = lax.axis_index("freq")
    group_index = lax.axis_index("grp")
    slots, _, rows, samples = voltages.shape
    stations = ingest_map.shape[0]
    inputs = 2 * stations
    total = samples * n_time
    core = freq_index % 2

    me = jnp.stack([freq_index, group_index]).astype(jnp.int32)
    base = ((freq_index * n_group + group_index) * rows).astype(jnp.int32).reshape(1)

    corr_send = ingest(
        voltages, corr_channels, ingest_map, station_flags, base, n_group,
        lambda slot, g: (slot // 2 * 2 + g, slot % 2),
    )
    corr_y = lax.all_to_all(corr_send, WIDE, split_axis=0, concat_axis=0, tiled=True)
    beam_send = ingest(
        voltages, beam_channels, ingest_map, station_flags, base, n_group,
        lambda slot, g: (slot, g),
    )
    z = cross(prior_gains[0], 0)
    beam_send, corr_y, z = lax.optimization_barrier((beam_send, corr_y, z))
    beam_y = lax.all_to_all(beam_send, WIDE, split_axis=0, concat_axis=0, tiled=True)

    my_beam = lax.dynamic_slice_in_dim(beam_channels, freq_index, 1, 0)[0]
    ratio = 0.875 + 0.25 * (my_beam.astype(F32) + 0.5) / slots
    slot_coords = jnp.take(station_coords, ingest_map, axis=1, mode="clip")
    east = (pointing[0].astype(F32) + 0.5) / GRID_CELLS - 0.5
    north = (pointing[1].astype(F32) + 0.5) / GRID_CELLS - 0.5
    phase = (2.0 * math.pi * ratio) * (
        east[:, None] * slot_coords[0][None, :] + north[:, None] * slot_coords[1][None, :]
    )
    cosine, sine = jnp.cos(phase), jnp.sin(phase)

    parts = correlate(corr_y, 1.0 / total)
    parts = lax.psum_scatter(parts, "tm", scatter_dimension=2, tiled=True)
    height = inputs // n_group
    near = lax.dynamic_slice_in_dim(parts, core * height, height, 1)
    far = lax.dynamic_slice_in_dim(parts, (1 - core) * height, height, 1)
    near, far = cross(near, 0), cross(far, 1)

    scale = float(inputs) / total
    sums = None
    for _ in range(ITERS):
        if sums is None:
            part = apply_visibilities(corr_y, z, None, scale)
        else:
            part, z = apply_visibilities(corr_y, z, sums, scale)
        sums = exchange(part)
    depth = slots // 4
    z, copies = finish(z, sums, scale, depth)
    copies, beam_y, cosine, sine = lax.optimization_barrier((copies, beam_y, cosine, sine))
    line = [
        [high * 2 * depth + 2 * i + c for i in range(depth)]
        for high in range(2)
        for c in range(2)
    ]
    line = lax.all_to_all(
        copies, "freq", split_axis=0, concat_axis=0, axis_index_groups=line, tiled=True
    )
    reach = [(0, 0), (0, 1), (1, 0), (1, 1)]
    picks = choose(corr_channels, beam_channels, me, line, reach)
    gains = [picks[0]] + [
        swap(pick, WIDE, high * 8 * depth // 2 + low)
        for (high, low), pick in zip(reach[1:], picks[1:])
    ]
    solved = cross(z, 0)
    gains, near, far, solved = lax.optimization_barrier((gains, near, far, solved))
    visibilities = (near.astype(F32) + far.astype(F32))[None]

    beams = beamform(
        reach, corr_channels, beam_channels, me, gains, cosine, sine, beam_y, n_group
    )
    own = lax.dynamic_index_in_dim(beams, group_index, 0, keepdims=False)
    away = lax.dynamic_index_in_dim(beams, 1 - group_index, 0, keepdims=False)
    other = swap(away, "grp", 1)
    first = jnp.where(group_index == 0, own, other)
    second = jnp.where(group_index == 0, other, own)
    return visibilities, solved[None], jnp.concatenate([first, second], axis=3)[None]


def solution(mesh):
    return jax.shard_map(
        body,
        mesh=mesh,
        in_specs=(
            P(None, None, ("freq", "grp"), "tm"),
            P("freq", None, None),
            P(),
            P(),
            P(),
            P(),
            P(),
            P(),
        ),
        out_specs=(
            P("freq", None, "grp", "tm"),
            P("freq", None, None),
            P("freq", None, None, "grp", "tm"),
        ),
        check_vma=False,
    )
```

```python
import functools
import math

import jax
import jax.numpy as jnp
from jax import lax
from jax.experimental import pallas as pl
from jax.experimental.pallas import tpu as pltpu
from jax.sharding import PartitionSpec as P

ITERS = 4
GRID_CELLS = 64.0
F32 = jnp.float32
BF16 = jnp.bfloat16
WIDE = ("freq", "grp")
TEAM = ("tm", "grp")
VMEM = pltpu.VMEM
SMEM = pltpu.SMEM


def whole(space=VMEM):
    return pl.BlockSpec(memory_space=space)


def params(mib=48):
    return pltpu.CompilerParams(vmem_limit_bytes=mib << 20)


def ingest_kernel(
    stations,
    pick,
    base_ref,
    chan_hbm,
    map_hbm,
    flag_hbm,
    volts_hbm,
    out_hbm,
    chan_ref,
    map_ref,
    flag_ref,
    volts_ref,
    out_ref,
    table_sem,
    volts_sem,
    out_sem,
):
    slots, groups, _, rows, half = out_ref.shape
    steps = out_sem.shape[0]
    per_step = slots // steps
    load = pltpu.make_async_copy(volts_hbm, volts_ref, volts_sem)
    load.start()
    tables = [
        pltpu.make_async_copy(source, target, table_sem.at[i])
        for i, (source, target) in enumerate(
            ((chan_hbm, chan_ref), (map_hbm, map_ref), (flag_hbm, flag_ref))
        )
    ]
    for copy in tables:
        copy.start()
    for copy in tables:
        copy.wait()
    line = lax.broadcasted_iota(jnp.int32, (rows, half), 0)
    keep = jnp.zeros((rows, half), F32)
    for row in range(rows):
        slot = lax.rem(base_ref[0] + row, stations)
        good = (1 - flag_ref[map_ref[slot]]).astype(F32)
        keep = jnp.where(line == row, good, keep)
    keep = keep.astype(BF16)
    load.wait()
    stores = []
    for step in range(steps):
        for slot in range(step * per_step, (step + 1) * per_step):
            for g in range(groups):
                index, cut = pick(slot, g)
                channel = chan_ref[index]
                for part in range(2):
                    piece = volts_ref[channel, part, :, cut * half : (cut + 1) * half]
                    out_ref[slot, g, part] = piece * keep
        span = pl.ds(step * per_step, per_step)
        store = pltpu.make_async_copy(out_ref.at[span], out_hbm.at[span], out_sem.at[step])
        store.start()
        stores.append(store)
    for store in stores:
        store.wait()


def ingest(voltages, channels, ingest_map, station_flags, base, groups, pick, grant):
    slots, parts, rows, samples = voltages.shape
    stations = ingest_map.shape[0]
    half = samples // 2
    shape = (slots, groups, parts, rows, half)
    steps = 8
    out = pl.pallas_call(
        functools.partial(ingest_kernel, stations, pick),
        in_specs=[whole(SMEM)] + [whole(pltpu.HBM)] * 4,
        out_specs=whole(pltpu.HBM),
        out_shape=pltpu.HBM(shape, BF16),
        scratch_shapes=[
            SMEM(channels.shape, jnp.int32),
            SMEM(ingest_map.shape, jnp.int32),
            SMEM(station_flags.shape, jnp.int32),
            VMEM(voltages.shape, BF16),
            VMEM(shape, BF16),
            pltpu.SemaphoreType.DMA((3,)),
            pltpu.SemaphoreType.DMA,
            pltpu.SemaphoreType.DMA((steps,)),
        ],
        compiler_params=params(grant),
        name="ingest",
    )(
        base,
        *(
            pltpu.with_memory_space_constraint(x, pltpu.HBM)
            for x in (channels, ingest_map, station_flags, voltages)
        ),
    )
    return out.reshape(slots * groups, parts, rows, half)


def load_part(ref, part):
    blocks, _, rows, samples = ref.shape
    return ref[:, part].reshape(blocks * rows, samples)


def nt_dot(a, b):
    return lax.dot_general(a, b, (((1,), (1,)), ((), ())), preferred_element_type=F32)


def correlate_kernel(
    scale, side_ref, y_ref, near_hbm, far_hbm, left_ref, turn_ref, out_ref, sems
):
    samples = y_ref.shape[3]
    inputs = left_ref.shape[0]
    blocks = sems.shape[0]
    tile = inputs // blocks
    half = blocks // 2
    real, imag = load_part(y_ref, 0), load_part(y_ref, 1)
    left_ref[:, :samples] = real
    left_ref[:, samples:] = imag
    turn_ref[:, :samples] = imag
    turn_ref[:, samples:] = -real

    def store(b, target):
        source = out_ref.at[:, pl.ds(b * tile, tile)]
        return pltpu.make_async_copy(
            source, target.at[:, pl.ds(b % half * tile, tile)], sems.at[b]
        )

    for b in reversed(range(blocks)):
        height = (b + 1) * tile
        cols = slice(b * tile, height)
        right = left_ref[cols, :]
        real = nt_dot(left_ref[:height, :], right) * scale
        imag = nt_dot(turn_ref[:height, :], right) * scale
        out_ref[0, :height, cols] = real.astype(BF16)
        out_ref[1, :height, cols] = imag.astype(BF16)
        for a in range(b):
            rows = slice(a * tile, (a + 1) * tile)
            out_ref[0, cols, rows] = real[rows].T.astype(BF16)
            out_ref[1, cols, rows] = (-imag[rows].T).astype(BF16)

        @pl.when(side_ref[0] == b // half)
        def _():
            store(b, near_hbm).start()

        @pl.when(side_ref[0] != b // half)
        def _():
            store(b, far_hbm).start()

    for b in reversed(range(blocks)):
        store(b, near_hbm).wait()


def correlate(y, side, scale):
    blocks, _, rows, samples = y.shape
    inputs = blocks * rows
    tiles = 4
    out = pltpu.HBM((2, inputs // 2, inputs), BF16)
    return pl.pallas_call(
        functools.partial(correlate_kernel, scale),
        in_specs=[whole(SMEM), whole(VMEM)],
        out_specs=[whole(pltpu.HBM)] * 2,
        out_shape=[out] * 2,
        scratch_shapes=[VMEM((inputs, 2 * samples), BF16)] * 2
        + [VMEM((2, inputs, inputs), BF16), pltpu.SemaphoreType.DMA((tiles,))],
        compiler_params=params(28),
        name="correlate",
    )(side, y)


def in_terms(x):
    high = x.astype(BF16).astype(F32)
    rest = x - high
    mid = rest.astype(BF16).astype(F32)
    low = rest - mid
    pad = jnp.zeros_like(x)
    return jnp.concatenate([high, mid, low, pad], axis=0).astype(BF16)


def add_terms(x):
    return x[0:2] + x[2:4] + x[4:6]


def advance(scale, z, update):
    power = jnp.sum(z * z) + 1e-06
    return 0.5 * (z + scale * update / power)


def apply_kernel(scale, first, y_ref, z_ref, *refs):
    z = z_ref[...]
    if first:
        (out_ref,) = refs
    else:
        near_ref, far_ref, out_ref, fresh_ref = refs
        z = advance(scale, z, near_ref[...] + far_ref[...])
        fresh_ref[...] = z
    real, imag = load_part(y_ref, 0), load_part(y_ref, 1)
    terms = in_terms(z)
    a = add_terms(jnp.dot(terms, real, preferred_element_type=F32))
    b = add_terms(jnp.dot(terms, imag, preferred_element_type=F32))
    w = jnp.concatenate([a[0:1] + b[1:2], a[1:2] - b[0:1]], axis=0)
    terms = in_terms(w)
    c = add_terms(nt_dot(terms, real))
    d = add_terms(nt_dot(terms, imag))
    out_ref[...] = jnp.concatenate([c[0:1] - d[1:2], c[1:2] + d[0:1]], axis=0)


def apply_visibilities(y, z, sums, scale):
    first = sums is None
    vector = jax.ShapeDtypeStruct(z.shape, F32)
    return pl.pallas_call(
        functools.partial(apply_kernel, scale, first),
        in_specs=[whole(VMEM)] * (2 if first else 4),
        out_specs=whole(VMEM) if first else [whole(VMEM)] * 2,
        out_shape=vector if first else [vector] * 2,
        compiler_params=params(16),
        name="apply",
    )(y, z, *(sums or ()))


def finish_kernel(scale, z_ref, near_ref, far_ref, fresh_ref, copies_ref):
    z = advance(scale, z_ref[...], near_ref[...] + far_ref[...])
    fresh_ref[...] = z
    for i in range(copies_ref.shape[0]):
        copies_ref[i] = z


def finish(z, sums, scale, copies):
    return pl.pallas_call(
        functools.partial(finish_kernel, scale),
        in_specs=[whole(VMEM)] * 3,
        out_specs=[whole(VMEM)] * 2,
        out_shape=[
            jax.ShapeDtypeStruct(z.shape, F32),
            jax.ShapeDtypeStruct((copies,) + z.shape, F32),
        ],
        compiler_params=params(8),
        name="finish",
    )(z, *sums)


def find_slot(corr_ref, channel):
    slot = jnp.int32(0)
    for k in range(corr_ref.shape[0]):
        slot = jnp.where(corr_ref[k] == channel, k, slot)
    return slot


def choose_kernel(reach, corr_ref, beam_ref, me_ref, line_ref, *out_refs):
    column, chip = me_ref[0] // 2, me_ref[0]
    for (high, _), out_ref in zip(reach, out_refs):
        peer = chip ^ (high * 2 * line_ref.shape[0])
        slot = find_slot(corr_ref, beam_ref[peer])
        out_ref[...] = line_ref[(slot // 2) % line_ref.shape[0]]


def choose(corr_channels, beam_channels, me, line, reach):
    vector = jax.ShapeDtypeStruct(line.shape[1:], F32)
    return pl.pallas_call(
        functools.partial(choose_kernel, reach),
        in_specs=[whole(SMEM)] * 3 + [whole(VMEM)],
        out_specs=[whole(VMEM)] * len(reach),
        out_shape=[vector] * len(reach),
        compiler_params=params(8),
        name="choose",
    )(corr_channels, beam_channels, me, line)


def beam_kernel(
    reach, corr_ref, beam_ref, me_ref, *refs
):
    gain_refs, (cos_ref, sin_ref, y_ref, *out_refs) = refs[: len(reach)], refs[len(reach) :]
    slot = find_slot(corr_ref, beam_ref[me_ref[0]])
    half_ring = corr_ref.shape[0] // 2
    far = (slot // half_ring) ^ (me_ref[0] // half_ring)
    side = (slot % 2) ^ me_ref[1]
    gains = gain_refs[0][...]
    for (high, low), ref in zip(reach[1:], gain_refs[1:]):
        hit = ((far == high) & (side == low)).astype(jnp.int32)
        gains = jnp.where(jnp.full(gains.shape, hit) == 1, ref[...], gains)
    blocks, _, rows, samples = y_ref.shape
    stations = blocks // 2 * rows
    beams = out_refs[0].shape[2]
    factor = 1.0 / math.sqrt(stations)
    for pol in range(2):
        gain_r = gains[0:1, pol * stations : (pol + 1) * stations]
        gain_i = gains[1:2, pol * stations : (pol + 1) * stations]
        denom = jnp.maximum(gain_r * gain_r + gain_i * gain_i, 0.5)
        along_r, along_i = gain_r / denom, gain_i / denom
        y_r = y_ref[pol * blocks // 2 : (pol + 1) * blocks // 2, 0].reshape(stations, samples)
        y_i = y_ref[pol * blocks // 2 : (pol + 1) * blocks // 2, 1].reshape(stations, samples)
        for turn, out_ref in enumerate(out_refs):
            half = pl.ds(pl.multiple_of((me_ref[1] ^ turn) * beams, beams), beams)
            cosine, sine = cos_ref[half, :], sin_ref[half, :]
            w_r = ((cosine * along_r - sine * along_i) * factor).astype(BF16)
            w_i = (-(cosine * along_i + sine * along_r) * factor).astype(BF16)
            dot = functools.partial(jnp.dot, preferred_element_type=F32)
            out_ref[pol, 0] = (dot(w_r, y_r) - dot(w_i, y_i)).astype(BF16)
            out_ref[pol, 1] = (dot(w_i, y_r) + dot(w_r, y_i)).astype(BF16)


def beamform(reach, corr_channels, beam_channels, me, gains, cosine, sine, y, groups):
    samples = y.shape[3]
    beams = cosine.shape[0] // groups
    return pl.pallas_call(
        functools.partial(beam_kernel, reach),
        in_specs=[whole(SMEM)] * 3 + [whole(VMEM)] * (3 + len(reach)),
        out_specs=[whole(VMEM)] * groups,
        out_shape=[jax.ShapeDtypeStruct((2, 2, beams, samples), BF16)] * groups,
        compiler_params=params(16),
        name="beamform",
    )(corr_channels, beam_channels, me, *gains, cosine, sine, y)


def swap(x, axis, mask):
    n = lax.axis_size(axis)
    return lax.ppermute(x, axis, [(i, i ^ mask) for i in range(n)])


def exchange(part):
    part = part + swap(part, "freq", 1)
    part = part + swap(part, "tm", 1)
    return part, swap(part, "tm", 3)


def cross(x, turn):
    pairs = []
    for i in range(lax.axis_size("freq") // 2):
        for core in range(2):
            for g in range(2):
                pairs.append(((2 * i + core) * 2 + g, (2 * i + g) * 2 + (core ^ turn)))
    return lax.ppermute(x, WIDE, pairs)


def body(
    voltages,
    prior_gains,
    station_flags,
    ingest_map,
    station_coords,
    pointing,
    corr_channels,
    beam_channels,
):
    n_freq = lax.axis_size("freq")
    n_time = lax.axis_size("tm")
    n_group = lax.axis_size("grp")
    freq_index = lax.axis_index("freq")
    group_index = lax.axis_index("grp")
    slots, _, rows, samples = voltages.shape
    stations = ingest_map.shape[0]
    inputs = 2 * stations
    total = samples * n_time
    core = freq_index % 2

    me = jnp.stack([freq_index, group_index]).astype(jnp.int32)
    base = ((freq_index * n_group + group_index) * rows).astype(jnp.int32).reshape(1)

    corr_send = ingest(
        voltages, corr_channels, ingest_map, station_flags, base, n_group,
        lambda slot, g: (slot // 2 * 2 + g, slot % 2), 16,
    )
    corr_y = lax.all_to_all(corr_send, WIDE, split_axis=0, concat_axis=0, tiled=True)
    beam_send = ingest(
        voltages, beam_channels, ingest_map, station_flags, base, n_group,
        lambda slot, g: (slot, g), 16,
    )
    my_beam = lax.dynamic_slice_in_dim(beam_channels, freq_index, 1, 0)[0]
    ratio = 0.875 + 0.25 * (my_beam.astype(F32) + 0.5) / slots
    slot_coords = jnp.take(station_coords, ingest_map, axis=1, mode="clip")
    east = (pointing[0].astype(F32) + 0.5) / GRID_CELLS - 0.5
    north = (pointing[1].astype(F32) + 0.5) / GRID_CELLS - 0.5
    phase = (2.0 * math.pi * ratio) * (
        east[:, None] * slot_coords[0][None, :] + north[:, None] * slot_coords[1][None, :]
    )
    cosine, sine = jnp.cos(phase), jnp.sin(phase)

    z = cross(prior_gains[0], 0)
    beam_send, corr_y, z, cosine, sine = lax.optimization_barrier(
        (beam_send, corr_y, z, cosine, sine)
    )
    beam_y = lax.all_to_all(beam_send, WIDE, split_axis=0, concat_axis=0, tiled=True)

    near, far = (
        lax.psum_scatter(part, "tm", scatter_dimension=2, tiled=True)
        for part in correlate(corr_y, core.astype(jnp.int32).reshape(1), 1.0 / total)
    )

    scale = float(inputs) / total
    sums = None
    for _ in range(ITERS):
        if sums is None:
            part = apply_visibilities(corr_y, z, None, scale)
        else:
            part, z = apply_visibilities(corr_y, z, sums, scale)
        sums = exchange(part)
    depth = slots // 4
    z, copies = finish(z, sums, scale, depth)
    copies, beam_y, near, far = lax.optimization_barrier((copies, beam_y, near, far))
    near, far = cross(near, 0), cross(far, 1)
    line = [
        [high * 2 * depth + 2 * i + c for i in range(depth)]
        for high in range(2)
        for c in range(2)
    ]
    line = lax.all_to_all(
        copies, "freq", split_axis=0, concat_axis=0, axis_index_groups=line, tiled=True
    )
    reach = [(0, 0), (0, 1), (1, 0), (1, 1)]
    picks = choose(corr_channels, beam_channels, me, line, reach)
    gains = [picks[0]] + [
        swap(pick, WIDE, high * 8 * depth // 2 + low)
        for (high, low), pick in zip(reach[1:], picks[1:])
    ]
    solved = cross(z, 0)
    gains, near, far = lax.optimization_barrier((gains, near, far))
    visibilities = (near.astype(F32) + far.astype(F32))[None]

    own, away = beamform(
        reach, corr_channels, beam_channels, me, gains, cosine, sine, beam_y, n_group
    )
    other = swap(away, "grp", 1)
    first = jnp.where(group_index == 0, own, other)
    second = jnp.where(group_index == 0, other, own)
    return visibilities, solved[None], jnp.concatenate([first, second], axis=3)[None]


def solution(mesh):
    return jax.shard_map(
        body,
        mesh=mesh,
        in_specs=(
            P(None, None, ("freq", "grp"), "tm"),
            P("freq", None, None),
            P(),
            P(),
            P(),
            P(),
            P(),
            P(),
        ),
        out_specs=(
            P("freq", None, "grp", "tm"),
            P("freq", None, None),
            P("freq", None, None, "grp", "tm"),
        ),
        check_vma=False,
    )
```

```python
import functools
import math

import jax
import jax.numpy as jnp
from jax import lax
from jax.experimental import pallas as pl
from jax.experimental.pallas import tpu as pltpu
from jax.sharding import PartitionSpec as P

ITERS = 4
GRID_CELLS = 64.0
F32 = jnp.float32
BF16 = jnp.bfloat16
WIDE = ("freq", "grp")
TEAM = ("tm", "grp")
VMEM = pltpu.VMEM
SMEM = pltpu.SMEM


def whole(space=VMEM):
    return pl.BlockSpec(memory_space=space)


def params(mib=48):
    return pltpu.CompilerParams(vmem_limit_bytes=mib << 20)


def ingest_kernel(
    stations,
    pick,
    base_ref,
    chan_hbm,
    map_hbm,
    flag_hbm,
    volts_hbm,
    out_hbm,
    chan_ref,
    map_ref,
    flag_ref,
    volts_ref,
    out_ref,
    table_sem,
    volts_sem,
    out_sem,
):
    slots, groups, _, rows, half = out_ref.shape
    steps = out_sem.shape[0]
    per_step = slots // steps
    load = pltpu.make_async_copy(volts_hbm, volts_ref, volts_sem)
    load.start()
    tables = [
        pltpu.make_async_copy(source, target, table_sem.at[i])
        for i, (source, target) in enumerate(
            ((chan_hbm, chan_ref), (map_hbm, map_ref), (flag_hbm, flag_ref))
        )
    ]
    for copy in tables:
        copy.start()
    for copy in tables:
        copy.wait()
    line = lax.broadcasted_iota(jnp.int32, (rows, half), 0)
    keep = jnp.zeros((rows, half), F32)
    for row in range(rows):
        slot = lax.rem(base_ref[0] + row, stations)
        good = (1 - flag_ref[map_ref[slot]]).astype(F32)
        keep = jnp.where(line == row, good, keep)
    keep = keep.astype(BF16)
    load.wait()
    stores = []
    for step in range(steps):
        for slot in range(step * per_step, (step + 1) * per_step):
            for g in range(groups):
                index, cut = pick(slot, g)
                channel = chan_ref[index]
                for part in range(2):
                    piece = volts_ref[channel, part, :, cut * half : (cut + 1) * half]
                    out_ref[slot, g, part] = piece * keep
        span = pl.ds(step * per_step, per_step)
        store = pltpu.make_async_copy(out_ref.at[span], out_hbm.at[span], out_sem.at[step])
        store.start()
        stores.append(store)
    for store in stores:
        store.wait()


def ingest(voltages, channels, ingest_map, station_flags, base, groups, pick, grant):
    slots, parts, rows, samples = voltages.shape
    stations = ingest_map.shape[0]
    half = samples // 2
    shape = (slots, groups, parts, rows, half)
    steps = 8
    out = pl.pallas_call(
        functools.partial(ingest_kernel, stations, pick),
        in_specs=[whole(SMEM)] + [whole(pltpu.HBM)] * 4,
        out_specs=whole(pltpu.HBM),
        out_shape=pltpu.HBM(shape, BF16),
        scratch_shapes=[
            SMEM(channels.shape, jnp.int32),
            SMEM(ingest_map.shape, jnp.int32),
            SMEM(station_flags.shape, jnp.int32),
            VMEM(voltages.shape, BF16),
            VMEM(shape, BF16),
            pltpu.SemaphoreType.DMA((3,)),
            pltpu.SemaphoreType.DMA,
            pltpu.SemaphoreType.DMA((steps,)),
        ],
        compiler_params=params(grant),
        name="ingest",
    )(
        base,
        *(
            pltpu.with_memory_space_constraint(x, pltpu.HBM)
            for x in (channels, ingest_map, station_flags, voltages)
        ),
    )
    return out.reshape(slots * groups, parts, rows, half)


def load_part(ref, part):
    blocks, _, rows, samples = ref.shape
    return ref[:, part].reshape(blocks * rows, samples)


def nt_dot(a, b):
    return lax.dot_general(a, b, (((1,), (1,)), ((), ())), preferred_element_type=F32)


def correlate_kernel(
    scale, side_ref, y_ref, out_hbm, left_ref, turn_ref, out_ref, sems
):
    samples = y_ref.shape[3]
    inputs = left_ref.shape[0]
    blocks = sems.shape[0]
    tile = inputs // blocks
    half = blocks // 2
    real, imag = load_part(y_ref, 0), load_part(y_ref, 1)
    left_ref[:, :samples] = real
    left_ref[:, samples:] = imag
    turn_ref[:, :samples] = imag
    turn_ref[:, samples:] = -real

    def store(b, far):
        source = out_ref.at[:, pl.ds(b * tile, tile)]
        target = out_hbm.at[far, :, pl.ds(b % half * tile, tile)]
        return pltpu.make_async_copy(source, target, sems.at[b])

    for b in reversed(range(blocks)):
        height = (b + 1) * tile
        cols = slice(b * tile, height)
        right = left_ref[cols, :]
        real = nt_dot(left_ref[:height, :], right) * scale
        imag = nt_dot(turn_ref[:height, :], right) * scale
        out_ref[0, :height, cols] = real.astype(BF16)
        out_ref[1, :height, cols] = imag.astype(BF16)
        for a in range(b):
            rows = slice(a * tile, (a + 1) * tile)
            out_ref[0, cols, rows] = real[rows].T.astype(BF16)
            out_ref[1, cols, rows] = (-imag[rows].T).astype(BF16)

        @pl.when(side_ref[0] == b // half)
        def _():
            store(b, 0).start()

        @pl.when(side_ref[0] != b // half)
        def _():
            store(b, 1).start()

    for b in reversed(range(blocks)):
        store(b, 0).wait()


def correlate(y, side, scale):
    blocks, _, rows, samples = y.shape
    inputs = blocks * rows
    tiles = 4
    out = pltpu.HBM((2, 2, inputs // 2, inputs), BF16)
    return pl.pallas_call(
        functools.partial(correlate_kernel, scale),
        in_specs=[whole(SMEM), whole(VMEM)],
        out_specs=whole(pltpu.HBM),
        out_shape=out,
        scratch_shapes=[VMEM((inputs, 2 * samples), BF16)] * 2
        + [VMEM((2, inputs, inputs), BF16), pltpu.SemaphoreType.DMA((tiles,))],
        compiler_params=params(28),
        name="correlate",
    )(side, y)


def in_terms(x):
    high = x.astype(BF16).astype(F32)
    rest = x - high
    mid = rest.astype(BF16).astype(F32)
    low = rest - mid
    pad = jnp.zeros_like(x)
    return jnp.concatenate([high, mid, low, pad], axis=0).astype(BF16)


def add_terms(x):
    return x[0:2] + x[2:4] + x[4:6]


def advance(scale, z, update):
    power = jnp.sum(z * z) + 1e-06
    return 0.5 * (z + scale * update / power)


def apply_kernel(scale, first, y_ref, z_ref, *refs):
    z = z_ref[...]
    if first:
        (out_ref,) = refs
    else:
        near_ref, far_ref, out_ref, fresh_ref = refs
        z = advance(scale, z, near_ref[...] + far_ref[...])
        fresh_ref[...] = z
    real, imag = load_part(y_ref, 0), load_part(y_ref, 1)
    terms = in_terms(z)
    a = add_terms(jnp.dot(terms, real, preferred_element_type=F32))
    b = add_terms(jnp.dot(terms, imag, preferred_element_type=F32))
    w = jnp.concatenate([a[0:1] + b[1:2], a[1:2] - b[0:1]], axis=0)
    terms = in_terms(w)
    c = add_terms(nt_dot(terms, real))
    d = add_terms(nt_dot(terms, imag))
    out_ref[...] = jnp.concatenate([c[0:1] - d[1:2], c[1:2] + d[0:1]], axis=0)


def apply_visibilities(y, z, sums, scale):
    first = sums is None
    vector = jax.ShapeDtypeStruct(z.shape, F32)
    return pl.pallas_call(
        functools.partial(apply_kernel, scale, first),
        in_specs=[whole(VMEM)] * (2 if first else 4),
        out_specs=whole(VMEM) if first else [whole(VMEM)] * 2,
        out_shape=vector if first else [vector] * 2,
        compiler_params=params(16),
        name="apply",
    )(y, z, *(sums or ()))


def finish_kernel(scale, z_ref, near_ref, far_ref, fresh_ref, copies_ref):
    z = advance(scale, z_ref[...], near_ref[...] + far_ref[...])
    fresh_ref[...] = z
    for i in range(copies_ref.shape[0]):
        copies_ref[i] = z


def finish(z, sums, scale, copies):
    return pl.pallas_call(
        functools.partial(finish_kernel, scale),
        in_specs=[whole(VMEM)] * 3,
        out_specs=[whole(VMEM)] * 2,
        out_shape=[
            jax.ShapeDtypeStruct(z.shape, F32),
            jax.ShapeDtypeStruct((copies,) + z.shape, F32),
        ],
        compiler_params=params(8),
        name="finish",
    )(z, *sums)


def find_slot(corr_ref, channel):
    slot = jnp.int32(0)
    for k in range(corr_ref.shape[0]):
        slot = jnp.where(corr_ref[k] == channel, k, slot)
    return slot


def choose_kernel(reach, corr_ref, beam_ref, me_ref, line_ref, *out_refs):
    column, chip = me_ref[0] // 2, me_ref[0]
    for (high, _), out_ref in zip(reach, out_refs):
        peer = chip ^ (high * 2 * line_ref.shape[0])
        slot = find_slot(corr_ref, beam_ref[peer])
        out_ref[...] = line_ref[(slot // 2) % line_ref.shape[0]]


def choose(corr_channels, beam_channels, me, line, reach):
    vector = jax.ShapeDtypeStruct(line.shape[1:], F32)
    return pl.pallas_call(
        functools.partial(choose_kernel, reach),
        in_specs=[whole(SMEM)] * 3 + [whole(VMEM)],
        out_specs=[whole(VMEM)] * len(reach),
        out_shape=[vector] * len(reach),
        compiler_params=params(8),
        name="choose",
    )(corr_channels, beam_channels, me, line)


def beam_kernel(
    reach, corr_ref, beam_ref, me_ref, *refs
):
    gain_refs = refs[: len(reach)]
    cos_ref, sin_ref, y_ref, own_hbm, away_ref, own_ref, sems = refs[len(reach) :]
    out_refs = (own_ref, away_ref)
    slot = find_slot(corr_ref, beam_ref[me_ref[0]])
    half_ring = corr_ref.shape[0] // 2
    far = (slot // half_ring) ^ (me_ref[0] // half_ring)
    side = (slot % 2) ^ me_ref[1]
    gains = gain_refs[0][...]
    for (high, low), ref in zip(reach[1:], gain_refs[1:]):
        hit = ((far == high) & (side == low)).astype(jnp.int32)
        gains = jnp.where(jnp.full(gains.shape, hit) == 1, ref[...], gains)
    blocks, _, rows, samples = y_ref.shape
    stations = blocks // 2 * rows
    beams = away_ref.shape[2]
    factor = 1.0 / math.sqrt(stations)
    span = pl.ds(pl.multiple_of(me_ref[1] * samples, samples), samples)
    stores = []
    for pol in range(2):
        gain_r = gains[0:1, pol * stations : (pol + 1) * stations]
        gain_i = gains[1:2, pol * stations : (pol + 1) * stations]
        denom = jnp.maximum(gain_r * gain_r + gain_i * gain_i, 0.5)
        along_r, along_i = gain_r / denom, gain_i / denom
        y_r = y_ref[pol * blocks // 2 : (pol + 1) * blocks // 2, 0].reshape(stations, samples)
        y_i = y_ref[pol * blocks // 2 : (pol + 1) * blocks // 2, 1].reshape(stations, samples)
        for turn, out_ref in enumerate(out_refs):
            half = pl.ds(pl.multiple_of((me_ref[1] ^ turn) * beams, beams), beams)
            cosine, sine = cos_ref[half, :], sin_ref[half, :]
            w_r = ((cosine * along_r - sine * along_i) * factor).astype(BF16)
            w_i = (-(cosine * along_i + sine * along_r) * factor).astype(BF16)
            dot = functools.partial(jnp.dot, preferred_element_type=F32)
            out_ref[pol, 0] = (dot(w_r, y_r) - dot(w_i, y_i)).astype(BF16)
            out_ref[pol, 1] = (dot(w_i, y_r) + dot(w_r, y_i)).astype(BF16)
            if turn == 0:
                store = pltpu.make_async_copy(
                    own_ref.at[pol], own_hbm.at[pol, :, :, span], sems.at[pol]
                )
                store.start()
                stores.append(store)
    for store in stores:
        store.wait()


def beamform(reach, corr_channels, beam_channels, me, gains, cosine, sine, y, groups):
    samples = y.shape[3]
    beams = cosine.shape[0] // groups
    shape = (2, 2, beams, samples)
    return pl.pallas_call(
        functools.partial(beam_kernel, reach),
        in_specs=[whole(SMEM)] * 3 + [whole(VMEM)] * (3 + len(reach)),
        out_specs=[whole(pltpu.HBM), whole(VMEM)],
        out_shape=[
            pltpu.HBM((2, 2, beams, groups * samples), BF16),
            jax.ShapeDtypeStruct(shape, BF16),
        ],
        scratch_shapes=[VMEM(shape, BF16), pltpu.SemaphoreType.DMA((2,))],
        compiler_params=params(16),
        name="beamform",
    )(corr_channels, beam_channels, me, *gains, cosine, sine, y)


def place_kernel(me_ref, own_hbm, other_ref, out_hbm, sem):
    samples = other_ref.shape[3]
    span = pl.ds(pl.multiple_of((1 - me_ref[1]) * samples, samples), samples)
    store = pltpu.make_async_copy(other_ref, out_hbm.at[:, :, :, span], sem)
    store.start()
    store.wait()


def place(me, own, other):
    return pl.pallas_call(
        place_kernel,
        in_specs=[whole(SMEM), whole(pltpu.HBM), whole(pl.ANY)],
        out_specs=whole(pltpu.HBM),
        out_shape=pltpu.HBM(own.shape, BF16),
        scratch_shapes=[pltpu.SemaphoreType.DMA],
        input_output_aliases={1: 0},
        compiler_params=params(8),
        name="place",
    )(me, own, other)


def join_kernel(near_ref, far_ref, z_ref, vis_ref, solved_ref):
    vis_ref[...] = near_ref[...].astype(F32) + far_ref[...].astype(F32)

    @pl.when(pl.program_id(0) == 0)
    def _():
        solved_ref[...] = z_ref[...]


def join(near, far, z):
    parts, rows, cols = near.shape
    steps = 4
    block = pl.BlockSpec((parts, rows // steps, cols), lambda i: (0, i, 0))
    fixed = pl.BlockSpec(z.shape, lambda i: (0, 0))
    near, far = (pltpu.with_memory_space_constraint(x, pltpu.HBM) for x in (near, far))
    return pl.pallas_call(
        join_kernel,
        grid=(steps,),
        in_specs=[block, block, fixed],
        out_specs=[block, fixed],
        out_shape=[pltpu.HBM(near.shape, F32), pltpu.HBM(z.shape, F32)],
        compiler_params=params(8),
        name="join",
    )(near, far, z)


def swap(x, axis, mask):
    n = lax.axis_size(axis)
    return lax.ppermute(x, axis, [(i, i ^ mask) for i in range(n)])


def exchange(part):
    part = part + swap(part, "freq", 1)
    part = part + swap(part, "tm", 1)
    return part, swap(part, "tm", 3)


def cross(x, turn):
    pairs = []
    for i in range(lax.axis_size("freq") // 2):
        for core in range(2):
            for g in range(2):
                pairs.append(((2 * i + core) * 2 + g, (2 * i + g) * 2 + (core ^ turn)))
    return lax.ppermute(x, WIDE, pairs)


def body(
    voltages,
    prior_gains,
    station_flags,
    ingest_map,
    station_coords,
    pointing,
    corr_channels,
    beam_channels,
):
    n_freq = lax.axis_size("freq")
    n_time = lax.axis_size("tm")
    n_group = lax.axis_size("grp")
    freq_index = lax.axis_index("freq")
    group_index = lax.axis_index("grp")
    slots, _, rows, samples = voltages.shape
    stations = ingest_map.shape[0]
    inputs = 2 * stations
    total = samples * n_time
    core = freq_index % 2

    me = jnp.stack([freq_index, group_index]).astype(jnp.int32)
    base = ((freq_index * n_group + group_index) * rows).astype(jnp.int32).reshape(1)

    corr_send = ingest(
        voltages, corr_channels, ingest_map, station_flags, base, n_group,
        lambda slot, g: (slot // 2 * 2 + g, slot % 2), 16,
    )
    corr_y = lax.all_to_all(corr_send, WIDE, split_axis=0, concat_axis=0, tiled=True)
    beam_send = ingest(
        voltages, beam_channels, ingest_map, station_flags, base, n_group,
        lambda slot, g: (slot, g), 16,
    )
    my_beam = lax.dynamic_slice_in_dim(beam_channels, freq_index, 1, 0)[0]
    ratio = 0.875 + 0.25 * (my_beam.astype(F32) + 0.5) / slots
    slot_coords = jnp.take(station_coords, ingest_map, axis=1, mode="clip")
    east = (pointing[0].astype(F32) + 0.5) / GRID_CELLS - 0.5
    north = (pointing[1].astype(F32) + 0.5) / GRID_CELLS - 0.5
    phase = (2.0 * math.pi * ratio) * (
        east[:, None] * slot_coords[0][None, :] + north[:, None] * slot_coords[1][None, :]
    )
    cosine, sine = jnp.cos(phase), jnp.sin(phase)

    z = cross(prior_gains[0], 0)
    beam_send, corr_y, z, cosine, sine = lax.optimization_barrier(
        (beam_send, corr_y, z, cosine, sine)
    )
    beam_y = lax.all_to_all(beam_send, WIDE, split_axis=0, concat_axis=0, tiled=True)

    scale = float(inputs) / total
    part = apply_visibilities(corr_y, z, None, scale)

    halves = correlate(corr_y, core.astype(jnp.int32).reshape(1), 1.0 / total)
    halves = lax.psum_scatter(halves, "tm", scatter_dimension=3, tiled=True)

    sums = exchange(part)
    for _ in range(ITERS - 1):
        part, z = apply_visibilities(corr_y, z, sums, scale)
        sums = exchange(part)
    depth = slots // 4
    z, copies = finish(z, sums, scale, depth)
    z, halves = lax.optimization_barrier((z, halves))
    near, far, solved = cross(halves[0], 0), cross(halves[1], 1), cross(z, 0)
    copies, beam_y = lax.optimization_barrier((copies, beam_y))
    line = [
        [high * 2 * depth + 2 * i + c for i in range(depth)]
        for high in range(2)
        for c in range(2)
    ]
    line = lax.all_to_all(
        copies, "freq", split_axis=0, concat_axis=0, axis_index_groups=line, tiled=True
    )
    reach = [(0, 0), (0, 1), (1, 0), (1, 1)]
    picks = choose(corr_channels, beam_channels, me, line, reach)
    gains = [picks[0]] + [
        swap(pick, WIDE, high * 8 * depth // 2 + low)
        for (high, low), pick in zip(reach[1:], picks[1:])
    ]
    gains, near, far, solved = lax.optimization_barrier((gains, near, far, solved))
    visibilities, solved = join(near, far, solved)

    own, away = beamform(
        reach, corr_channels, beam_channels, me, gains, cosine, sine, beam_y, n_group
    )
    beams = place(me, own, swap(away, "grp", 1))
    return visibilities[None], solved[None], beams[None]


def solution(mesh):
    return jax.shard_map(
        body,
        mesh=mesh,
        in_specs=(
            P(None, None, ("freq", "grp"), "tm"),
            P("freq", None, None),
            P(),
            P(),
            P(),
            P(),
            P(),
            P(),
        ),
        out_specs=(
            P("freq", None, "grp", "tm"),
            P("freq", None, None),
            P("freq", None, None, "grp", "tm"),
        ),
        check_vma=False,
    )
```

```python
import functools
import math

import jax
import jax.numpy as jnp
from jax import lax
from jax.experimental import pallas as pl
from jax.experimental.pallas import tpu as pltpu
from jax.sharding import PartitionSpec as P

ITERS = 4
GRID_CELLS = 64.0
F32 = jnp.float32
BF16 = jnp.bfloat16
WIDE = ("freq", "grp")
TEAM = ("tm", "grp")
VMEM = pltpu.VMEM
SMEM = pltpu.SMEM


def whole(space=VMEM):
    return pl.BlockSpec(memory_space=space)


def params(mib=48):
    return pltpu.CompilerParams(vmem_limit_bytes=mib << 20)


def ingest_kernel(
    stations,
    pick,
    base_ref,
    chan_hbm,
    map_hbm,
    flag_hbm,
    volts_hbm,
    out_hbm,
    chan_ref,
    map_ref,
    flag_ref,
    volts_ref,
    out_ref,
    table_sem,
    volts_sem,
    out_sem,
):
    slots, groups, _, rows, half = out_ref.shape
    steps = out_sem.shape[0]
    per_step = slots // steps
    load = pltpu.make_async_copy(volts_hbm, volts_ref, volts_sem)
    load.start()
    tables = [
        pltpu.make_async_copy(source, target, table_sem.at[i])
        for i, (source, target) in enumerate(
            ((chan_hbm, chan_ref), (map_hbm, map_ref), (flag_hbm, flag_ref))
        )
    ]
    for copy in tables:
        copy.start()
    for copy in tables:
        copy.wait()
    line = lax.broadcasted_iota(jnp.int32, (rows, half), 0)
    keep = jnp.zeros((rows, half), F32)
    for row in range(rows):
        slot = lax.rem(base_ref[0] + row, stations)
        good = (1 - flag_ref[map_ref[slot]]).astype(F32)
        keep = jnp.where(line == row, good, keep)
    keep = keep.astype(BF16)
    load.wait()
    stores = []
    for step in range(steps):
        for slot in range(step * per_step, (step + 1) * per_step):
            for g in range(groups):
                index, cut = pick(slot, g)
                channel = chan_ref[index]
                for part in range(2):
                    piece = volts_ref[channel, part, :, cut * half : (cut + 1) * half]
                    out_ref[slot, g, part] = piece * keep
        span = pl.ds(step * per_step, per_step)
        store = pltpu.make_async_copy(out_ref.at[span], out_hbm.at[span], out_sem.at[step])
        store.start()
        stores.append(store)
    for store in stores:
        store.wait()


def ingest(voltages, channels, ingest_map, station_flags, base, groups, pick, grant):
    slots, parts, rows, samples = voltages.shape
    stations = ingest_map.shape[0]
    half = samples // 2
    shape = (slots, groups, parts, rows, half)
    steps = 8
    out = pl.pallas_call(
        functools.partial(ingest_kernel, stations, pick),
        in_specs=[whole(SMEM)] + [whole(pltpu.HBM)] * 4,
        out_specs=whole(pltpu.HBM),
        out_shape=pltpu.HBM(shape, BF16),
        scratch_shapes=[
            SMEM(channels.shape, jnp.int32),
            SMEM(ingest_map.shape, jnp.int32),
            SMEM(station_flags.shape, jnp.int32),
            VMEM(voltages.shape, BF16),
            VMEM(shape, BF16),
            pltpu.SemaphoreType.DMA((3,)),
            pltpu.SemaphoreType.DMA,
            pltpu.SemaphoreType.DMA((steps,)),
        ],
        compiler_params=params(grant),
        name="ingest",
    )(
        base,
        *(
            pltpu.with_memory_space_constraint(x, pltpu.HBM)
            for x in (channels, ingest_map, station_flags, voltages)
        ),
    )
    return out.reshape(slots * groups, parts, rows, half)


def load_part(ref, part):
    blocks, _, rows, samples = ref.shape
    return ref[:, part].reshape(blocks * rows, samples)


def nt_dot(a, b):
    return lax.dot_general(a, b, (((1,), (1,)), ((), ())), preferred_element_type=F32)


def correlate_kernel(scale, me_ref, y_ref, *refs):
    samples = y_ref.shape[3]
    *out_hbms, left_ref, turn_ref, out_ref, sems = refs
    inputs = left_ref.shape[0]
    blocks = sems.shape[0]
    tile, half = inputs // blocks, inputs // 2
    core, time = me_ref[0] % 2, me_ref[2]
    real, imag = load_part(y_ref, 0), load_part(y_ref, 1)
    left_ref[:, :samples] = real
    left_ref[:, samples:] = imag
    turn_ref[:, :samples] = imag
    turn_ref[:, samples:] = -real

    def store(b, side, target):
        source = out_ref.at[:, side * half : (side + 1) * half, b * tile : (b + 1) * tile]
        return pltpu.make_async_copy(source, target.at[core ^ side], sems.at[b, side])

    for b in reversed(range(blocks)):
        height = (b + 1) * tile
        cols = slice(b * tile, height)
        right = left_ref[cols, :]
        real = nt_dot(left_ref[:height, :], right) * scale
        imag = nt_dot(turn_ref[:height, :], right) * scale
        out_ref[0, :height, cols] = real.astype(BF16)
        out_ref[1, :height, cols] = imag.astype(BF16)
        for a in range(b):
            rows = slice(a * tile, (a + 1) * tile)
            out_ref[0, cols, rows] = real[rows].T.astype(BF16)
            out_ref[1, cols, rows] = (-imag[rows].T).astype(BF16)
        for mask, target in enumerate(out_hbms):

            @pl.when((time ^ mask) == b)
            def _(b=b, target=target):
                store(b, 0, target).start()
                store(b, 1, target).start()

    for b in reversed(range(blocks)):
        for side in range(2):
            store(b, side, out_hbms[0]).wait()


def correlate(y, me, scale, n_time):
    blocks, _, rows, samples = y.shape
    inputs = blocks * rows
    out = pltpu.HBM((2, 2, inputs // 2, inputs // n_time), BF16)
    return pl.pallas_call(
        functools.partial(correlate_kernel, scale),
        in_specs=[whole(SMEM), whole(VMEM)],
        out_specs=[whole(pltpu.HBM)] * n_time,
        out_shape=[out] * n_time,
        scratch_shapes=[VMEM((inputs, 2 * samples), BF16)] * 2
        + [VMEM((2, inputs, inputs), BF16), pltpu.SemaphoreType.DMA((n_time, 2))],
        compiler_params=params(28),
        name="correlate",
    )(me, y)


def gather_kernel(*refs):
    *part_refs, near_ref, far_ref = refs
    for side, out_ref in enumerate((near_ref, far_ref)):
        pieces = [ref[side].astype(F32) for ref in part_refs]
        out_ref[...] = ((pieces[0] + pieces[1]) + (pieces[2] + pieces[3])).astype(BF16)


def gather(pieces):
    _, parts, rows, cols = pieces[0].shape
    steps = 4
    return pl.pallas_call(
        gather_kernel,
        grid=(steps,),
        in_specs=[pl.BlockSpec((2, parts, rows // steps, cols), lambda i: (0, 0, i, 0))]
        * len(pieces),
        out_specs=[pl.BlockSpec((parts, rows // steps, cols), lambda i: (0, i, 0))] * 2,
        out_shape=[pltpu.HBM((parts, rows, cols), BF16)] * 2,
        compiler_params=params(16),
        name="gather",
    )(*pieces)


def in_terms(x):
    high = x.astype(BF16).astype(F32)
    rest = x - high
    mid = rest.astype(BF16).astype(F32)
    low = rest - mid
    pad = jnp.zeros_like(x)
    return jnp.concatenate([high, mid, low, pad], axis=0).astype(BF16)


def add_terms(x):
    return x[0:2] + x[2:4] + x[4:6]


def advance(scale, z, update):
    power = jnp.sum(z * z) + 1e-06
    return 0.5 * (z + scale * update / power)


def apply_kernel(scale, first, y_ref, z_ref, *refs):
    z = z_ref[...]
    if first:
        (out_ref,) = refs
    else:
        near_ref, far_ref, out_ref, fresh_ref = refs
        z = advance(scale, z, near_ref[...] + far_ref[...])
        fresh_ref[...] = z
    real, imag = load_part(y_ref, 0), load_part(y_ref, 1)
    terms = in_terms(z)
    a = add_terms(jnp.dot(terms, real, preferred_element_type=F32))
    b = add_terms(jnp.dot(terms, imag, preferred_element_type=F32))
    w = jnp.concatenate([a[0:1] + b[1:2], a[1:2] - b[0:1]], axis=0)
    terms = in_terms(w)
    c = add_terms(nt_dot(terms, real))
    d = add_terms(nt_dot(terms, imag))
    out_ref[...] = jnp.concatenate([c[0:1] - d[1:2], c[1:2] + d[0:1]], axis=0)


def apply_visibilities(y, z, sums, scale):
    first = sums is None
    vector = jax.ShapeDtypeStruct(z.shape, F32)
    return pl.pallas_call(
        functools.partial(apply_kernel, scale, first),
        in_specs=[whole(VMEM)] * (2 if first else 4),
        out_specs=whole(VMEM) if first else [whole(VMEM)] * 2,
        out_shape=vector if first else [vector] * 2,
        compiler_params=params(16),
        name="apply",
    )(y, z, *(sums or ()))


def finish_kernel(scale, z_ref, near_ref, far_ref, fresh_ref):
    fresh_ref[...] = advance(scale, z_ref[...], near_ref[...] + far_ref[...])


def finish(z, sums, scale):
    return pl.pallas_call(
        functools.partial(finish_kernel, scale),
        in_specs=[whole(VMEM)] * 3,
        out_specs=whole(VMEM),
        out_shape=jax.ShapeDtypeStruct(z.shape, F32),
        compiler_params=params(8),
        name="finish",
    )(z, *sums)


def choose_kernel(reach, source_ref, me_ref, *refs):
    z_refs, (copies_ref, solved_ref) = refs[: len(reach)], refs[len(reach) :]
    depth = copies_ref.shape[0]
    chip, grp = me_ref[0], me_ref[1]
    core, high_half = chip % 2, chip // (2 * depth)
    vectors = [ref[...] for ref in z_refs]
    own = jnp.full(vectors[0].shape, (core == grp).astype(jnp.int32)) == 1
    solved_ref[...] = jnp.where(own, vectors[0], vectors[1])
    for i in range(depth):
        slot = source_ref[high_half * 2 * depth + 2 * i + core]
        far, side = (slot // (2 * depth)) ^ high_half, (slot % 2) ^ grp
        which = jnp.full(vectors[0].shape, 2 * far + side)
        chosen = vectors[0]
        for (high, low), vector in zip(reach[1:], vectors[1:]):
            chosen = jnp.where(which == 2 * high + low, vector, chosen)
        copies_ref[i] = chosen


def choose(source, me, vectors, reach, depth):
    shape = vectors[0].shape
    return pl.pallas_call(
        functools.partial(choose_kernel, reach),
        in_specs=[whole(SMEM)] * 2 + [whole(VMEM)] * len(reach),
        out_specs=[whole(VMEM)] * 2,
        out_shape=[
            jax.ShapeDtypeStruct((depth,) + shape, F32),
            jax.ShapeDtypeStruct(shape, F32),
        ],
        compiler_params=params(8),
        name="choose",
    )(source, me, *vectors)


def beam_kernel(turn, source_ref, me_ref, line_ref, cos_ref, sin_ref, y_ref, *refs):
    out_ref = refs[0] if turn else refs[1]
    slot = source_ref[me_ref[0]]
    gains = line_ref[(slot // 2) % line_ref.shape[0]]
    blocks, _, rows, samples = y_ref.shape
    stations = blocks // 2 * rows
    beams = out_ref.shape[2]
    factor = 1.0 / math.sqrt(stations)
    half = pl.ds(pl.multiple_of((me_ref[1] ^ turn) * beams, beams), beams)
    cosine, sine = cos_ref[half, :], sin_ref[half, :]
    span = pl.ds(pl.multiple_of(me_ref[1] * samples, samples), samples)
    dot = functools.partial(jnp.dot, preferred_element_type=F32)
    stores = []
    for pol in range(2):
        gain_r = gains[0:1, pol * stations : (pol + 1) * stations]
        gain_i = gains[1:2, pol * stations : (pol + 1) * stations]
        denom = jnp.maximum(gain_r * gain_r + gain_i * gain_i, 0.5)
        along_r, along_i = gain_r / denom, gain_i / denom
        y_r = y_ref[pol * blocks // 2 : (pol + 1) * blocks // 2, 0].reshape(stations, samples)
        y_i = y_ref[pol * blocks // 2 : (pol + 1) * blocks // 2, 1].reshape(stations, samples)
        w_r = ((cosine * along_r - sine * along_i) * factor).astype(BF16)
        w_i = (-(cosine * along_i + sine * along_r) * factor).astype(BF16)
        out_ref[pol, 0] = (dot(w_r, y_r) - dot(w_i, y_i)).astype(BF16)
        out_ref[pol, 1] = (dot(w_i, y_r) + dot(w_r, y_i)).astype(BF16)
        if not turn:
            store = pltpu.make_async_copy(
                out_ref.at[pol], refs[0].at[pol, :, :, span], refs[2].at[pol]
            )
            store.start()
            stores.append(store)
    for store in stores:
        store.wait()


def beamform(turn, source, me, line, cosine, sine, y, groups):
    samples = y.shape[3]
    beams = cosine.shape[0] // groups
    shape = (2, 2, beams, samples)
    if turn:
        out_spec, out_shape, scratch = whole(VMEM), jax.ShapeDtypeStruct(shape, BF16), []
    else:
        out_spec = whole(pltpu.HBM)
        out_shape = pltpu.HBM((2, 2, beams, groups * samples), BF16)
        scratch = [VMEM(shape, BF16), pltpu.SemaphoreType.DMA((2,))]
    return pl.pallas_call(
        functools.partial(beam_kernel, turn),
        in_specs=[whole(SMEM)] * 2 + [whole(VMEM)] * 4,
        out_specs=out_spec,
        out_shape=out_shape,
        scratch_shapes=scratch,
        compiler_params=params(16),
        name="beamform",
    )(source, me, line, cosine, sine, y)


def place_kernel(me_ref, own_hbm, other_ref, out_hbm, sem):
    samples = other_ref.shape[3]
    span = pl.ds(pl.multiple_of((1 - me_ref[1]) * samples, samples), samples)
    store = pltpu.make_async_copy(other_ref, out_hbm.at[:, :, :, span], sem)
    store.start()
    store.wait()


def place(me, own, other):
    return pl.pallas_call(
        place_kernel,
        in_specs=[whole(SMEM), whole(pltpu.HBM), whole(pl.ANY)],
        out_specs=whole(pltpu.HBM),
        out_shape=pltpu.HBM(own.shape, BF16),
        scratch_shapes=[pltpu.SemaphoreType.DMA],
        input_output_aliases={1: 0},
        compiler_params=params(8),
        name="place",
    )(me, own, other)


def join_kernel(near_ref, far_ref, vis_ref):
    vis_ref[...] = near_ref[...].astype(F32) + far_ref[...].astype(F32)


def join(near, far):
    parts, rows, cols = near.shape
    steps = 4
    block = pl.BlockSpec((parts, rows // steps, cols), lambda i: (0, i, 0))
    return pl.pallas_call(
        join_kernel,
        grid=(steps,),
        in_specs=[block, block],
        out_specs=block,
        out_shape=pltpu.HBM(near.shape, F32),
        compiler_params=params(8),
        name="join",
    )(near, far)


def swap(x, axis, mask):
    n = lax.axis_size(axis)
    return lax.ppermute(x, axis, [(i, i ^ mask) for i in range(n)])


def exchange(part):
    part = part + swap(part, "freq", 1)
    part = part + swap(part, "tm", 1)
    return part, swap(part, "tm", 3)


def cross(x, turn):
    pairs = []
    for i in range(lax.axis_size("freq") // 2):
        for core in range(2):
            for g in range(2):
                pairs.append(((2 * i + core) * 2 + g, (2 * i + g) * 2 + (core ^ turn)))
    return lax.ppermute(x, WIDE, pairs)


def body(
    voltages,
    prior_gains,
    station_flags,
    ingest_map,
    station_coords,
    pointing,
    corr_channels,
    beam_channels,
):
    n_freq = lax.axis_size("freq")
    n_time = lax.axis_size("tm")
    n_group = lax.axis_size("grp")
    freq_index = lax.axis_index("freq")
    group_index = lax.axis_index("grp")
    slots, _, rows, samples = voltages.shape
    stations = ingest_map.shape[0]
    inputs = 2 * stations
    total = samples * n_time
    core = freq_index % 2

    me = jnp.stack([freq_index, group_index, lax.axis_index("tm")]).astype(jnp.int32)
    base = ((freq_index * n_group + group_index) * rows).astype(jnp.int32).reshape(1)

    corr_send = ingest(
        voltages, corr_channels, ingest_map, station_flags, base, n_group,
        lambda slot, g: (slot // 2 * 2 + g, slot % 2), 16,
    )
    corr_y = lax.all_to_all(corr_send, WIDE, split_axis=0, concat_axis=0, tiled=True)
    beam_send = ingest(
        voltages, beam_channels, ingest_map, station_flags, base, n_group,
        lambda slot, g: (slot, g), 16,
    )
    my_beam = lax.dynamic_slice_in_dim(beam_channels, freq_index, 1, 0)[0]
    ratio = 0.875 + 0.25 * (my_beam.astype(F32) + 0.5) / slots
    slot_coords = jnp.take(station_coords, ingest_map, axis=1, mode="clip")
    east = (pointing[0].astype(F32) + 0.5) / GRID_CELLS - 0.5
    north = (pointing[1].astype(F32) + 0.5) / GRID_CELLS - 0.5
    phase = (2.0 * math.pi * ratio) * (
        east[:, None] * slot_coords[0][None, :] + north[:, None] * slot_coords[1][None, :]
    )
    cosine, sine = jnp.cos(phase), jnp.sin(phase)

    z = cross(prior_gains[0], 0)
    slot = lax.broadcasted_iota(jnp.int32, (slots, slots), 1)
    same = corr_channels[None, :] == beam_channels[:, None]
    source = jnp.sum(jnp.where(same, slot, 0), axis=1)
    beam_send, corr_y, z, cosine, sine, source, me = lax.optimization_barrier(
        (beam_send, corr_y, z, cosine, sine, source, me)
    )
    beam_y = lax.all_to_all(beam_send, WIDE, split_axis=0, concat_axis=0, tiled=True)

    scale = float(inputs) / total
    part = apply_visibilities(corr_y, z, None, scale)

    pieces = correlate(corr_y, me, 1.0 / total, n_time)
    pieces = [pieces[0]] + [swap(x, "tm", m + 1) for m, x in enumerate(pieces[1:])]

    sums = exchange(part)
    for _ in range(ITERS - 1):
        part, z = apply_visibilities(corr_y, z, sums, scale)
        sums = exchange(part)
    depth = slots // 4
    z = finish(z, sums, scale)
    reach = [(0, 0), (0, 1), (1, 0), (1, 1)]
    half_ring = slots // 2 * n_group
    vectors = [z] + [swap(z, WIDE, high * half_ring + low) for high, low in reach[1:]]
    copies, solved = choose(source, me, vectors, reach, depth)
    copies, near, far = lax.optimization_barrier((copies, *gather(pieces)))
    near, far = cross(near, 0), cross(far, 1)
    copies, beam_y = lax.optimization_barrier((copies, beam_y))
    groups = [
        [high * 2 * depth + 2 * i + c for i in range(depth)]
        for high in range(2)
        for c in range(2)
    ]
    line = lax.all_to_all(
        copies, "freq", split_axis=0, concat_axis=0, axis_index_groups=groups, tiled=True
    )

    line, near, far = lax.optimization_barrier((line, near, far))
    away = beamform(1, source, me, line, cosine, sine, beam_y, n_group)
    other = swap(away, "grp", 1)
    own = beamform(0, source, me, line, cosine, sine, beam_y, n_group)
    visibilities = join(near, far)
    beams = place(me, own, other)
    return visibilities[None], solved[None], beams[None]


def solution(mesh):
    return jax.shard_map(
        body,
        mesh=mesh,
        in_specs=(
            P(None, None, ("freq", "grp"), "tm"),
            P("freq", None, None),
            P(),
            P(),
            P(),
            P(),
            P(),
            P(),
        ),
        out_specs=(
            P("freq", None, "grp", "tm"),
            P("freq", None, None),
            P("freq", None, None, "grp", "tm"),
        ),
        check_vma=False,
    )
```

```python
import functools
import math

import jax
import jax.numpy as jnp
from jax import lax
from jax.experimental import pallas as pl
from jax.experimental.pallas import tpu as pltpu
from jax.sharding import PartitionSpec as P

ITERS = 4
GRID_CELLS = 64.0
F32 = jnp.float32
BF16 = jnp.bfloat16
WIDE = ("freq", "grp")
TEAM = ("tm", "grp")
VMEM = pltpu.VMEM
SMEM = pltpu.SMEM


def whole(space=VMEM):
    return pl.BlockSpec(memory_space=space)


def params(mib=48):
    return pltpu.CompilerParams(vmem_limit_bytes=mib << 20)


def ingest_kernel(
    stations,
    pick,
    base_ref,
    chan_hbm,
    map_hbm,
    flag_hbm,
    volts_hbm,
    out_hbm,
    chan_ref,
    map_ref,
    flag_ref,
    volts_ref,
    out_ref,
    table_sem,
    volts_sem,
    out_sem,
):
    slots, groups, _, rows, half = out_ref.shape
    steps = out_sem.shape[0]
    per_step = slots // steps
    load = pltpu.make_async_copy(volts_hbm, volts_ref, volts_sem)
    load.start()
    tables = [
        pltpu.make_async_copy(source, target, table_sem.at[i])
        for i, (source, target) in enumerate(
            ((chan_hbm, chan_ref), (map_hbm, map_ref), (flag_hbm, flag_ref))
        )
    ]
    for copy in tables:
        copy.start()
    for copy in tables:
        copy.wait()
    line = lax.broadcasted_iota(jnp.int32, (rows, half), 0)
    keep = jnp.zeros((rows, half), F32)
    for row in range(rows):
        slot = lax.rem(base_ref[0] + row, stations)
        good = (1 - flag_ref[map_ref[slot]]).astype(F32)
        keep = jnp.where(line == row, good, keep)
    keep = keep.astype(BF16)
    load.wait()
    stores = []
    for step in range(steps):
        for slot in range(step * per_step, (step + 1) * per_step):
            for g in range(groups):
                index, cut = pick(slot, g)
                channel = chan_ref[index]
                for part in range(2):
                    piece = volts_ref[channel, part, :, cut * half : (cut + 1) * half]
                    out_ref[slot, g, part] = piece * keep
        span = pl.ds(step * per_step, per_step)
        store = pltpu.make_async_copy(out_ref.at[span], out_hbm.at[span], out_sem.at[step])
        store.start()
        stores.append(store)
    for store in stores:
        store.wait()


def ingest(voltages, channels, ingest_map, station_flags, base, groups, pick, grant):
    slots, parts, rows, samples = voltages.shape
    stations = ingest_map.shape[0]
    half = samples // 2
    shape = (slots, groups, parts, rows, half)
    steps = 8
    out = pl.pallas_call(
        functools.partial(ingest_kernel, stations, pick),
        in_specs=[whole(SMEM)] + [whole(pltpu.HBM)] * 4,
        out_specs=whole(pltpu.HBM),
        out_shape=pltpu.HBM(shape, BF16),
        scratch_shapes=[
            SMEM(channels.shape, jnp.int32),
            SMEM(ingest_map.shape, jnp.int32),
            SMEM(station_flags.shape, jnp.int32),
            VMEM(voltages.shape, BF16),
            VMEM(shape, BF16),
            pltpu.SemaphoreType.DMA((3,)),
            pltpu.SemaphoreType.DMA,
            pltpu.SemaphoreType.DMA((steps,)),
        ],
        compiler_params=params(grant),
        name="ingest",
    )(
        base,
        *(
            pltpu.with_memory_space_constraint(x, pltpu.HBM)
            for x in (channels, ingest_map, station_flags, voltages)
        ),
    )
    return out.reshape(slots * groups, parts, rows, half)


def load_part(ref, part):
    blocks, _, rows, samples = ref.shape
    return ref[:, part].reshape(blocks * rows, samples)


def nt_dot(a, b):
    return lax.dot_general(a, b, (((1,), (1,)), ((), ())), preferred_element_type=F32)


def correlate_kernel(scale, mask, me_ref, *refs):
    *y_refs, out_ref = refs
    blocks = y_refs[0].shape[0]
    _, height, width = out_ref.shape
    rows = blocks * height // (height * 2)
    cols = blocks * width // (height * 2)
    high = pl.ds(pl.multiple_of((me_ref[0] % 2) * rows, rows), rows)
    wide = pl.ds(pl.multiple_of((me_ref[2] ^ mask) * cols, cols), cols)
    samples = y_refs[0].shape[3]
    real, imag = 0.0, 0.0
    for y_ref in y_refs:
        left_r = y_ref[high, 0].reshape(height, samples)
        left_i = y_ref[high, 1].reshape(height, samples)
        right_r = y_ref[wide, 0].reshape(width, samples)
        right_i = y_ref[wide, 1].reshape(width, samples)
        real = real + nt_dot(left_r, right_r) + nt_dot(left_i, right_i)
        imag = imag + nt_dot(left_i, right_r) + nt_dot(-left_r, right_i)
    out_ref[0] = (real * scale).astype(BF16)
    out_ref[1] = (imag * scale).astype(BF16)


def correlate(ys, me, scale, mask, n_time):
    blocks, _, rows, samples = ys[0].shape
    inputs = blocks * rows
    return pl.pallas_call(
        functools.partial(correlate_kernel, scale, mask),
        in_specs=[whole(SMEM)] + [whole(VMEM)] * len(ys),
        out_specs=whole(VMEM),
        out_shape=jax.ShapeDtypeStruct((2, inputs // 2, inputs // n_time), BF16),
        compiler_params=params(16),
        name="correlate",
    )(me, *ys)


def gather_kernel(*refs):
    *part_refs, out_ref = refs
    pieces = [ref[...].astype(F32) for ref in part_refs]
    out_ref[...] = ((pieces[0] + pieces[1]) + (pieces[2] + pieces[3])).astype(BF16)


def gather(pieces):
    parts, rows, cols = pieces[0].shape
    steps = 2
    block = pl.BlockSpec((parts, rows // steps, cols), lambda i: (0, i, 0))
    return pl.pallas_call(
        gather_kernel,
        grid=(steps,),
        in_specs=[block] * len(pieces),
        out_specs=block,
        out_shape=jax.ShapeDtypeStruct((parts, rows, cols), BF16),
        compiler_params=params(16),
        name="gather",
    )(*pieces)


def in_terms(x):
    high = x.astype(BF16).astype(F32)
    rest = x - high
    mid = rest.astype(BF16).astype(F32)
    low = rest - mid
    pad = jnp.zeros_like(x)
    return jnp.concatenate([high, mid, low, pad], axis=0).astype(BF16)


def add_terms(x):
    return x[0:2] + x[2:4] + x[4:6]


def advance(scale, z, update):
    power = jnp.sum(z * z) + 1e-06
    return 0.5 * (z + scale * update / power)


def apply_half(terms, y_ref):
    real, imag = load_part(y_ref, 0), load_part(y_ref, 1)
    a = add_terms(jnp.dot(terms, real, preferred_element_type=F32))
    b = add_terms(jnp.dot(terms, imag, preferred_element_type=F32))
    w = jnp.concatenate([a[0:1] + b[1:2], a[1:2] - b[0:1]], axis=0)
    terms = in_terms(w)
    c = add_terms(nt_dot(terms, real))
    d = add_terms(nt_dot(terms, imag))
    return jnp.concatenate([c[0:1] - d[1:2], c[1:2] + d[0:1]], axis=0)


def apply_kernel(scale, first, mine_ref, other_ref, z_ref, *refs):
    z = z_ref[...]
    if first:
        (out_ref,) = refs
    else:
        near_ref, far_ref, out_ref, fresh_ref = refs
        z = advance(scale, z, near_ref[...] + far_ref[...])
        fresh_ref[...] = z
    terms = in_terms(z)
    out_ref[...] = apply_half(terms, mine_ref) + apply_half(terms, other_ref)


def apply_visibilities(ys, z, sums, scale):
    first = sums is None
    vector = jax.ShapeDtypeStruct(z.shape, F32)
    return pl.pallas_call(
        functools.partial(apply_kernel, scale, first),
        in_specs=[whole(VMEM)] * (3 if first else 5),
        out_specs=whole(VMEM) if first else [whole(VMEM)] * 2,
        out_shape=vector if first else [vector] * 2,
        compiler_params=params(16),
        name="apply",
    )(*ys, z, *(sums or ()))


def finish_kernel(scale, z_ref, near_ref, far_ref, fresh_ref):
    fresh_ref[...] = advance(scale, z_ref[...], near_ref[...] + far_ref[...])


def finish(z, sums, scale):
    return pl.pallas_call(
        functools.partial(finish_kernel, scale),
        in_specs=[whole(VMEM)] * 3,
        out_specs=whole(VMEM),
        out_shape=jax.ShapeDtypeStruct(z.shape, F32),
        compiler_params=params(8),
        name="finish",
    )(z, *sums)


def choose_kernel(reach, source_ref, me_ref, *refs):
    z_refs, (copies_ref, solved_ref) = refs[: len(reach)], refs[len(reach) :]
    depth = copies_ref.shape[0]
    chip, grp = me_ref[0], me_ref[1]
    core, high_half = chip % 2, chip // (2 * depth)
    vectors = [ref[...] for ref in z_refs]
    own = jnp.full(vectors[0].shape, (core == grp).astype(jnp.int32)) == 1
    solved_ref[...] = jnp.where(own, vectors[0], vectors[1])
    for i in range(depth):
        slot = source_ref[high_half * 2 * depth + 2 * i + core]
        far, side = (slot // (2 * depth)) ^ high_half, (slot % 2) ^ grp
        which = jnp.full(vectors[0].shape, 2 * far + side)
        chosen = vectors[0]
        for (high, low), vector in zip(reach[1:], vectors[1:]):
            chosen = jnp.where(which == 2 * high + low, vector, chosen)
        copies_ref[i] = chosen


def choose(source, me, vectors, reach, depth):
    shape = vectors[0].shape
    return pl.pallas_call(
        functools.partial(choose_kernel, reach),
        in_specs=[whole(SMEM)] * 2 + [whole(VMEM)] * len(reach),
        out_specs=[whole(VMEM)] * 2,
        out_shape=[
            jax.ShapeDtypeStruct((depth,) + shape, F32),
            jax.ShapeDtypeStruct(shape, F32),
        ],
        compiler_params=params(8),
        name="choose",
    )(source, me, *vectors)


def beam_kernel(turn, source_ref, me_ref, line_ref, cos_ref, sin_ref, y_ref, *refs):
    out_ref = refs[0] if turn else refs[1]
    slot = source_ref[me_ref[0]]
    gains = line_ref[(slot // 2) % line_ref.shape[0]]
    blocks, _, rows, samples = y_ref.shape
    stations = blocks // 2 * rows
    beams = out_ref.shape[2]
    factor = 1.0 / math.sqrt(stations)
    half = pl.ds(pl.multiple_of((me_ref[1] ^ turn) * beams, beams), beams)
    cosine, sine = cos_ref[half, :], sin_ref[half, :]
    span = pl.ds(pl.multiple_of(me_ref[1] * samples, samples), samples)
    dot = functools.partial(jnp.dot, preferred_element_type=F32)
    stores = []
    for pol in range(2):
        gain_r = gains[0:1, pol * stations : (pol + 1) * stations]
        gain_i = gains[1:2, pol * stations : (pol + 1) * stations]
        denom = jnp.maximum(gain_r * gain_r + gain_i * gain_i, 0.5)
        along_r, along_i = gain_r / denom, gain_i / denom
        y_r = y_ref[pol * blocks // 2 : (pol + 1) * blocks // 2, 0].reshape(stations, samples)
        y_i = y_ref[pol * blocks // 2 : (pol + 1) * blocks // 2, 1].reshape(stations, samples)
        w_r = ((cosine * along_r - sine * along_i) * factor).astype(BF16)
        w_i = (-(cosine * along_i + sine * along_r) * factor).astype(BF16)
        out_ref[pol, 0] = (dot(w_r, y_r) - dot(w_i, y_i)).astype(BF16)
        out_ref[pol, 1] = (dot(w_i, y_r) + dot(w_r, y_i)).astype(BF16)
        if not turn:
            store = pltpu.make_async_copy(
                out_ref.at[pol], refs[0].at[pol, :, :, span], refs[2].at[pol]
            )
            store.start()
            stores.append(store)
    for store in stores:
        store.wait()


def beamform(turn, source, me, line, cosine, sine, y, groups):
    samples = y.shape[3]
    beams = cosine.shape[0] // groups
    shape = (2, 2, beams, samples)
    if turn:
        out_spec, out_shape, scratch = whole(VMEM), jax.ShapeDtypeStruct(shape, BF16), []
    else:
        out_spec = whole(pltpu.HBM)
        out_shape = pltpu.HBM((2, 2, beams, groups * samples), BF16)
        scratch = [VMEM(shape, BF16), pltpu.SemaphoreType.DMA((2,))]
    return pl.pallas_call(
        functools.partial(beam_kernel, turn),
        in_specs=[whole(SMEM)] * 2 + [whole(VMEM)] * 4,
        out_specs=out_spec,
        out_shape=out_shape,
        scratch_shapes=scratch,
        compiler_params=params(16),
        name="beamform",
    )(source, me, line, cosine, sine, y)


def place_kernel(me_ref, own_hbm, other_ref, out_hbm, sem):
    samples = other_ref.shape[3]
    span = pl.ds(pl.multiple_of((1 - me_ref[1]) * samples, samples), samples)
    store = pltpu.make_async_copy(other_ref, out_hbm.at[:, :, :, span], sem)
    store.start()
    store.wait()


def place(me, own, other):
    return pl.pallas_call(
        place_kernel,
        in_specs=[whole(SMEM), whole(pltpu.HBM), whole(pl.ANY)],
        out_specs=whole(pltpu.HBM),
        out_shape=pltpu.HBM(own.shape, BF16),
        scratch_shapes=[pltpu.SemaphoreType.DMA],
        input_output_aliases={1: 0},
        compiler_params=params(8),
        name="place",
    )(me, own, other)


def widen_kernel(in_ref, out_ref):
    out_ref[...] = in_ref[...].astype(F32)


def widen(x):
    parts, rows, cols = x.shape
    steps = 2
    block = pl.BlockSpec((parts, rows // steps, cols), lambda i: (0, i, 0))
    return pl.pallas_call(
        widen_kernel,
        grid=(steps,),
        in_specs=[block],
        out_specs=block,
        out_shape=pltpu.HBM(x.shape, F32),
        compiler_params=params(8),
        name="widen",
    )(x)


def swap(x, axis, mask):
    n = lax.axis_size(axis)
    return lax.ppermute(x, axis, [(i, i ^ mask) for i in range(n)])


def cross(x):
    pairs = []
    for i in range(lax.axis_size("freq") // 2):
        for core in range(2):
            for g in range(2):
                pairs.append(((2 * i + core) * 2 + g, (2 * i + g) * 2 + core))
    return lax.ppermute(x, WIDE, pairs)


def body(
    voltages,
    prior_gains,
    station_flags,
    ingest_map,
    station_coords,
    pointing,
    corr_channels,
    beam_channels,
):
    n_freq = lax.axis_size("freq")
    n_time = lax.axis_size("tm")
    n_group = lax.axis_size("grp")
    freq_index = lax.axis_index("freq")
    group_index = lax.axis_index("grp")
    slots, _, rows, samples = voltages.shape
    stations = ingest_map.shape[0]
    inputs = 2 * stations
    total = samples * n_time

    me = jnp.stack([freq_index, group_index, lax.axis_index("tm")]).astype(jnp.int32)
    base = ((freq_index * n_group + group_index) * rows).astype(jnp.int32).reshape(1)

    corr_send = ingest(
        voltages, corr_channels, ingest_map, station_flags, base, n_group,
        lambda slot, g: (slot // 2 * 2 + g, slot % 2), 16,
    )
    corr_y = lax.all_to_all(corr_send, WIDE, split_axis=0, concat_axis=0, tiled=True)
    beam_send = ingest(
        voltages, beam_channels, ingest_map, station_flags, base, n_group,
        lambda slot, g: (slot, g), 16,
    )
    my_beam = lax.dynamic_slice_in_dim(beam_channels, freq_index, 1, 0)[0]
    ratio = 0.875 + 0.25 * (my_beam.astype(F32) + 0.5) / slots
    slot_coords = jnp.take(station_coords, ingest_map, axis=1, mode="clip")
    east = (pointing[0].astype(F32) + 0.5) / GRID_CELLS - 0.5
    north = (pointing[1].astype(F32) + 0.5) / GRID_CELLS - 0.5
    phase = (2.0 * math.pi * ratio) * (
        east[:, None] * slot_coords[0][None, :] + north[:, None] * slot_coords[1][None, :]
    )
    cosine, sine = jnp.cos(phase), jnp.sin(phase)

    z = cross(prior_gains[0])
    slot = lax.broadcasted_iota(jnp.int32, (slots, slots), 1)
    same = corr_channels[None, :] == beam_channels[:, None]
    source = jnp.sum(jnp.where(same, slot, 0), axis=1)
    beam_send, corr_y, z, cosine, sine, source, me = lax.optimization_barrier(
        (beam_send, corr_y, z, cosine, sine, source, me)
    )
    beam_y = lax.all_to_all(beam_send, WIDE, split_axis=0, concat_axis=0, tiled=True)

    ys = [corr_y, swap(corr_y, "freq", 1)]
    scale = float(inputs) / total
    part = apply_visibilities(ys, z, None, scale)
    pieces = []
    for step in range(ITERS):
        if step:
            part, z = apply_visibilities(ys, z, sums, scale)
        part = part + swap(part, "tm", 1)
        far = swap(part, "tm", 3)
        part, *late = lax.optimization_barrier((part, *ys))
        piece = correlate(late, me, 1.0 / total, step, n_time)
        far, piece = lax.optimization_barrier((far, piece))
        pieces.append(piece)
        sums = (part, far)
    depth = slots // 4
    part, far, *pieces = lax.optimization_barrier((*sums, *pieces))
    pieces = [pieces[0]] + [swap(x, "tm", m + 1) for m, x in enumerate(pieces[1:])]
    z = finish(z, (part, far), scale)
    reach = [(0, 0), (0, 1), (1, 0), (1, 1)]
    half_ring = slots // 2 * n_group
    vectors = [z] + [swap(z, WIDE, high * half_ring + low) for high, low in reach[1:]]
    copies, solved = choose(source, me, vectors, reach, depth)
    copies, beam_y = lax.optimization_barrier((copies, beam_y))
    groups = [
        [high * 2 * depth + 2 * i + c for i in range(depth)]
        for high in range(2)
        for c in range(2)
    ]
    line = lax.all_to_all(
        copies, "freq", split_axis=0, concat_axis=0, axis_index_groups=groups, tiled=True
    )

    block = cross(gather(pieces))
    away = beamform(1, source, me, line, cosine, sine, beam_y, n_group)
    other = swap(away, "grp", 1)
    own = beamform(0, source, me, line, cosine, sine, beam_y, n_group)
    visibilities = widen(block)
    beams = place(me, own, other)
    return visibilities[None], solved[None], beams[None]


def solution(mesh):
    return jax.shard_map(
        body,
        mesh=mesh,
        in_specs=(
            P(None, None, ("freq", "grp"), "tm"),
            P("freq", None, None),
            P(),
            P(),
            P(),
            P(),
            P(),
            P(),
        ),
        out_specs=(
            P("freq", None, "grp", "tm"),
            P("freq", None, None),
            P("freq", None, None, "grp", "tm"),
        ),
        check_vma=False,
    )
```

```python
import functools
import math

import jax
import jax.numpy as jnp
from jax import lax
from jax.experimental import pallas as pl
from jax.experimental.pallas import tpu as pltpu
from jax.sharding import PartitionSpec as P

ITERS = 4
GRID_CELLS = 64.0
F32 = jnp.float32
BF16 = jnp.bfloat16
WIDE = ("freq", "grp")
TEAM = ("tm", "grp")
VMEM = pltpu.VMEM
SMEM = pltpu.SMEM


def whole(space=VMEM):
    return pl.BlockSpec(memory_space=space)


def params(mib=48):
    return pltpu.CompilerParams(vmem_limit_bytes=mib << 20)


def ingest_kernel(
    stations,
    pick,
    base_ref,
    chan_hbm,
    map_hbm,
    flag_hbm,
    volts_hbm,
    out_hbm,
    chan_ref,
    map_ref,
    flag_ref,
    volts_ref,
    out_ref,
    table_sem,
    volts_sem,
    out_sem,
):
    slots, groups, _, rows, half = out_ref.shape
    steps = out_sem.shape[0]
    per_step = slots // steps
    load = pltpu.make_async_copy(volts_hbm, volts_ref, volts_sem)
    load.start()
    tables = [
        pltpu.make_async_copy(source, target, table_sem.at[i])
        for i, (source, target) in enumerate(
            ((chan_hbm, chan_ref), (map_hbm, map_ref), (flag_hbm, flag_ref))
        )
    ]
    for copy in tables:
        copy.start()
    for copy in tables:
        copy.wait()
    line = lax.broadcasted_iota(jnp.int32, (rows, half), 0)
    keep = jnp.zeros((rows, half), F32)
    for row in range(rows):
        slot = lax.rem(base_ref[0] + row, stations)
        good = (1 - flag_ref[map_ref[slot]]).astype(F32)
        keep = jnp.where(line == row, good, keep)
    keep = keep.astype(BF16)
    load.wait()
    stores = []
    for step in range(steps):
        for slot in range(step * per_step, (step + 1) * per_step):
            for g in range(groups):
                index, cut = pick(slot, g)
                channel = chan_ref[index]
                for part in range(2):
                    piece = volts_ref[channel, part, :, cut * half : (cut + 1) * half]
                    out_ref[slot, g, part] = piece * keep
        span = pl.ds(step * per_step, per_step)
        store = pltpu.make_async_copy(out_ref.at[span], out_hbm.at[span], out_sem.at[step])
        store.start()
        stores.append(store)
    for store in stores:
        store.wait()


def ingest(voltages, channels, ingest_map, station_flags, base, groups, pick, grant):
    slots, parts, rows, samples = voltages.shape
    stations = ingest_map.shape[0]
    half = samples // 2
    shape = (slots, groups, parts, rows, half)
    steps = 8
    out = pl.pallas_call(
        functools.partial(ingest_kernel, stations, pick),
        in_specs=[whole(SMEM)] + [whole(pltpu.HBM)] * 4,
        out_specs=whole(pltpu.HBM),
        out_shape=pltpu.HBM(shape, BF16),
        scratch_shapes=[
            SMEM(channels.shape, jnp.int32),
            SMEM(ingest_map.shape, jnp.int32),
            SMEM(station_flags.shape, jnp.int32),
            VMEM(voltages.shape, BF16),
            VMEM(shape, BF16),
            pltpu.SemaphoreType.DMA((3,)),
            pltpu.SemaphoreType.DMA,
            pltpu.SemaphoreType.DMA((steps,)),
        ],
        compiler_params=params(grant),
        name="ingest",
    )(
        base,
        *(
            pltpu.with_memory_space_constraint(x, pltpu.HBM)
            for x in (channels, ingest_map, station_flags, voltages)
        ),
    )
    return out.reshape(slots * groups, parts, rows, half)


def load_part(ref, part):
    blocks, _, rows, samples = ref.shape
    return ref[:, part].reshape(blocks * rows, samples)


def nt_dot(a, b):
    return lax.dot_general(a, b, (((1,), (1,)), ((), ())), preferred_element_type=F32)


def correlate_kernel(scale, mask, me_ref, *refs):
    *y_refs, out_ref = refs
    blocks = y_refs[0].shape[0]
    _, height, width = out_ref.shape
    rows = blocks * height // (height * 2)
    cols = blocks * width // (height * 2)
    high = pl.ds(pl.multiple_of((me_ref[0] % 2) * rows, rows), rows)
    wide = pl.ds(pl.multiple_of((me_ref[2] ^ mask) * cols, cols), cols)
    samples = y_refs[0].shape[3]
    real, imag = 0.0, 0.0
    for y_ref in y_refs:
        left_r = y_ref[high, 0].reshape(height, samples)
        left_i = y_ref[high, 1].reshape(height, samples)
        right_r = y_ref[wide, 0].reshape(width, samples)
        right_i = y_ref[wide, 1].reshape(width, samples)
        real = real + nt_dot(left_r, right_r) + nt_dot(left_i, right_i)
        imag = imag + nt_dot(left_i, right_r) + nt_dot(-left_r, right_i)
    out_ref[0] = (real * scale).astype(BF16)
    out_ref[1] = (imag * scale).astype(BF16)


def correlate(ys, me, scale, mask, n_time):
    blocks, _, rows, samples = ys[0].shape
    inputs = blocks * rows
    return pl.pallas_call(
        functools.partial(correlate_kernel, scale, mask),
        in_specs=[whole(SMEM)] + [whole(VMEM)] * len(ys),
        out_specs=whole(VMEM),
        out_shape=pltpu.HBM((2, inputs // 2, inputs // n_time), BF16),
        compiler_params=params(16),
        name="correlate",
    )(me, *ys)


def gather_kernel(*refs):
    *part_refs, out_ref = refs
    pieces = [ref[...].astype(F32) for ref in part_refs]
    out_ref[...] = ((pieces[0] + pieces[1]) + (pieces[2] + pieces[3])).astype(BF16)


def gather(pieces):
    parts, rows, cols = pieces[0].shape
    steps = 2
    block = pl.BlockSpec((parts, rows // steps, cols), lambda i: (0, i, 0))
    pieces = [pltpu.with_memory_space_constraint(pieces[0], pltpu.HBM), *pieces[1:]]
    return pl.pallas_call(
        gather_kernel,
        grid=(steps,),
        in_specs=[block] * len(pieces),
        out_specs=block,
        out_shape=jax.ShapeDtypeStruct((parts, rows, cols), BF16),
        compiler_params=params(16),
        name="gather",
    )(*pieces)


def in_terms(x):
    high = x.astype(BF16).astype(F32)
    rest = x - high
    mid = rest.astype(BF16).astype(F32)
    low = rest - mid
    pad = jnp.zeros_like(x)
    return jnp.concatenate([high, mid, low, pad], axis=0).astype(BF16)


def add_terms(x):
    return x[0:2] + x[2:4] + x[4:6]


def advance(scale, z, update):
    power = jnp.sum(z * z) + 1e-06
    return 0.5 * (z + scale * update / power)


def apply_half(terms, y_ref):
    real, imag = load_part(y_ref, 0), load_part(y_ref, 1)
    a = add_terms(jnp.dot(terms, real, preferred_element_type=F32))
    b = add_terms(jnp.dot(terms, imag, preferred_element_type=F32))
    w = jnp.concatenate([a[0:1] + b[1:2], a[1:2] - b[0:1]], axis=0)
    terms = in_terms(w)
    c = add_terms(nt_dot(terms, real))
    d = add_terms(nt_dot(terms, imag))
    return jnp.concatenate([c[0:1] - d[1:2], c[1:2] + d[0:1]], axis=0)


def apply_kernel(scale, mine_ref, other_ref, z_ref, near_ref, far_ref, out_ref, fresh_ref):
    z = advance(scale, z_ref[...], near_ref[...] + far_ref[...])
    fresh_ref[...] = z
    terms = in_terms(z)
    out_ref[...] = apply_half(terms, mine_ref) + apply_half(terms, other_ref)


def apply_visibilities(ys, z, sums, scale):
    return pl.pallas_call(
        functools.partial(apply_kernel, scale),
        in_specs=[whole(VMEM)] * 5,
        out_specs=[whole(VMEM)] * 2,
        out_shape=[jax.ShapeDtypeStruct(z.shape, F32)] * 2,
        compiler_params=params(16),
        name="apply",
    )(*ys, z, *sums)


def begin_kernel(y_ref, z_ref, out_ref):
    out_ref[...] = apply_half(in_terms(z_ref[...]), y_ref)


def begin(y, z):
    return pl.pallas_call(
        begin_kernel,
        in_specs=[whole(VMEM)] * 2,
        out_specs=whole(VMEM),
        out_shape=jax.ShapeDtypeStruct(z.shape, F32),
        compiler_params=params(16),
        name="begin",
    )(y, z)


def finish_kernel(scale, z_ref, near_ref, far_ref, fresh_ref):
    fresh_ref[...] = advance(scale, z_ref[...], near_ref[...] + far_ref[...])


def finish(z, sums, scale):
    return pl.pallas_call(
        functools.partial(finish_kernel, scale),
        in_specs=[whole(VMEM)] * 3,
        out_specs=whole(VMEM),
        out_shape=jax.ShapeDtypeStruct(z.shape, F32),
        compiler_params=params(8),
        name="finish",
    )(z, *sums)


def choose_kernel(reach, source_ref, me_ref, *refs):
    *z_refs, copies_ref, solved_ref, table_ref = refs
    depth = copies_ref.shape[0]
    chip, grp = me_ref[0], me_ref[1]
    core, high_half = chip % 2, chip // (2 * depth)
    for (high, low), z_ref in zip(reach, z_refs):
        table_ref[2 * high + low] = z_ref[...]
    solved_ref[...] = table_ref[core ^ grp]
    for i in range(depth):
        slot = source_ref[high_half * 2 * depth + 2 * i + core]
        far, side = (slot // (2 * depth)) ^ high_half, (slot % 2) ^ grp
        copies_ref[i] = table_ref[2 * far + side]


def choose(source, me, vectors, reach, depth):
    shape = vectors[0].shape
    return pl.pallas_call(
        functools.partial(choose_kernel, reach),
        in_specs=[whole(SMEM)] * 2 + [whole(VMEM)] * len(reach),
        out_specs=[whole(VMEM)] * 2,
        out_shape=[
            jax.ShapeDtypeStruct((depth,) + shape, F32),
            jax.ShapeDtypeStruct(shape, F32),
        ],
        scratch_shapes=[VMEM((len(reach),) + shape, F32)],
        compiler_params=params(8),
        name="choose",
    )(source, me, *vectors)


def beam_kernel(turn, source_ref, me_ref, line_ref, cos_ref, sin_ref, y_ref, *refs):
    out_ref = refs[0] if turn else refs[1]
    slot = source_ref[me_ref[0]]
    gains = line_ref[(slot // 2) % line_ref.shape[0]]
    blocks, _, rows, samples = y_ref.shape
    stations = blocks // 2 * rows
    beams = out_ref.shape[2]
    factor = 1.0 / math.sqrt(stations)
    half = pl.ds(pl.multiple_of((me_ref[1] ^ turn) * beams, beams), beams)
    cosine, sine = cos_ref[half, :], sin_ref[half, :]
    span = pl.ds(pl.multiple_of(me_ref[1] * samples, samples), samples)
    dot = functools.partial(jnp.dot, preferred_element_type=F32)
    stores = []
    for pol in range(2):
        gain_r = gains[0:1, pol * stations : (pol + 1) * stations]
        gain_i = gains[1:2, pol * stations : (pol + 1) * stations]
        denom = jnp.maximum(gain_r * gain_r + gain_i * gain_i, 0.5)
        along_r, along_i = gain_r / denom, gain_i / denom
        y_r = y_ref[pol * blocks // 2 : (pol + 1) * blocks // 2, 0].reshape(stations, samples)
        y_i = y_ref[pol * blocks // 2 : (pol + 1) * blocks // 2, 1].reshape(stations, samples)
        w_r = ((cosine * along_r - sine * along_i) * factor).astype(BF16)
        w_i = (-(cosine * along_i + sine * along_r) * factor).astype(BF16)
        out_ref[pol, 0] = (dot(w_r, y_r) - dot(w_i, y_i)).astype(BF16)
        out_ref[pol, 1] = (dot(w_i, y_r) + dot(w_r, y_i)).astype(BF16)
        if not turn:
            store = pltpu.make_async_copy(
                out_ref.at[pol], refs[0].at[pol, :, :, span], refs[2].at[pol]
            )
            store.start()
            stores.append(store)
    for store in stores:
        store.wait()


def beamform(turn, source, me, line, cosine, sine, y, groups):
    samples = y.shape[3]
    beams = cosine.shape[0] // groups
    shape = (2, 2, beams, samples)
    if turn:
        out_spec, out_shape, scratch = whole(VMEM), jax.ShapeDtypeStruct(shape, BF16), []
    else:
        out_spec = whole(pltpu.HBM)
        out_shape = pltpu.HBM((2, 2, beams, groups * samples), BF16)
        scratch = [VMEM(shape, BF16), pltpu.SemaphoreType.DMA((2,))]
    return pl.pallas_call(
        functools.partial(beam_kernel, turn),
        in_specs=[whole(SMEM)] * 2 + [whole(VMEM)] * 4,
        out_specs=out_spec,
        out_shape=out_shape,
        scratch_shapes=scratch,
        compiler_params=params(16),
        name="beamform",
    )(source, me, line, cosine, sine, y)


def place_kernel(me_ref, own_hbm, other_ref, out_hbm, sem):
    samples = other_ref.shape[3]
    span = pl.ds(pl.multiple_of((1 - me_ref[1]) * samples, samples), samples)
    store = pltpu.make_async_copy(other_ref, out_hbm.at[:, :, :, span], sem)
    store.start()
    store.wait()


def place(me, own, other):
    return pl.pallas_call(
        place_kernel,
        in_specs=[whole(SMEM), whole(pltpu.HBM), whole(pl.ANY)],
        out_specs=whole(pltpu.HBM),
        out_shape=pltpu.HBM(own.shape, BF16),
        scratch_shapes=[pltpu.SemaphoreType.DMA],
        input_output_aliases={1: 0},
        compiler_params=params(8),
        name="place",
    )(me, own, other)


def widen_kernel(in_ref, out_ref):
    out_ref[...] = in_ref[...].astype(F32)


def widen(x):
    parts, rows, cols = x.shape
    steps = 2
    block = pl.BlockSpec((parts, rows // steps, cols), lambda i: (0, i, 0))
    return pl.pallas_call(
        widen_kernel,
        grid=(steps,),
        in_specs=[block],
        out_specs=block,
        out_shape=pltpu.HBM(x.shape, F32),
        compiler_params=params(8),
        name="widen",
    )(x)


def swap(x, axis, mask):
    n = lax.axis_size(axis)
    return lax.ppermute(x, axis, [(i, i ^ mask) for i in range(n)])


def cross(x):
    pairs = []
    for i in range(lax.axis_size("freq") // 2):
        for core in range(2):
            for g in range(2):
                pairs.append(((2 * i + core) * 2 + g, (2 * i + g) * 2 + core))
    return lax.ppermute(x, WIDE, pairs)


def body(
    voltages,
    prior_gains,
    station_flags,
    ingest_map,
    station_coords,
    pointing,
    corr_channels,
    beam_channels,
):
    n_freq = lax.axis_size("freq")
    n_time = lax.axis_size("tm")
    n_group = lax.axis_size("grp")
    freq_index = lax.axis_index("freq")
    group_index = lax.axis_index("grp")
    slots, _, rows, samples = voltages.shape
    stations = ingest_map.shape[0]
    inputs = 2 * stations
    total = samples * n_time

    me = jnp.stack([freq_index, group_index, lax.axis_index("tm")]).astype(jnp.int32)
    base = ((freq_index * n_group + group_index) * rows).astype(jnp.int32).reshape(1)

    corr_send = ingest(
        voltages, corr_channels, ingest_map, station_flags, base, n_group,
        lambda slot, g: (slot // 2 * 2 + g, slot % 2), 16,
    )
    corr_y = lax.all_to_all(corr_send, WIDE, split_axis=0, concat_axis=0, tiled=True)
    beam_send = ingest(
        voltages, beam_channels, ingest_map, station_flags, base, n_group,
        lambda slot, g: (slot, g), 16,
    )
    my_beam = lax.dynamic_slice_in_dim(beam_channels, freq_index, 1, 0)[0]
    ratio = 0.875 + 0.25 * (my_beam.astype(F32) + 0.5) / slots
    slot_coords = jnp.take(station_coords, ingest_map, axis=1, mode="clip")
    east = (pointing[0].astype(F32) + 0.5) / GRID_CELLS - 0.5
    north = (pointing[1].astype(F32) + 0.5) / GRID_CELLS - 0.5
    phase = (2.0 * math.pi * ratio) * (
        east[:, None] * slot_coords[0][None, :] + north[:, None] * slot_coords[1][None, :]
    )
    cosine, sine = jnp.cos(phase), jnp.sin(phase)

    z = cross(prior_gains[0])
    slot = lax.broadcasted_iota(jnp.int32, (slots, slots), 1)
    same = corr_channels[None, :] == beam_channels[:, None]
    source = jnp.sum(jnp.where(same, slot, 0), axis=1)
    beam_send, corr_y, z, cosine, sine, source, me = lax.optimization_barrier(
        (beam_send, corr_y, z, cosine, sine, source, me)
    )
    part = begin(corr_y, z)
    beam_y = lax.all_to_all(beam_send, WIDE, split_axis=0, concat_axis=0, tiled=True)

    scale = float(inputs) / total
    part = part + swap(part, "freq", 1)
    part, late = lax.optimization_barrier((part, corr_y))
    ys = [corr_y, swap(late, "freq", 1)]
    pieces = {}
    for step in range(ITERS):
        if step:
            part, z = apply_visibilities(ys, z, sums, scale)
        near = swap(part, "tm", 1)
        if step == 2:
            part, *late = lax.optimization_barrier((part, *ys))
            near, pieces[0] = lax.optimization_barrier(
                (near, correlate(late, me, 1.0 / total, 0, n_time))
            )
        part = part + near
        far = swap(part, "tm", 3)
        if step:
            part, *late = lax.optimization_barrier((part, *ys))
            far, pieces[step] = lax.optimization_barrier(
                (far, correlate(late, me, 1.0 / total, step, n_time))
            )
        sums = (part, far)
    depth = slots // 4
    part, far, *bulk = lax.optimization_barrier(
        (*sums, *(pieces[m] for m in range(1, n_time)))
    )
    pieces = [pieces[0]] + [swap(x, "tm", m + 1) for m, x in enumerate(bulk)]
    z = finish(z, (part, far), scale)
    reach = [(0, 0), (0, 1), (1, 0), (1, 1)]
    half_ring = slots // 2 * n_group
    vectors = [z] + [swap(z, WIDE, high * half_ring + low) for high, low in reach[1:]]
    copies, solved = choose(source, me, vectors, reach, depth)
    copies, beam_y = lax.optimization_barrier((copies, beam_y))
    groups = [
        [high * 2 * depth + 2 * i + c for i in range(depth)]
        for high in range(2)
        for c in range(2)
    ]
    line = lax.all_to_all(
        copies, "freq", split_axis=0, concat_axis=0, axis_index_groups=groups, tiled=True
    )

    block = cross(gather(pieces))
    away = beamform(1, source, me, line, cosine, sine, beam_y, n_group)
    other = swap(away, "grp", 1)
    own = beamform(0, source, me, line, cosine, sine, beam_y, n_group)
    visibilities = widen(block)
    beams = place(me, own, other)
    return visibilities[None], solved[None], beams[None]


def solution(mesh):
    return jax.shard_map(
        body,
        mesh=mesh,
        in_specs=(
            P(None, None, ("freq", "grp"), "tm"),
            P("freq", None, None),
            P(),
            P(),
            P(),
            P(),
            P(),
            P(),
        ),
        out_specs=(
            P("freq", None, "grp", "tm"),
            P("freq", None, None),
            P("freq", None, None, "grp", "tm"),
        ),
        check_vma=False,
    )
```

```python
import functools
import math

import jax
import jax.numpy as jnp
from jax import lax
from jax.experimental import pallas as pl
from jax.experimental.pallas import tpu as pltpu
from jax.sharding import PartitionSpec as P

ITERS = 4
GRID_CELLS = 64.0
F32 = jnp.float32
BF16 = jnp.bfloat16
WIDE = ("freq", "grp")
TEAM = ("tm", "grp")
VMEM = pltpu.VMEM
SMEM = pltpu.SMEM


def whole(space=VMEM):
    return pl.BlockSpec(memory_space=space)


def params(mib=48):
    return pltpu.CompilerParams(vmem_limit_bytes=mib << 20)


def ingest_kernel(
    stations,
    pick,
    base_ref,
    chan_hbm,
    map_hbm,
    flag_hbm,
    volts_hbm,
    out_hbm,
    chan_ref,
    map_ref,
    flag_ref,
    volts_ref,
    out_ref,
    table_sem,
    volts_sem,
    out_sem,
):
    slots, groups, _, rows, half = out_ref.shape
    steps = out_sem.shape[0]
    per_step = slots // steps
    load = pltpu.make_async_copy(volts_hbm, volts_ref, volts_sem)
    load.start()
    tables = [
        pltpu.make_async_copy(source, target, table_sem.at[i])
        for i, (source, target) in enumerate(
            ((chan_hbm, chan_ref), (map_hbm, map_ref), (flag_hbm, flag_ref))
        )
    ]
    for copy in tables:
        copy.start()
    for copy in tables:
        copy.wait()
    line = lax.broadcasted_iota(jnp.int32, (rows, half), 0)
    keep = jnp.zeros((rows, half), F32)
    for row in range(rows):
        slot = lax.rem(base_ref[0] + row, stations)
        good = (1 - flag_ref[map_ref[slot]]).astype(F32)
        keep = jnp.where(line == row, good, keep)
    keep = keep.astype(BF16)
    load.wait()
    stores = []
    for step in range(steps):
        for slot in range(step * per_step, (step + 1) * per_step):
            for g in range(groups):
                index, cut = pick(slot, g)
                channel = chan_ref[index]
                for part in range(2):
                    piece = volts_ref[channel, part, :, cut * half : (cut + 1) * half]
                    out_ref[slot, g, part] = piece * keep
        span = pl.ds(step * per_step, per_step)
        store = pltpu.make_async_copy(out_ref.at[span], out_hbm.at[span], out_sem.at[step])
        store.start()
        stores.append(store)
    for store in stores:
        store.wait()


def ingest(voltages, channels, ingest_map, station_flags, base, groups, pick, grant):
    slots, parts, rows, samples = voltages.shape
    stations = ingest_map.shape[0]
    half = samples // 2
    shape = (slots, groups, parts, rows, half)
    steps = 8
    out = pl.pallas_call(
        functools.partial(ingest_kernel, stations, pick),
        in_specs=[whole(SMEM)] + [whole(pltpu.HBM)] * 4,
        out_specs=whole(pltpu.HBM),
        out_shape=pltpu.HBM(shape, BF16),
        scratch_shapes=[
            SMEM(channels.shape, jnp.int32),
            SMEM(ingest_map.shape, jnp.int32),
            SMEM(station_flags.shape, jnp.int32),
            VMEM(voltages.shape, BF16),
            VMEM(shape, BF16),
            pltpu.SemaphoreType.DMA((3,)),
            pltpu.SemaphoreType.DMA,
            pltpu.SemaphoreType.DMA((steps,)),
        ],
        compiler_params=params(grant),
        name="ingest",
    )(
        base,
        *(
            pltpu.with_memory_space_constraint(x, pltpu.HBM)
            for x in (channels, ingest_map, station_flags, voltages)
        ),
    )
    return out.reshape(slots * groups, parts, rows, half)


def load_part(ref, part):
    blocks, _, rows, samples = ref.shape
    return ref[:, part].reshape(blocks * rows, samples)


def nt_dot(a, b):
    return lax.dot_general(a, b, (((1,), (1,)), ((), ())), preferred_element_type=F32)


def correlate_kernel(scale, mask, me_ref, *refs):
    *y_refs, out_ref = refs
    blocks = y_refs[0].shape[0]
    _, height, width = out_ref.shape
    rows = blocks * height // (height * 2)
    cols = blocks * width // (height * 2)
    high = pl.ds(pl.multiple_of((me_ref[0] % 2) * rows, rows), rows)
    wide = pl.ds(pl.multiple_of((me_ref[2] ^ mask) * cols, cols), cols)
    samples = y_refs[0].shape[3]
    real, imag = 0.0, 0.0
    for y_ref in y_refs:
        left_r = y_ref[high, 0].reshape(height, samples)
        left_i = y_ref[high, 1].reshape(height, samples)
        right_r = y_ref[wide, 0].reshape(width, samples)
        right_i = y_ref[wide, 1].reshape(width, samples)
        real = real + nt_dot(left_r, right_r) + nt_dot(left_i, right_i)
        imag = imag + nt_dot(left_i, right_r) + nt_dot(-left_r, right_i)
    out_ref[0] = (real * scale).astype(BF16)
    out_ref[1] = (imag * scale).astype(BF16)


def correlate(ys, me, scale, mask, n_time):
    blocks, _, rows, samples = ys[0].shape
    inputs = blocks * rows
    return pl.pallas_call(
        functools.partial(correlate_kernel, scale, mask),
        in_specs=[whole(SMEM)] + [whole(VMEM)] * len(ys),
        out_specs=whole(VMEM),
        out_shape=pltpu.HBM((2, inputs // 2, inputs // n_time), BF16),
        compiler_params=params(16),
        name="correlate",
    )(me, *ys)


def gather_kernel(*refs):
    *part_refs, out_ref = refs
    pieces = [ref[...].astype(F32) for ref in part_refs]
    out_ref[...] = ((pieces[0] + pieces[1]) + (pieces[2] + pieces[3])).astype(BF16)


def gather(pieces):
    parts, rows, cols = pieces[0].shape
    steps = 2
    block = pl.BlockSpec((parts, rows // steps, cols), lambda i: (0, i, 0))
    pieces = [pltpu.with_memory_space_constraint(pieces[0], pltpu.HBM), *pieces[1:]]
    return pl.pallas_call(
        gather_kernel,
        grid=(steps,),
        in_specs=[block] * len(pieces),
        out_specs=block,
        out_shape=jax.ShapeDtypeStruct((parts, rows, cols), BF16),
        compiler_params=params(16),
        name="gather",
    )(*pieces)


def in_terms(x):
    high = x.astype(BF16).astype(F32)
    rest = x - high
    mid = rest.astype(BF16).astype(F32)
    low = rest - mid
    pad = jnp.zeros_like(x)
    return jnp.concatenate([high, mid, low, pad], axis=0).astype(BF16)


def add_terms(x):
    return x[0:2] + x[2:4] + x[4:6]


def advance(scale, z, update):
    power = jnp.sum(z * z) + 1e-06
    return 0.5 * (z + scale * update / power)


def apply_half(terms, y_ref):
    real, imag = load_part(y_ref, 0), load_part(y_ref, 1)
    a = add_terms(jnp.dot(terms, real, preferred_element_type=F32))
    b = add_terms(jnp.dot(terms, imag, preferred_element_type=F32))
    w = jnp.concatenate([a[0:1] + b[1:2], a[1:2] - b[0:1]], axis=0)
    terms = in_terms(w)
    c = add_terms(nt_dot(terms, real))
    d = add_terms(nt_dot(terms, imag))
    return jnp.concatenate([c[0:1] - d[1:2], c[1:2] + d[0:1]], axis=0)


def apply_kernel(scale, mine_ref, other_ref, z_ref, near_ref, far_ref, out_ref, fresh_ref):
    z = advance(scale, z_ref[...], near_ref[...] + far_ref[...])
    fresh_ref[...] = z
    terms = in_terms(z)
    out_ref[...] = apply_half(terms, mine_ref) + apply_half(terms, other_ref)


def apply_visibilities(ys, z, sums, scale):
    return pl.pallas_call(
        functools.partial(apply_kernel, scale),
        in_specs=[whole(VMEM)] * 5,
        out_specs=[whole(VMEM)] * 2,
        out_shape=[jax.ShapeDtypeStruct(z.shape, F32)] * 2,
        compiler_params=params(16),
        name="apply",
    )(*ys, z, *sums)


def begin_kernel(y_ref, z_ref, out_ref):
    out_ref[...] = apply_half(in_terms(z_ref[...]), y_ref)


def begin(y, z):
    return pl.pallas_call(
        begin_kernel,
        in_specs=[whole(VMEM)] * 2,
        out_specs=whole(VMEM),
        out_shape=jax.ShapeDtypeStruct(z.shape, F32),
        compiler_params=params(16),
        name="begin",
    )(y, z)


def finish_kernel(scale, z_ref, near_ref, far_ref, fresh_ref):
    fresh_ref[...] = advance(scale, z_ref[...], near_ref[...] + far_ref[...])


def finish(z, sums, scale):
    return pl.pallas_call(
        functools.partial(finish_kernel, scale),
        in_specs=[whole(VMEM)] * 3,
        out_specs=whole(VMEM),
        out_shape=jax.ShapeDtypeStruct(z.shape, F32),
        compiler_params=params(8),
        name="finish",
    )(z, *sums)


def choose_kernel(reach, source_ref, me_ref, *refs):
    *z_refs, copies_ref, table_ref = refs
    depth = copies_ref.shape[0]
    high_half, grp = me_ref[0] // (2 * depth), me_ref[1]
    for (high, low), z_ref in zip(reach, z_refs):
        table_ref[2 * high + low] = z_ref[...]
    for i in range(depth):
        for core in range(2):
            slot = source_ref[high_half * 2 * depth + 2 * i + core]
            far, side = (slot // (2 * depth)) ^ high_half, (slot % 2) ^ grp
            copies_ref[i, core] = table_ref[2 * far + side]


def choose(source, me, vectors, reach, depth):
    shape = vectors[0].shape
    return pl.pallas_call(
        functools.partial(choose_kernel, reach),
        in_specs=[whole(SMEM)] * 2 + [whole(VMEM)] * len(reach),
        out_specs=whole(VMEM),
        out_shape=jax.ShapeDtypeStruct((depth, 2) + shape, F32),
        scratch_shapes=[VMEM((len(reach),) + shape, F32)],
        compiler_params=params(8),
        name="choose",
    )(source, me, *vectors)


def hand_kernel(source_ref, me_ref, line_ref, vector_ref, hand_ref):
    slot = source_ref[me_ref[0] // 2 * 2]
    hand_ref[0] = line_ref[(slot // 2) % line_ref.shape[0], 0]
    hand_ref[1] = vector_ref[...]


def hand(source, me, line, vector):
    return pl.pallas_call(
        hand_kernel,
        in_specs=[whole(SMEM)] * 2 + [whole(VMEM)] * 2,
        out_specs=whole(VMEM),
        out_shape=jax.ShapeDtypeStruct((2,) + vector.shape, F32),
        compiler_params=params(8),
        name="hand",
    )(source, me, line, vector)


def settle_kernel(me_ref, z_ref, vector_ref, handed_ref, solved_ref):
    core, grp = me_ref[0] % 2, me_ref[1]
    shape = z_ref.shape
    first = jnp.full(shape, core) == 0
    away = jnp.where(first, handed_ref[1], vector_ref[...])
    solved_ref[...] = jnp.where(jnp.full(shape, core ^ grp) == 0, z_ref[...], away)


def settle(me, z, vector, handed):
    return pl.pallas_call(
        settle_kernel,
        in_specs=[whole(SMEM)] + [whole(VMEM)] * 3,
        out_specs=pl.BlockSpec(z.shape, lambda: (0, 0)),
        out_shape=pltpu.HBM(z.shape, F32),
        compiler_params=params(8),
        name="settle",
    )(me, z, vector, handed)


def beam_kernel(turn, source_ref, me_ref, line_ref, handed_ref, cos_ref, sin_ref, y_ref, *refs):
    out_ref = refs[0] if turn else refs[1]
    slot = source_ref[me_ref[0]]
    gains = line_ref[(slot // 2) % line_ref.shape[0], 1]
    first = jnp.full(gains.shape, me_ref[0] % 2) == 0
    gains = jnp.where(first, handed_ref[0], gains)
    blocks, _, rows, samples = y_ref.shape
    stations = blocks // 2 * rows
    beams = out_ref.shape[2]
    factor = 1.0 / math.sqrt(stations)
    half = pl.ds(pl.multiple_of((me_ref[1] ^ turn) * beams, beams), beams)
    cosine, sine = cos_ref[half, :], sin_ref[half, :]
    span = pl.ds(pl.multiple_of(me_ref[1] * samples, samples), samples)
    dot = functools.partial(jnp.dot, preferred_element_type=F32)
    stores = []
    for pol in range(2):
        gain_r = gains[0:1, pol * stations : (pol + 1) * stations]
        gain_i = gains[1:2, pol * stations : (pol + 1) * stations]
        denom = jnp.maximum(gain_r * gain_r + gain_i * gain_i, 0.5)
        along_r, along_i = gain_r / denom, gain_i / denom
        y_r = y_ref[pol * blocks // 2 : (pol + 1) * blocks // 2, 0].reshape(stations, samples)
        y_i = y_ref[pol * blocks // 2 : (pol + 1) * blocks // 2, 1].reshape(stations, samples)
        w_r = ((cosine * along_r - sine * along_i) * factor).astype(BF16)
        w_i = (-(cosine * along_i + sine * along_r) * factor).astype(BF16)
        out_ref[pol, 0] = (dot(w_r, y_r) - dot(w_i, y_i)).astype(BF16)
        out_ref[pol, 1] = (dot(w_i, y_r) + dot(w_r, y_i)).astype(BF16)
        if not turn:
            store = pltpu.make_async_copy(
                out_ref.at[pol], refs[0].at[pol, :, :, span], refs[2].at[pol]
            )
            store.start()
            stores.append(store)
    for store in stores:
        store.wait()


def beamform(turn, source, me, line, handed, cosine, sine, y, groups):
    samples = y.shape[3]
    beams = cosine.shape[0] // groups
    shape = (2, 2, beams, samples)
    if turn:
        out_spec, out_shape, scratch = whole(VMEM), jax.ShapeDtypeStruct(shape, BF16), []
    else:
        out_spec = whole(pltpu.HBM)
        out_shape = pltpu.HBM((2, 2, beams, groups * samples), BF16)
        scratch = [VMEM(shape, BF16), pltpu.SemaphoreType.DMA((2,))]
    return pl.pallas_call(
        functools.partial(beam_kernel, turn),
        in_specs=[whole(SMEM)] * 2 + [whole(VMEM)] * 5,
        out_specs=out_spec,
        out_shape=out_shape,
        scratch_shapes=scratch,
        compiler_params=params(16),
        name="beamform",
    )(source, me, line, handed, cosine, sine, y)


def place_kernel(me_ref, own_hbm, other_ref, out_hbm, sem):
    samples = other_ref.shape[3]
    span = pl.ds(pl.multiple_of((1 - me_ref[1]) * samples, samples), samples)
    store = pltpu.make_async_copy(other_ref, out_hbm.at[:, :, :, span], sem)
    store.start()
    store.wait()


def place(me, own, other):
    return pl.pallas_call(
        place_kernel,
        in_specs=[whole(SMEM), whole(pltpu.HBM), whole(pl.ANY)],
        out_specs=whole(pltpu.HBM),
        out_shape=pltpu.HBM(own.shape, BF16),
        scratch_shapes=[pltpu.SemaphoreType.DMA],
        input_output_aliases={1: 0},
        compiler_params=params(8),
        name="place",
    )(me, own, other)


def widen_kernel(in_ref, out_ref):
    out_ref[...] = in_ref[...].astype(F32)


def widen(x):
    parts, rows, cols = x.shape
    steps = 2
    block = pl.BlockSpec((parts, rows // steps, cols), lambda i: (0, i, 0))
    return pl.pallas_call(
        widen_kernel,
        grid=(steps,),
        in_specs=[block],
        out_specs=block,
        out_shape=pltpu.HBM(x.shape, F32),
        compiler_params=params(8),
        name="widen",
    )(x)


def swap(x, axis, mask):
    n = lax.axis_size(axis)
    return lax.ppermute(x, axis, [(i, i ^ mask) for i in range(n)])


def swap_odd(x, mask):
    n = lax.axis_size("freq") * lax.axis_size("grp")
    return lax.ppermute(x, WIDE, [(i, i ^ mask) for i in range(n) if i // 2 % 2])


def cross(x):
    pairs = []
    for i in range(lax.axis_size("freq") // 2):
        for core in range(2):
            for g in range(2):
                pairs.append(((2 * i + core) * 2 + g, (2 * i + g) * 2 + core))
    return lax.ppermute(x, WIDE, pairs)


def body(
    voltages,
    prior_gains,
    station_flags,
    ingest_map,
    station_coords,
    pointing,
    corr_channels,
    beam_channels,
):
    n_freq = lax.axis_size("freq")
    n_time = lax.axis_size("tm")
    n_group = lax.axis_size("grp")
    freq_index = lax.axis_index("freq")
    group_index = lax.axis_index("grp")
    slots, _, rows, samples = voltages.shape
    stations = ingest_map.shape[0]
    inputs = 2 * stations
    total = samples * n_time

    me = jnp.stack([freq_index, group_index, lax.axis_index("tm")]).astype(jnp.int32)
    base = ((freq_index * n_group + group_index) * rows).astype(jnp.int32).reshape(1)

    corr_send = ingest(
        voltages, corr_channels, ingest_map, station_flags, base, n_group,
        lambda slot, g: (slot // 2 * 2 + g, slot % 2), 16,
    )
    corr_y = lax.all_to_all(corr_send, WIDE, split_axis=0, concat_axis=0, tiled=True)
    beam_send = ingest(
        voltages, beam_channels, ingest_map, station_flags, base, n_group,
        lambda slot, g: (slot, g), 16,
    )
    my_beam = lax.dynamic_slice_in_dim(beam_channels, freq_index, 1, 0)[0]
    ratio = 0.875 + 0.25 * (my_beam.astype(F32) + 0.5) / slots
    slot_coords = jnp.take(station_coords, ingest_map, axis=1, mode="clip")
    east = (pointing[0].astype(F32) + 0.5) / GRID_CELLS - 0.5
    north = (pointing[1].astype(F32) + 0.5) / GRID_CELLS - 0.5
    phase = (2.0 * math.pi * ratio) * (
        east[:, None] * slot_coords[0][None, :] + north[:, None] * slot_coords[1][None, :]
    )
    cosine, sine = jnp.cos(phase), jnp.sin(phase)

    z = cross(prior_gains[0])
    slot = lax.broadcasted_iota(jnp.int32, (slots, slots), 1)
    same = corr_channels[None, :] == beam_channels[:, None]
    source = jnp.sum(jnp.where(same, slot, 0), axis=1)
    beam_send, corr_y, z, cosine, sine, source, me = lax.optimization_barrier(
        (beam_send, corr_y, z, cosine, sine, source, me)
    )
    part = begin(corr_y, z)
    beam_y = lax.all_to_all(beam_send, WIDE, split_axis=0, concat_axis=0, tiled=True)

    scale = float(inputs) / total
    part = part + swap(part, "freq", 1)
    part, late = lax.optimization_barrier((part, corr_y))
    ys = [corr_y, swap(late, "freq", 1)]
    pieces = {}
    for step in range(ITERS):
        if step:
            part, z = apply_visibilities(ys, z, sums, scale)
        near = swap(part, "tm", 1)
        if step == 2:
            part, *late = lax.optimization_barrier((part, *ys))
            near, pieces[0] = lax.optimization_barrier(
                (near, correlate(late, me, 1.0 / total, 0, n_time))
            )
        part = part + near
        far = swap(part, "tm", 3)
        if step:
            part, *late = lax.optimization_barrier((part, *ys))
            far, pieces[step] = lax.optimization_barrier(
                (far, correlate(late, me, 1.0 / total, step, n_time))
            )
        sums = (part, far)
    depth = slots // 4
    part, far, *bulk = lax.optimization_barrier(
        (*sums, *(pieces[m] for m in range(1, n_time)))
    )
    pieces = [pieces[0]] + [swap(x, "tm", m + 1) for m, x in enumerate(bulk)]
    z = finish(z, (part, far), scale)
    reach = [(0, 0), (0, 1), (1, 0), (1, 1)]
    half_ring = slots // 2 * n_group
    vectors = [z] + [swap_odd(z, high * half_ring + low) for high, low in reach[1:]]
    copies = choose(source, me, vectors, reach, depth)
    copies, beam_y = lax.optimization_barrier((copies, beam_y))
    groups = [
        [high * 2 * depth + 2 * i + c for i in range(depth)]
        for high in range(2)
        for c in range(2)
    ]
    line = lax.all_to_all(
        copies, "freq", split_axis=0, concat_axis=0, axis_index_groups=groups, tiled=True
    )

    line, block = lax.optimization_barrier((line, gather(pieces)))
    block = cross(block)
    handed = lax.ppermute(
        hand(source, me, line, vectors[1]),
        "freq",
        [(i + 1, i) for i in range(0, slots, 2)],
    )
    away = beamform(1, source, me, line, handed, cosine, sine, beam_y, n_group)
    other = swap(away, "grp", 1)
    own = beamform(0, source, me, line, handed, cosine, sine, beam_y, n_group)
    visibilities = widen(block)
    solved = settle(me, z, vectors[1], handed)
    beams = place(me, own, other)
    return visibilities[None], solved[None], beams[None]


def solution(mesh):
    return jax.shard_map(
        body,
        mesh=mesh,
        in_specs=(
            P(None, None, ("freq", "grp"), "tm"),
            P("freq", None, None),
            P(),
            P(),
            P(),
            P(),
            P(),
            P(),
        ),
        out_specs=(
            P("freq", None, "grp", "tm"),
            P("freq", None, None),
            P("freq", None, None, "grp", "tm"),
        ),
        check_vma=False,
    )
```

```python
import functools
import math

import jax
import jax.numpy as jnp
from jax import lax
from jax.experimental import pallas as pl
from jax.experimental.pallas import tpu as pltpu
from jax.sharding import PartitionSpec as P

ITERS = 4
GRID_CELLS = 64.0
F32 = jnp.float32
BF16 = jnp.bfloat16
WIDE = ("freq", "grp")
TEAM = ("tm", "grp")
VMEM = pltpu.VMEM
SMEM = pltpu.SMEM
LONG = pl.CostEstimate(flops=40 << 30, bytes_accessed=64 << 20, transcendentals=0)


def whole(space=VMEM):
    return pl.BlockSpec(memory_space=space)


def params(mib=48):
    return pltpu.CompilerParams(vmem_limit_bytes=mib << 20)


def ingest_kernel(
    stations,
    pick,
    base_ref,
    chan_hbm,
    map_hbm,
    flag_hbm,
    volts_hbm,
    out_hbm,
    chan_ref,
    map_ref,
    flag_ref,
    volts_ref,
    out_ref,
    table_sem,
    volts_sem,
    out_sem,
):
    slots, groups, _, rows, half = out_ref.shape
    steps = out_sem.shape[0]
    per_step = slots // steps
    load = pltpu.make_async_copy(volts_hbm, volts_ref, volts_sem)
    load.start()
    tables = [
        pltpu.make_async_copy(source, target, table_sem.at[i])
        for i, (source, target) in enumerate(
            ((chan_hbm, chan_ref), (map_hbm, map_ref), (flag_hbm, flag_ref))
        )
    ]
    for copy in tables:
        copy.start()
    for copy in tables:
        copy.wait()
    line = lax.broadcasted_iota(jnp.int32, (rows, half), 0)
    keep = jnp.zeros((rows, half), F32)
    for row in range(rows):
        slot = lax.rem(base_ref[0] + row, stations)
        good = (1 - flag_ref[map_ref[slot]]).astype(F32)
        keep = jnp.where(line == row, good, keep)
    keep = keep.astype(BF16)
    load.wait()
    stores = []
    for step in range(steps):
        for slot in range(step * per_step, (step + 1) * per_step):
            for g in range(groups):
                index, cut = pick(slot, g)
                channel = chan_ref[index]
                for part in range(2):
                    piece = volts_ref[channel, part, :, cut * half : (cut + 1) * half]
                    out_ref[slot, g, part] = piece * keep
        span = pl.ds(step * per_step, per_step)
        store = pltpu.make_async_copy(out_ref.at[span], out_hbm.at[span], out_sem.at[step])
        store.start()
        stores.append(store)
    for store in stores:
        store.wait()


def ingest(voltages, channels, ingest_map, station_flags, base, groups, pick, grant):
    slots, parts, rows, samples = voltages.shape
    stations = ingest_map.shape[0]
    half = samples // 2
    shape = (slots, groups, parts, rows, half)
    steps = 8
    out = pl.pallas_call(
        functools.partial(ingest_kernel, stations, pick),
        in_specs=[whole(SMEM)] + [whole(pltpu.HBM)] * 4,
        out_specs=whole(pltpu.HBM),
        out_shape=pltpu.HBM(shape, BF16),
        scratch_shapes=[
            SMEM(channels.shape, jnp.int32),
            SMEM(ingest_map.shape, jnp.int32),
            SMEM(station_flags.shape, jnp.int32),
            VMEM(voltages.shape, BF16),
            VMEM(shape, BF16),
            pltpu.SemaphoreType.DMA((3,)),
            pltpu.SemaphoreType.DMA,
            pltpu.SemaphoreType.DMA((steps,)),
        ],
        compiler_params=params(grant),
        name="ingest",
    )(
        base,
        *(
            pltpu.with_memory_space_constraint(x, pltpu.HBM)
            for x in (channels, ingest_map, station_flags, voltages)
        ),
    )
    return out.reshape(slots * groups, parts, rows, half)


def load_part(ref, part):
    blocks, _, rows, samples = ref.shape
    return ref[:, part].reshape(blocks * rows, samples)


def nt_dot(a, b):
    return lax.dot_general(a, b, (((1,), (1,)), ((), ())), preferred_element_type=F32)


def correlate_kernel(scale, mask, me_ref, *refs):
    *y_refs, out_ref = refs
    blocks = y_refs[0].shape[0]
    _, height, width = out_ref.shape
    rows = blocks * height // (height * 2)
    cols = blocks * width // (height * 2)
    high = pl.ds(pl.multiple_of((me_ref[0] % 2) * rows, rows), rows)
    wide = pl.ds(pl.multiple_of((me_ref[2] ^ mask) * cols, cols), cols)
    samples = y_refs[0].shape[3]
    real, imag = 0.0, 0.0
    for y_ref in y_refs:
        left_r = y_ref[high, 0].reshape(height, samples)
        left_i = y_ref[high, 1].reshape(height, samples)
        right_r = y_ref[wide, 0].reshape(width, samples)
        right_i = y_ref[wide, 1].reshape(width, samples)
        real = real + nt_dot(left_r, right_r) + nt_dot(left_i, right_i)
        imag = imag + nt_dot(left_i, right_r) + nt_dot(-left_r, right_i)
    out_ref[0] = (real * scale).astype(BF16)
    out_ref[1] = (imag * scale).astype(BF16)


def correlate(ys, me, scale, mask, n_time):
    blocks, _, rows, samples = ys[0].shape
    inputs = blocks * rows
    return pl.pallas_call(
        functools.partial(correlate_kernel, scale, mask),
        in_specs=[whole(SMEM)] + [whole(VMEM)] * len(ys),
        out_specs=whole(VMEM),
        out_shape=pltpu.HBM((2, inputs // 2, inputs // n_time), BF16),
        compiler_params=params(16),
        name="correlate",
    )(me, *ys)


def gather_kernel(*refs):
    *part_refs, out_ref = refs
    pieces = [ref[...].astype(F32) for ref in part_refs]
    out_ref[...] = ((pieces[0] + pieces[1]) + (pieces[2] + pieces[3])).astype(BF16)


def gather(pieces):
    parts, rows, cols = pieces[0].shape
    steps = 2
    block = pl.BlockSpec((parts, rows // steps, cols), lambda i: (0, i, 0))
    pieces = [pltpu.with_memory_space_constraint(pieces[0], pltpu.HBM), *pieces[1:]]
    return pl.pallas_call(
        gather_kernel,
        grid=(steps,),
        in_specs=[block] * len(pieces),
        out_specs=block,
        out_shape=jax.ShapeDtypeStruct((parts, rows, cols), BF16),
        compiler_params=params(16),
        name="gather",
    )(*pieces)


def in_terms(x):
    high = x.astype(BF16).astype(F32)
    rest = x - high
    mid = rest.astype(BF16).astype(F32)
    low = rest - mid
    pad = jnp.zeros_like(x)
    return jnp.concatenate([high, mid, low, pad], axis=0).astype(BF16)


def add_terms(x):
    return x[0:2] + x[2:4] + x[4:6]


def advance(scale, z, update):
    power = jnp.sum(z * z) + 1e-06
    return 0.5 * (z + scale * update / power)


def apply_half(terms, y_ref):
    real, imag = load_part(y_ref, 0), load_part(y_ref, 1)
    a = add_terms(jnp.dot(terms, real, preferred_element_type=F32))
    b = add_terms(jnp.dot(terms, imag, preferred_element_type=F32))
    w = jnp.concatenate([a[0:1] + b[1:2], a[1:2] - b[0:1]], axis=0)
    terms = in_terms(w)
    c = add_terms(nt_dot(terms, real))
    d = add_terms(nt_dot(terms, imag))
    return jnp.concatenate([c[0:1] - d[1:2], c[1:2] + d[0:1]], axis=0)


def apply_kernel(scale, mine_ref, other_ref, z_ref, near_ref, far_ref, out_ref, fresh_ref):
    z = advance(scale, z_ref[...], near_ref[...] + far_ref[...])
    fresh_ref[...] = z
    terms = in_terms(z)
    out_ref[...] = apply_half(terms, mine_ref) + apply_half(terms, other_ref)


def apply_visibilities(ys, z, sums, scale):
    return pl.pallas_call(
        functools.partial(apply_kernel, scale),
        in_specs=[whole(VMEM)] * 5,
        out_specs=[whole(VMEM)] * 2,
        out_shape=[jax.ShapeDtypeStruct(z.shape, F32)] * 2,
        compiler_params=params(16),
        name="apply",
    )(*ys, z, *sums)


def begin_kernel(y_ref, z_ref, out_ref):
    out_ref[...] = apply_half(in_terms(z_ref[...]), y_ref)


def begin(y, z):
    return pl.pallas_call(
        begin_kernel,
        in_specs=[whole(VMEM)] * 2,
        out_specs=whole(VMEM),
        out_shape=jax.ShapeDtypeStruct(z.shape, F32),
        compiler_params=params(16),
        name="begin",
    )(y, z)


def finish_kernel(scale, z_ref, near_ref, far_ref, fresh_ref):
    fresh_ref[...] = advance(scale, z_ref[...], near_ref[...] + far_ref[...])


def finish(z, sums, scale):
    return pl.pallas_call(
        functools.partial(finish_kernel, scale),
        in_specs=[whole(VMEM)] * 3,
        out_specs=whole(VMEM),
        out_shape=jax.ShapeDtypeStruct(z.shape, F32),
        compiler_params=params(8),
        name="finish",
    )(z, *sums)


def choose_kernel(reach, source_ref, me_ref, *refs):
    *z_refs, copies_ref, solved_ref, table_ref = refs
    depth = copies_ref.shape[0]
    chip, grp = me_ref[0], me_ref[1]
    core, high_half = chip % 2, chip // (2 * depth)
    for (high, low), z_ref in zip(reach, z_refs):
        table_ref[2 * high + low] = z_ref[...]
    solved_ref[...] = table_ref[core ^ grp]
    for i in range(depth):
        slot = source_ref[high_half * 2 * depth + 2 * i + core]
        far, side = (slot // (2 * depth)) ^ high_half, (slot % 2) ^ grp
        copies_ref[i] = table_ref[2 * far + side]


def choose(source, me, vectors, reach, depth):
    shape = vectors[0].shape
    return pl.pallas_call(
        functools.partial(choose_kernel, reach),
        in_specs=[whole(SMEM)] * 2 + [whole(VMEM)] * len(reach),
        out_specs=[whole(VMEM)] * 2,
        out_shape=[
            jax.ShapeDtypeStruct((depth,) + shape, F32),
            jax.ShapeDtypeStruct(shape, F32),
        ],
        scratch_shapes=[VMEM((len(reach),) + shape, F32)],
        compiler_params=params(8),
        name="choose",
    )(source, me, *vectors)


def beam_kernel(turn, source_ref, me_ref, line_ref, cos_ref, sin_ref, y_ref, *refs):
    out_ref = refs[0] if turn else refs[1]
    slot = source_ref[me_ref[0]]
    gains = line_ref[(slot // 2) % line_ref.shape[0]]
    blocks, _, rows, samples = y_ref.shape
    stations = blocks // 2 * rows
    beams = out_ref.shape[2]
    factor = 1.0 / math.sqrt(stations)
    half = pl.ds(pl.multiple_of((me_ref[1] ^ turn) * beams, beams), beams)
    cosine, sine = cos_ref[half, :], sin_ref[half, :]
    span = pl.ds(pl.multiple_of(me_ref[1] * samples, samples), samples)
    dot = functools.partial(jnp.dot, preferred_element_type=F32)
    stores = []
    for pol in range(2):
        gain_r = gains[0:1, pol * stations : (pol + 1) * stations]
        gain_i = gains[1:2, pol * stations : (pol + 1) * stations]
        denom = jnp.maximum(gain_r * gain_r + gain_i * gain_i, 0.5)
        along_r, along_i = gain_r / denom, gain_i / denom
        y_r = y_ref[pol * blocks // 2 : (pol + 1) * blocks // 2, 0].reshape(stations, samples)
        y_i = y_ref[pol * blocks // 2 : (pol + 1) * blocks // 2, 1].reshape(stations, samples)
        w_r = ((cosine * along_r - sine * along_i) * factor).astype(BF16)
        w_i = (-(cosine * along_i + sine * along_r) * factor).astype(BF16)
        out_ref[pol, 0] = (dot(w_r, y_r) - dot(w_i, y_i)).astype(BF16)
        out_ref[pol, 1] = (dot(w_i, y_r) + dot(w_r, y_i)).astype(BF16)
        if not turn:
            store = pltpu.make_async_copy(
                out_ref.at[pol], refs[0].at[pol, :, :, span], refs[2].at[pol]
            )
            store.start()
            stores.append(store)
    for store in stores:
        store.wait()


def beamform(turn, source, me, line, cosine, sine, y, groups):
    samples = y.shape[3]
    beams = cosine.shape[0] // groups
    shape = (2, 2, beams, samples)
    if turn:
        out_spec, out_shape, scratch = whole(VMEM), jax.ShapeDtypeStruct(shape, BF16), []
    else:
        out_spec = whole(pltpu.HBM)
        out_shape = pltpu.HBM((2, 2, beams, groups * samples), BF16)
        scratch = [VMEM(shape, BF16), pltpu.SemaphoreType.DMA((2,))]
    return pl.pallas_call(
        functools.partial(beam_kernel, turn),
        in_specs=[whole(SMEM)] * 2 + [whole(VMEM)] * 4,
        out_specs=out_spec,
        out_shape=out_shape,
        scratch_shapes=scratch,
        compiler_params=params(16),
        cost_estimate=LONG,
        name="beamform",
    )(source, me, line, cosine, sine, y)


def place_kernel(me_ref, own_hbm, other_ref, out_hbm, sem):
    samples = other_ref.shape[3]
    span = pl.ds(pl.multiple_of((1 - me_ref[1]) * samples, samples), samples)
    store = pltpu.make_async_copy(other_ref, out_hbm.at[:, :, :, span], sem)
    store.start()
    store.wait()


def place(me, own, other):
    return pl.pallas_call(
        place_kernel,
        in_specs=[whole(SMEM), whole(pltpu.HBM), whole(pl.ANY)],
        out_specs=whole(pltpu.HBM),
        out_shape=pltpu.HBM(own.shape, BF16),
        scratch_shapes=[pltpu.SemaphoreType.DMA],
        input_output_aliases={1: 0},
        compiler_params=params(8),
        name="place",
    )(me, own, other)


def widen_kernel(in_ref, out_ref):
    out_ref[...] = in_ref[...].astype(F32)


def widen(x):
    parts, rows, cols = x.shape
    steps = 2
    block = pl.BlockSpec((parts, rows // steps, cols), lambda i: (0, i, 0))
    return pl.pallas_call(
        widen_kernel,
        grid=(steps,),
        in_specs=[block],
        out_specs=block,
        out_shape=pltpu.HBM(x.shape, F32),
        compiler_params=params(8),
        name="widen",
    )(x)


def swap(x, axis, mask):
    n = lax.axis_size(axis)
    return lax.ppermute(x, axis, [(i, i ^ mask) for i in range(n)])


def cross(x):
    pairs = []
    for i in range(lax.axis_size("freq") // 2):
        for core in range(2):
            for g in range(2):
                pairs.append(((2 * i + core) * 2 + g, (2 * i + g) * 2 + core))
    return lax.ppermute(x, WIDE, pairs)


def body(
    voltages,
    prior_gains,
    station_flags,
    ingest_map,
    station_coords,
    pointing,
    corr_channels,
    beam_channels,
):
    n_freq = lax.axis_size("freq")
    n_time = lax.axis_size("tm")
    n_group = lax.axis_size("grp")
    freq_index = lax.axis_index("freq")
    group_index = lax.axis_index("grp")
    slots, _, rows, samples = voltages.shape
    stations = ingest_map.shape[0]
    inputs = 2 * stations
    total = samples * n_time

    me = jnp.stack([freq_index, group_index, lax.axis_index("tm")]).astype(jnp.int32)
    base = ((freq_index * n_group + group_index) * rows).astype(jnp.int32).reshape(1)

    corr_send = ingest(
        voltages, corr_channels, ingest_map, station_flags, base, n_group,
        lambda slot, g: (slot // 2 * 2 + g, slot % 2), 16,
    )
    corr_y = lax.all_to_all(corr_send, WIDE, split_axis=0, concat_axis=0, tiled=True)
    beam_send = ingest(
        voltages, beam_channels, ingest_map, station_flags, base, n_group,
        lambda slot, g: (slot, g), 16,
    )
    my_beam = lax.dynamic_slice_in_dim(beam_channels, freq_index, 1, 0)[0]
    ratio = 0.875 + 0.25 * (my_beam.astype(F32) + 0.5) / slots
    slot_coords = jnp.take(station_coords, ingest_map, axis=1, mode="clip")
    east = (pointing[0].astype(F32) + 0.5) / GRID_CELLS - 0.5
    north = (pointing[1].astype(F32) + 0.5) / GRID_CELLS - 0.5
    phase = (2.0 * math.pi * ratio) * (
        east[:, None] * slot_coords[0][None, :] + north[:, None] * slot_coords[1][None, :]
    )
    cosine, sine = jnp.cos(phase), jnp.sin(phase)

    z = cross(prior_gains[0])
    slot = lax.broadcasted_iota(jnp.int32, (slots, slots), 1)
    same = corr_channels[None, :] == beam_channels[:, None]
    source = jnp.sum(jnp.where(same, slot, 0), axis=1)
    beam_send, corr_y, z, cosine, sine, source, me = lax.optimization_barrier(
        (beam_send, corr_y, z, cosine, sine, source, me)
    )
    part = begin(corr_y, z)
    beam_y = lax.all_to_all(beam_send, WIDE, split_axis=0, concat_axis=0, tiled=True)

    scale = float(inputs) / total
    part = part + swap(part, "freq", 1)
    part, late = lax.optimization_barrier((part, corr_y))
    ys = [corr_y, swap(late, "freq", 1)]
    pieces = {}
    for step in range(ITERS):
        if step:
            part, z = apply_visibilities(ys, z, sums, scale)
        near = swap(part, "tm", 1)
        if step == 2:
            part, *late = lax.optimization_barrier((part, *ys))
            near, pieces[0] = lax.optimization_barrier(
                (near, correlate(late, me, 1.0 / total, 0, n_time))
            )
        part = part + near
        far = swap(part, "tm", 3)
        if step:
            part, *late = lax.optimization_barrier((part, *ys))
            far, pieces[step] = lax.optimization_barrier(
                (far, correlate(late, me, 1.0 / total, step, n_time))
            )
        sums = (part, far)
    depth = slots // 4
    part, far, piece = lax.optimization_barrier((*sums, pieces[2]))
    pieces[2] = swap(piece, "tm", 2)
    z = finish(z, (part, far), scale)
    reach = [(0, 0), (0, 1), (1, 0), (1, 1)]
    half_ring = slots // 2 * n_group
    vectors = [z] + [swap(z, WIDE, high * half_ring + low) for high, low in reach[1:]]
    copies, solved = choose(source, me, vectors, reach, depth)
    copies, beam_y, *bulk = lax.optimization_barrier(
        (copies, beam_y, pieces[1], pieces[3])
    )
    pieces[1], pieces[3] = swap(bulk[0], "tm", 1), swap(bulk[1], "tm", 3)
    pieces = [pieces[m] for m in range(n_time)]
    copies, beam_y = lax.optimization_barrier((copies, beam_y))
    groups = [
        [high * 2 * depth + 2 * i + c for i in range(depth)]
        for high in range(2)
        for c in range(2)
    ]
    line = lax.all_to_all(
        copies, "freq", split_axis=0, concat_axis=0, axis_index_groups=groups, tiled=True
    )

    away = beamform(1, source, me, line, cosine, sine, beam_y, n_group)
    other = swap(away, "grp", 1)
    own = beamform(0, source, me, line, cosine, sine, beam_y, n_group)
    own, *pieces = lax.optimization_barrier((own, *pieces))
    visibilities = widen(cross(gather(pieces)))
    beams = place(me, own, other)
    return visibilities[None], solved[None], beams[None]


def solution(mesh):
    return jax.shard_map(
        body,
        mesh=mesh,
        in_specs=(
            P(None, None, ("freq", "grp"), "tm"),
            P("freq", None, None),
            P(),
            P(),
            P(),
            P(),
            P(),
            P(),
        ),
        out_specs=(
            P("freq", None, "grp", "tm"),
            P("freq", None, None),
            P("freq", None, None, "grp", "tm"),
        ),
        check_vma=False,
    )
```

```python
import functools
import math

import jax
import jax.numpy as jnp
from jax import lax
from jax.experimental import pallas as pl
from jax.experimental.pallas import tpu as pltpu
from jax.sharding import PartitionSpec as P

ITERS = 4
GRID_CELLS = 64.0
F32 = jnp.float32
BF16 = jnp.bfloat16
WIDE = ("freq", "grp")
TEAM = ("tm", "grp")
VMEM = pltpu.VMEM
SMEM = pltpu.SMEM
LONG = pl.CostEstimate(flops=40 << 30, bytes_accessed=64 << 20, transcendentals=0)


def whole(space=VMEM):
    return pl.BlockSpec(memory_space=space)


def params(mib=48):
    return pltpu.CompilerParams(vmem_limit_bytes=mib << 20)


def ingest_kernel(
    stations,
    pick,
    base_ref,
    chan_hbm,
    map_hbm,
    flag_hbm,
    volts_hbm,
    out_hbm,
    chan_ref,
    map_ref,
    flag_ref,
    volts_ref,
    out_ref,
    table_sem,
    volts_sem,
    out_sem,
):
    slots, groups, _, rows, half = out_ref.shape
    steps = out_sem.shape[0]
    per_step = slots // steps
    load = pltpu.make_async_copy(volts_hbm, volts_ref, volts_sem)
    load.start()
    tables = [
        pltpu.make_async_copy(source, target, table_sem.at[i])
        for i, (source, target) in enumerate(
            ((chan_hbm, chan_ref), (map_hbm, map_ref), (flag_hbm, flag_ref))
        )
    ]
    for copy in tables:
        copy.start()
    for copy in tables:
        copy.wait()
    line = lax.broadcasted_iota(jnp.int32, (rows, half), 0)
    keep = jnp.zeros((rows, half), F32)
    for row in range(rows):
        slot = lax.rem(base_ref[0] + row, stations)
        good = (1 - flag_ref[map_ref[slot]]).astype(F32)
        keep = jnp.where(line == row, good, keep)
    keep = keep.astype(BF16)
    load.wait()
    stores = []
    for step in range(steps):
        for slot in range(step * per_step, (step + 1) * per_step):
            for g in range(groups):
                index, cut = pick(slot, g)
                channel = chan_ref[index]
                for part in range(2):
                    piece = volts_ref[channel, part, :, cut * half : (cut + 1) * half]
                    out_ref[slot, g, part] = piece * keep
        span = pl.ds(step * per_step, per_step)
        store = pltpu.make_async_copy(out_ref.at[span], out_hbm.at[span], out_sem.at[step])
        store.start()
        stores.append(store)
    for store in stores:
        store.wait()


def ingest(voltages, channels, ingest_map, station_flags, base, groups, pick, grant):
    slots, parts, rows, samples = voltages.shape
    stations = ingest_map.shape[0]
    half = samples // 2
    shape = (slots, groups, parts, rows, half)
    steps = 8
    out = pl.pallas_call(
        functools.partial(ingest_kernel, stations, pick),
        in_specs=[whole(SMEM)] + [whole(pltpu.HBM)] * 4,
        out_specs=whole(pltpu.HBM),
        out_shape=pltpu.HBM(shape, BF16),
        scratch_shapes=[
            SMEM(channels.shape, jnp.int32),
            SMEM(ingest_map.shape, jnp.int32),
            SMEM(station_flags.shape, jnp.int32),
            VMEM(voltages.shape, BF16),
            VMEM(shape, BF16),
            pltpu.SemaphoreType.DMA((3,)),
            pltpu.SemaphoreType.DMA,
            pltpu.SemaphoreType.DMA((steps,)),
        ],
        compiler_params=params(grant),
        name="ingest",
    )(
        base,
        *(
            pltpu.with_memory_space_constraint(x, pltpu.HBM)
            for x in (channels, ingest_map, station_flags, voltages)
        ),
    )
    return out.reshape(slots * groups, parts, rows, half)


def load_part(ref, part):
    blocks, _, rows, samples = ref.shape
    return ref[:, part].reshape(blocks * rows, samples)


def nt_dot(a, b):
    return lax.dot_general(a, b, (((1,), (1,)), ((), ())), preferred_element_type=F32)


def correlate_kernel(scale, mask, me_ref, *refs):
    *y_refs, out_ref = refs
    blocks = y_refs[0].shape[0]
    _, height, width = out_ref.shape
    rows = blocks * height // (height * 2)
    cols = blocks * width // (height * 2)
    high = pl.ds(pl.multiple_of((me_ref[0] % 2) * rows, rows), rows)
    wide = pl.ds(pl.multiple_of((me_ref[2] ^ mask) * cols, cols), cols)
    samples = y_refs[0].shape[3]
    real, imag = 0.0, 0.0
    for y_ref in y_refs:
        left_r = y_ref[high, 0].reshape(height, samples)
        left_i = y_ref[high, 1].reshape(height, samples)
        right_r = y_ref[wide, 0].reshape(width, samples)
        right_i = y_ref[wide, 1].reshape(width, samples)
        real = real + nt_dot(left_r, right_r) + nt_dot(left_i, right_i)
        imag = imag + nt_dot(left_i, right_r) + nt_dot(-left_r, right_i)
    out_ref[0] = (real * scale).astype(BF16)
    out_ref[1] = (imag * scale).astype(BF16)


def correlate(ys, me, scale, mask, n_time):
    blocks, _, rows, samples = ys[0].shape
    inputs = blocks * rows
    return pl.pallas_call(
        functools.partial(correlate_kernel, scale, mask),
        in_specs=[whole(SMEM)] + [whole(VMEM)] * len(ys),
        out_specs=whole(VMEM),
        out_shape=pltpu.HBM((2, inputs // 2, inputs // n_time), BF16),
        compiler_params=params(16),
        name="correlate",
    )(me, *ys)


def gather_kernel(*refs):
    *part_refs, out_ref = refs
    pieces = [ref[...].astype(F32) for ref in part_refs]
    out_ref[...] = ((pieces[0] + pieces[1]) + (pieces[2] + pieces[3])).astype(BF16)


def gather(pieces):
    parts, rows, cols = pieces[0].shape
    steps = 2
    block = pl.BlockSpec((parts, rows // steps, cols), lambda i: (0, i, 0))
    pieces = [pltpu.with_memory_space_constraint(pieces[0], pltpu.HBM), *pieces[1:]]
    return pl.pallas_call(
        gather_kernel,
        grid=(steps,),
        in_specs=[block] * len(pieces),
        out_specs=block,
        out_shape=jax.ShapeDtypeStruct((parts, rows, cols), BF16),
        compiler_params=params(16),
        name="gather",
    )(*pieces)


def in_terms(x):
    high = x.astype(BF16).astype(F32)
    rest = x - high
    mid = rest.astype(BF16).astype(F32)
    low = rest - mid
    pad = jnp.zeros_like(x)
    return jnp.concatenate([high, mid, low, pad], axis=0).astype(BF16)


def add_terms(x):
    return x[0:2] + x[2:4] + x[4:6]


def advance(scale, z, update):
    power = jnp.sum(z * z) + 1e-06
    return 0.5 * (z + scale * update / power)


def apply_half(terms, y_ref):
    real, imag = load_part(y_ref, 0), load_part(y_ref, 1)
    a = add_terms(jnp.dot(terms, real, preferred_element_type=F32))
    b = add_terms(jnp.dot(terms, imag, preferred_element_type=F32))
    w = jnp.concatenate([a[0:1] + b[1:2], a[1:2] - b[0:1]], axis=0)
    terms = in_terms(w)
    c = add_terms(nt_dot(terms, real))
    d = add_terms(nt_dot(terms, imag))
    return jnp.concatenate([c[0:1] - d[1:2], c[1:2] + d[0:1]], axis=0)


def apply_kernel(scale, mine_ref, other_ref, z_ref, near_ref, far_ref, out_ref, fresh_ref):
    z = advance(scale, z_ref[...], near_ref[...] + far_ref[...])
    fresh_ref[...] = z
    terms = in_terms(z)
    out_ref[...] = apply_half(terms, mine_ref) + apply_half(terms, other_ref)


def apply_visibilities(ys, z, sums, scale):
    return pl.pallas_call(
        functools.partial(apply_kernel, scale),
        in_specs=[whole(VMEM)] * 5,
        out_specs=[whole(VMEM)] * 2,
        out_shape=[jax.ShapeDtypeStruct(z.shape, F32)] * 2,
        compiler_params=params(16),
        name="apply",
    )(*ys, z, *sums)


def begin_kernel(y_ref, z_ref, out_ref):
    out_ref[...] = apply_half(in_terms(z_ref[...]), y_ref)


def begin(y, z):
    return pl.pallas_call(
        begin_kernel,
        in_specs=[whole(VMEM)] * 2,
        out_specs=whole(VMEM),
        out_shape=jax.ShapeDtypeStruct(z.shape, F32),
        compiler_params=params(16),
        name="begin",
    )(y, z)


def finish_kernel(scale, z_ref, near_ref, far_ref, fresh_ref):
    fresh_ref[...] = advance(scale, z_ref[...], near_ref[...] + far_ref[...])


def finish(z, sums, scale):
    return pl.pallas_call(
        functools.partial(finish_kernel, scale),
        in_specs=[whole(VMEM)] * 3,
        out_specs=whole(VMEM),
        out_shape=jax.ShapeDtypeStruct(z.shape, F32),
        compiler_params=params(8),
        name="finish",
    )(z, *sums)


def choose_kernel(reach, source_ref, me_ref, *refs):
    *z_refs, copies_ref, solved_ref, table_ref = refs
    depth = copies_ref.shape[0]
    chip, grp = me_ref[0], me_ref[1]
    core, high_half = chip % 2, chip // (2 * depth)
    for (high, low), z_ref in zip(reach, z_refs):
        table_ref[2 * high + low] = z_ref[...]
    solved_ref[...] = table_ref[core ^ grp]
    for i in range(depth):
        slot = source_ref[high_half * 2 * depth + 2 * i + core]
        far, side = (slot // (2 * depth)) ^ high_half, (slot % 2) ^ grp
        copies_ref[i] = table_ref[2 * far + side]


def choose(source, me, vectors, reach, depth):
    shape = vectors[0].shape
    return pl.pallas_call(
        functools.partial(choose_kernel, reach),
        in_specs=[whole(SMEM)] * 2 + [whole(VMEM)] * len(reach),
        out_specs=[whole(VMEM)] * 2,
        out_shape=[
            jax.ShapeDtypeStruct((depth,) + shape, F32),
            jax.ShapeDtypeStruct(shape, F32),
        ],
        scratch_shapes=[VMEM((len(reach),) + shape, F32)],
        compiler_params=params(8),
        name="choose",
    )(source, me, *vectors)


def beam_kernel(turn, source_ref, me_ref, line_ref, cos_ref, sin_ref, y_ref, *refs):
    out_ref = refs[0] if turn else refs[1]
    slot = source_ref[me_ref[0]]
    gains = line_ref[(slot // 2) % line_ref.shape[0]]
    blocks, _, rows, samples = y_ref.shape
    stations = blocks // 2 * rows
    beams = out_ref.shape[2]
    factor = 1.0 / math.sqrt(stations)
    half = pl.ds(pl.multiple_of((me_ref[1] ^ turn) * beams, beams), beams)
    cosine, sine = cos_ref[half, :], sin_ref[half, :]
    span = pl.ds(pl.multiple_of(me_ref[1] * samples, samples), samples)
    dot = functools.partial(jnp.dot, preferred_element_type=F32)
    stores = []
    for pol in range(2):
        gain_r = gains[0:1, pol * stations : (pol + 1) * stations]
        gain_i = gains[1:2, pol * stations : (pol + 1) * stations]
        denom = jnp.maximum(gain_r * gain_r + gain_i * gain_i, 0.5)
        along_r, along_i = gain_r / denom, gain_i / denom
        y_r = y_ref[pol * blocks // 2 : (pol + 1) * blocks // 2, 0].reshape(stations, samples)
        y_i = y_ref[pol * blocks // 2 : (pol + 1) * blocks // 2, 1].reshape(stations, samples)
        w_r = ((cosine * along_r - sine * along_i) * factor).astype(BF16)
        w_i = (-(cosine * along_i + sine * along_r) * factor).astype(BF16)
        out_ref[pol, 0] = (dot(w_r, y_r) - dot(w_i, y_i)).astype(BF16)
        out_ref[pol, 1] = (dot(w_i, y_r) + dot(w_r, y_i)).astype(BF16)
        if not turn:
            store = pltpu.make_async_copy(
                out_ref.at[pol], refs[0].at[pol, :, :, span], refs[2].at[pol]
            )
            store.start()
            stores.append(store)
    for store in stores:
        store.wait()


def beamform(turn, source, me, line, cosine, sine, y, groups):
    samples = y.shape[3]
    beams = cosine.shape[0] // groups
    shape = (2, 2, beams, samples)
    if turn:
        out_spec, out_shape, scratch = whole(VMEM), jax.ShapeDtypeStruct(shape, BF16), []
    else:
        out_spec = whole(pltpu.HBM)
        out_shape = pltpu.HBM((2, 2, beams, groups * samples), BF16)
        scratch = [VMEM(shape, BF16), pltpu.SemaphoreType.DMA((2,))]
    return pl.pallas_call(
        functools.partial(beam_kernel, turn),
        in_specs=[whole(SMEM)] * 2 + [whole(VMEM)] * 4,
        out_specs=out_spec,
        out_shape=out_shape,
        scratch_shapes=scratch,
        compiler_params=params(16),
        cost_estimate=LONG,
        name="beamform",
    )(source, me, line, cosine, sine, y)


def place_kernel(me_ref, own_hbm, other_ref, out_hbm, sem):
    samples = other_ref.shape[3]
    span = pl.ds(pl.multiple_of((1 - me_ref[1]) * samples, samples), samples)
    store = pltpu.make_async_copy(other_ref, out_hbm.at[:, :, :, span], sem)
    store.start()
    store.wait()


def place(me, own, other):
    return pl.pallas_call(
        place_kernel,
        in_specs=[whole(SMEM), whole(pltpu.HBM), whole(pl.ANY)],
        out_specs=whole(pltpu.HBM),
        out_shape=pltpu.HBM(own.shape, BF16),
        scratch_shapes=[pltpu.SemaphoreType.DMA],
        input_output_aliases={1: 0},
        compiler_params=params(8),
        name="place",
    )(me, own, other)


def widen_kernel(in_ref, out_ref):
    out_ref[...] = in_ref[...].astype(F32)


def widen(x):
    parts, rows, cols = x.shape
    steps = 2
    block = pl.BlockSpec((parts, rows // steps, cols), lambda i: (0, i, 0))
    return pl.pallas_call(
        widen_kernel,
        grid=(steps,),
        in_specs=[block],
        out_specs=block,
        out_shape=pltpu.HBM(x.shape, F32),
        compiler_params=params(8),
        name="widen",
    )(x)


def swap(x, axis, mask):
    n = lax.axis_size(axis)
    return lax.ppermute(x, axis, [(i, i ^ mask) for i in range(n)])


def cross(x):
    pairs = []
    for i in range(lax.axis_size("freq") // 2):
        for core in range(2):
            for g in range(2):
                pairs.append(((2 * i + core) * 2 + g, (2 * i + g) * 2 + core))
    return lax.ppermute(x, WIDE, pairs)


def body(
    voltages,
    prior_gains,
    station_flags,
    ingest_map,
    station_coords,
    pointing,
    corr_channels,
    beam_channels,
):
    n_freq = lax.axis_size("freq")
    n_time = lax.axis_size("tm")
    n_group = lax.axis_size("grp")
    freq_index = lax.axis_index("freq")
    group_index = lax.axis_index("grp")
    slots, _, rows, samples = voltages.shape
    stations = ingest_map.shape[0]
    inputs = 2 * stations
    total = samples * n_time

    me = jnp.stack([freq_index, group_index, lax.axis_index("tm")]).astype(jnp.int32)
    base = ((freq_index * n_group + group_index) * rows).astype(jnp.int32).reshape(1)

    corr_send = ingest(
        voltages, corr_channels, ingest_map, station_flags, base, n_group,
        lambda slot, g: (slot // 2 * 2 + g, slot % 2), 16,
    )
    corr_y = lax.all_to_all(corr_send, WIDE, split_axis=0, concat_axis=0, tiled=True)
    beam_send = ingest(
        voltages, beam_channels, ingest_map, station_flags, base, n_group,
        lambda slot, g: (slot, g), 16,
    )
    my_beam = lax.dynamic_slice_in_dim(beam_channels, freq_index, 1, 0)[0]
    ratio = 0.875 + 0.25 * (my_beam.astype(F32) + 0.5) / slots
    slot_coords = jnp.take(station_coords, ingest_map, axis=1, mode="clip")
    east = (pointing[0].astype(F32) + 0.5) / GRID_CELLS - 0.5
    north = (pointing[1].astype(F32) + 0.5) / GRID_CELLS - 0.5
    phase = (2.0 * math.pi * ratio) * (
        east[:, None] * slot_coords[0][None, :] + north[:, None] * slot_coords[1][None, :]
    )
    cosine, sine = jnp.cos(phase), jnp.sin(phase)

    z = cross(prior_gains[0])
    slot = lax.broadcasted_iota(jnp.int32, (slots, slots), 1)
    same = corr_channels[None, :] == beam_channels[:, None]
    source = jnp.sum(jnp.where(same, slot, 0), axis=1)
    beam_send, corr_y, z, cosine, sine, source, me = lax.optimization_barrier(
        (beam_send, corr_y, z, cosine, sine, source, me)
    )
    part = begin(corr_y, z)
    beam_y = lax.all_to_all(beam_send, WIDE, split_axis=0, concat_axis=0, tiled=True)

    scale = float(inputs) / total
    part = part + swap(part, "freq", 1)
    part, late = lax.optimization_barrier((part, corr_y))
    ys = [corr_y, swap(late, "freq", 1)]
    pieces = {}
    for step in range(ITERS):
        if step:
            part, z = apply_visibilities(ys, z, sums, scale)
        near = swap(part, "tm", 1)
        if step == 2:
            part, *late = lax.optimization_barrier((part, *ys))
            near, pieces[0] = lax.optimization_barrier(
                (near, correlate(late, me, 1.0 / total, 0, n_time))
            )
        part = part + near
        far = swap(part, "tm", 3)
        if step:
            part, *late = lax.optimization_barrier((part, *ys))
            far, pieces[step] = lax.optimization_barrier(
                (far, correlate(late, me, 1.0 / total, step, n_time))
            )
        sums = (part, far)
    depth = slots // 4
    part, far, piece = lax.optimization_barrier((*sums, pieces[2]))
    pieces[2] = swap(piece, "tm", 2)
    z = finish(z, (part, far), scale)
    reach = [(0, 0), (0, 1), (1, 0), (1, 1)]
    half_ring = slots // 2 * n_group
    vectors = [z] + [swap(z, WIDE, high * half_ring + low) for high, low in reach[1:]]
    copies, solved = choose(source, me, vectors, reach, depth)
    copies, beam_y, *bulk = lax.optimization_barrier(
        (copies, beam_y, pieces[1], pieces[3])
    )
    pieces[1], pieces[3] = swap(bulk[0], "tm", 1), swap(bulk[1], "tm", 3)
    pieces = [pieces[m] for m in range(n_time)]
    copies, beam_y = lax.optimization_barrier((copies, beam_y))
    groups = [
        [high * 2 * depth + 2 * i + c for i in range(depth)]
        for high in range(2)
        for c in range(2)
    ]
    line = lax.all_to_all(
        copies, "freq", split_axis=0, concat_axis=0, axis_index_groups=groups, tiled=True
    )

    line, pieces[2] = lax.optimization_barrier((line, pieces[2]))
    away = beamform(1, source, me, line, cosine, sine, beam_y, n_group)
    other = swap(away, "grp", 1)
    late, *pieces = lax.optimization_barrier((line, *pieces))
    visibilities = widen(cross(gather(pieces)))
    own = beamform(0, source, me, late, cosine, sine, beam_y, n_group)
    beams = place(me, own, other)
    return visibilities[None], solved[None], beams[None]


def solution(mesh):
    return jax.shard_map(
        body,
        mesh=mesh,
        in_specs=(
            P(None, None, ("freq", "grp"), "tm"),
            P("freq", None, None),
            P(),
            P(),
            P(),
            P(),
            P(),
            P(),
        ),
        out_specs=(
            P("freq", None, "grp", "tm"),
            P("freq", None, None),
            P("freq", None, None, "grp", "tm"),
        ),
        check_vma=False,
    )
```

```python
import functools
import math

import jax
import jax.numpy as jnp
from jax import lax
from jax.experimental import pallas as pl
from jax.experimental.pallas import tpu as pltpu
from jax.sharding import PartitionSpec as P

ITERS = 4
GRID_CELLS = 64.0
F32 = jnp.float32
BF16 = jnp.bfloat16
WIDE = ("freq", "grp")
TEAM = ("tm", "grp")
VMEM = pltpu.VMEM
SMEM = pltpu.SMEM
LONG = pl.CostEstimate(flops=40 << 30, bytes_accessed=64 << 20, transcendentals=0)


def whole(space=VMEM):
    return pl.BlockSpec(memory_space=space)


def params(mib=48):
    return pltpu.CompilerParams(vmem_limit_bytes=mib << 20)


def ingest_kernel(
    stations,
    pick,
    base_ref,
    chan_hbm,
    map_hbm,
    flag_hbm,
    volts_hbm,
    out_hbm,
    chan_ref,
    map_ref,
    flag_ref,
    volts_ref,
    out_ref,
    table_sem,
    volts_sem,
    out_sem,
):
    slots, groups, _, rows, half = out_ref.shape
    steps = out_sem.shape[0]
    per_step = slots // steps
    load = pltpu.make_async_copy(volts_hbm, volts_ref, volts_sem)
    load.start()
    tables = [
        pltpu.make_async_copy(source, target, table_sem.at[i])
        for i, (source, target) in enumerate(
            ((chan_hbm, chan_ref), (map_hbm, map_ref), (flag_hbm, flag_ref))
        )
    ]
    for copy in tables:
        copy.start()
    for copy in tables:
        copy.wait()
    line = lax.broadcasted_iota(jnp.int32, (rows, half), 0)
    keep = jnp.zeros((rows, half), F32)
    for row in range(rows):
        slot = lax.rem(base_ref[0] + row, stations)
        good = (1 - flag_ref[map_ref[slot]]).astype(F32)
        keep = jnp.where(line == row, good, keep)
    keep = keep.astype(BF16)
    load.wait()
    stores = []
    for step in range(steps):
        for slot in range(step * per_step, (step + 1) * per_step):
            for g in range(groups):
                index, cut = pick(slot, g)
                channel = chan_ref[index]
                for part in range(2):
                    piece = volts_ref[channel, part, :, cut * half : (cut + 1) * half]
                    out_ref[slot, g, part] = piece * keep
        span = pl.ds(step * per_step, per_step)
        store = pltpu.make_async_copy(out_ref.at[span], out_hbm.at[span], out_sem.at[step])
        store.start()
        stores.append(store)
    for store in stores:
        store.wait()


def ingest(voltages, channels, ingest_map, station_flags, base, groups, pick, grant):
    slots, parts, rows, samples = voltages.shape
    stations = ingest_map.shape[0]
    half = samples // 2
    shape = (slots, groups, parts, rows, half)
    steps = 8
    out = pl.pallas_call(
        functools.partial(ingest_kernel, stations, pick),
        in_specs=[whole(SMEM)] + [whole(pltpu.HBM)] * 4,
        out_specs=whole(pltpu.HBM),
        out_shape=pltpu.HBM(shape, BF16),
        scratch_shapes=[
            SMEM(channels.shape, jnp.int32),
            SMEM(ingest_map.shape, jnp.int32),
            SMEM(station_flags.shape, jnp.int32),
            VMEM(voltages.shape, BF16),
            VMEM(shape, BF16),
            pltpu.SemaphoreType.DMA((3,)),
            pltpu.SemaphoreType.DMA,
            pltpu.SemaphoreType.DMA((steps,)),
        ],
        compiler_params=params(grant),
        name="ingest",
    )(
        base,
        *(
            pltpu.with_memory_space_constraint(x, pltpu.HBM)
            for x in (channels, ingest_map, station_flags, voltages)
        ),
    )
    return out.reshape(slots * groups, parts, rows, half)


def load_part(ref, part):
    blocks, _, rows, samples = ref.shape
    return ref[:, part].reshape(blocks * rows, samples)


def nt_dot(a, b):
    return lax.dot_general(a, b, (((1,), (1,)), ((), ())), preferred_element_type=F32)


def correlate_kernel(scale, mask, me_ref, *refs):
    *y_refs, out_ref = refs
    blocks = y_refs[0].shape[0]
    _, height, width = out_ref.shape
    rows = blocks * height // (height * 2)
    cols = blocks * width // (height * 2)
    high = pl.ds(pl.multiple_of((me_ref[0] % 2) * rows, rows), rows)
    wide = pl.ds(pl.multiple_of((me_ref[2] ^ mask) * cols, cols), cols)
    samples = y_refs[0].shape[3]
    real, imag = 0.0, 0.0
    for y_ref in y_refs:
        left_r = y_ref[high, 0].reshape(height, samples)
        left_i = y_ref[high, 1].reshape(height, samples)
        right_r = y_ref[wide, 0].reshape(width, samples)
        right_i = y_ref[wide, 1].reshape(width, samples)
        real = real + nt_dot(left_r, right_r) + nt_dot(left_i, right_i)
        imag = imag + nt_dot(left_i, right_r) + nt_dot(-left_r, right_i)
    out_ref[0] = (real * scale).astype(BF16)
    out_ref[1] = (imag * scale).astype(BF16)


def correlate(ys, me, scale, mask, n_time):
    blocks, _, rows, samples = ys[0].shape
    inputs = blocks * rows
    return pl.pallas_call(
        functools.partial(correlate_kernel, scale, mask),
        in_specs=[whole(SMEM)] + [whole(VMEM)] * len(ys),
        out_specs=whole(VMEM),
        out_shape=(pltpu.VMEM if mask in (1,3,) else pltpu.HBM)(
            (2, inputs // 2, inputs // n_time), BF16
        ),
        compiler_params=params(16),
        name="correlate",
    )(me, *ys)


def gather_kernel(*refs):
    *part_refs, out_ref = refs
    pieces = [ref[...].astype(F32) for ref in part_refs]
    out_ref[...] = ((pieces[0] + pieces[1]) + (pieces[2] + pieces[3])).astype(BF16)


def gather(pieces):
    parts, rows, cols = pieces[0].shape
    steps = 2
    block = pl.BlockSpec((parts, rows // steps, cols), lambda i: (0, i, 0))
    pieces = [pltpu.with_memory_space_constraint(pieces[0], pltpu.HBM), *pieces[1:]]
    return pl.pallas_call(
        gather_kernel,
        grid=(steps,),
        in_specs=[block] * len(pieces),
        out_specs=block,
        out_shape=jax.ShapeDtypeStruct((parts, rows, cols), BF16),
        compiler_params=params(16),
        name="gather",
    )(*pieces)


def in_terms(x):
    high = x.astype(BF16).astype(F32)
    rest = x - high
    mid = rest.astype(BF16).astype(F32)
    low = rest - mid
    pad = jnp.zeros_like(x)
    return jnp.concatenate([high, mid, low, pad], axis=0).astype(BF16)


def add_terms(x):
    return x[0:2] + x[2:4] + x[4:6]


def advance(scale, z, update):
    power = jnp.sum(z * z) + 1e-06
    return 0.5 * (z + scale * update / power)


def apply_half(terms, y_ref):
    real, imag = load_part(y_ref, 0), load_part(y_ref, 1)
    a = add_terms(jnp.dot(terms, real, preferred_element_type=F32))
    b = add_terms(jnp.dot(terms, imag, preferred_element_type=F32))
    w = jnp.concatenate([a[0:1] + b[1:2], a[1:2] - b[0:1]], axis=0)
    terms = in_terms(w)
    c = add_terms(nt_dot(terms, real))
    d = add_terms(nt_dot(terms, imag))
    return jnp.concatenate([c[0:1] - d[1:2], c[1:2] + d[0:1]], axis=0)


def apply_kernel(scale, mine_ref, other_ref, z_ref, near_ref, far_ref, out_ref, fresh_ref):
    z = advance(scale, z_ref[...], near_ref[...] + far_ref[...])
    fresh_ref[...] = z
    terms = in_terms(z)
    out_ref[...] = apply_half(terms, mine_ref) + apply_half(terms, other_ref)


def apply_visibilities(ys, z, sums, scale):
    return pl.pallas_call(
        functools.partial(apply_kernel, scale),
        in_specs=[whole(VMEM)] * 5,
        out_specs=[whole(VMEM)] * 2,
        out_shape=[jax.ShapeDtypeStruct(z.shape, F32)] * 2,
        compiler_params=params(16),
        name="apply",
    )(*ys, z, *sums)


def begin_kernel(y_ref, z_ref, out_ref):
    out_ref[...] = apply_half(in_terms(z_ref[...]), y_ref)


def begin(y, z):
    return pl.pallas_call(
        begin_kernel,
        in_specs=[whole(VMEM)] * 2,
        out_specs=whole(VMEM),
        out_shape=jax.ShapeDtypeStruct(z.shape, F32),
        compiler_params=params(16),
        name="begin",
    )(y, z)


def finish_kernel(scale, z_ref, near_ref, far_ref, fresh_ref):
    fresh_ref[...] = advance(scale, z_ref[...], near_ref[...] + far_ref[...])


def finish(z, sums, scale):
    return pl.pallas_call(
        functools.partial(finish_kernel, scale),
        in_specs=[whole(VMEM)] * 3,
        out_specs=whole(VMEM),
        out_shape=jax.ShapeDtypeStruct(z.shape, F32),
        compiler_params=params(8),
        name="finish",
    )(z, *sums)


def choose_kernel(reach, source_ref, me_ref, *refs):
    *z_refs, copies_ref, solved_ref, table_ref = refs
    depth = copies_ref.shape[0]
    chip, grp = me_ref[0], me_ref[1]
    core, high_half = chip % 2, chip // (2 * depth)
    for (high, low), z_ref in zip(reach, z_refs):
        table_ref[2 * high + low] = z_ref[...]
    solved_ref[...] = table_ref[core ^ grp]
    for i in range(depth):
        slot = source_ref[high_half * 2 * depth + 2 * i + core]
        far, side = (slot // (2 * depth)) ^ high_half, (slot % 2) ^ grp
        copies_ref[i] = table_ref[2 * far + side]


def choose(source, me, vectors, reach, depth):
    shape = vectors[0].shape
    return pl.pallas_call(
        functools.partial(choose_kernel, reach),
        in_specs=[whole(SMEM)] * 2 + [whole(VMEM)] * len(reach),
        out_specs=[whole(VMEM)] * 2,
        out_shape=[
            jax.ShapeDtypeStruct((depth,) + shape, F32),
            jax.ShapeDtypeStruct(shape, F32),
        ],
        scratch_shapes=[VMEM((len(reach),) + shape, F32)],
        compiler_params=params(8),
        name="choose",
    )(source, me, *vectors)


def beam_kernel(turn, source_ref, me_ref, line_ref, cos_ref, sin_ref, y_ref, *refs):
    out_ref = refs[0] if turn else refs[1]
    slot = source_ref[me_ref[0]]
    gains = line_ref[(slot // 2) % line_ref.shape[0]]
    blocks, _, rows, samples = y_ref.shape
    stations = blocks // 2 * rows
    beams = out_ref.shape[2]
    factor = 1.0 / math.sqrt(stations)
    half = pl.ds(pl.multiple_of((me_ref[1] ^ turn) * beams, beams), beams)
    cosine, sine = cos_ref[half, :], sin_ref[half, :]
    span = pl.ds(pl.multiple_of(me_ref[1] * samples, samples), samples)
    dot = functools.partial(jnp.dot, preferred_element_type=F32)
    stores = []
    for pol in range(2):
        gain_r = gains[0:1, pol * stations : (pol + 1) * stations]
        gain_i = gains[1:2, pol * stations : (pol + 1) * stations]
        denom = jnp.maximum(gain_r * gain_r + gain_i * gain_i, 0.5)
        along_r, along_i = gain_r / denom, gain_i / denom
        y_r = y_ref[pol * blocks // 2 : (pol + 1) * blocks // 2, 0].reshape(stations, samples)
        y_i = y_ref[pol * blocks // 2 : (pol + 1) * blocks // 2, 1].reshape(stations, samples)
        w_r = ((cosine * along_r - sine * along_i) * factor).astype(BF16)
        w_i = (-(cosine * along_i + sine * along_r) * factor).astype(BF16)
        out_ref[pol, 0] = (dot(w_r, y_r) - dot(w_i, y_i)).astype(BF16)
        out_ref[pol, 1] = (dot(w_i, y_r) + dot(w_r, y_i)).astype(BF16)
        if not turn:
            store = pltpu.make_async_copy(
                out_ref.at[pol], refs[0].at[pol, :, :, span], refs[2].at[pol]
            )
            store.start()
            stores.append(store)
    for store in stores:
        store.wait()


def beamform(turn, source, me, line, cosine, sine, y, groups):
    samples = y.shape[3]
    beams = cosine.shape[0] // groups
    shape = (2, 2, beams, samples)
    if turn:
        out_spec, out_shape, scratch = whole(VMEM), jax.ShapeDtypeStruct(shape, BF16), []
    else:
        out_spec = whole(pltpu.HBM)
        out_shape = pltpu.HBM((2, 2, beams, groups * samples), BF16)
        scratch = [VMEM(shape, BF16), pltpu.SemaphoreType.DMA((2,))]
    return pl.pallas_call(
        functools.partial(beam_kernel, turn),
        in_specs=[whole(SMEM)] * 2 + [whole(VMEM)] * 4,
        out_specs=out_spec,
        out_shape=out_shape,
        scratch_shapes=scratch,
        compiler_params=params(16),
        cost_estimate=LONG,
        name="beamform",
    )(
        source,
        me,
        line,
        pltpu.with_memory_space_constraint(cosine, pltpu.HBM),
        pltpu.with_memory_space_constraint(sine, pltpu.HBM),
        y,
    )


def place_kernel(me_ref, own_hbm, other_ref, out_hbm, sem):
    samples = other_ref.shape[3]
    span = pl.ds(pl.multiple_of((1 - me_ref[1]) * samples, samples), samples)
    store = pltpu.make_async_copy(other_ref, out_hbm.at[:, :, :, span], sem)
    store.start()
    store.wait()


def place(me, own, other):
    return pl.pallas_call(
        place_kernel,
        in_specs=[whole(SMEM), whole(pltpu.HBM), whole(pl.ANY)],
        out_specs=whole(pltpu.HBM),
        out_shape=pltpu.HBM(own.shape, BF16),
        scratch_shapes=[pltpu.SemaphoreType.DMA],
        input_output_aliases={1: 0},
        compiler_params=params(8),
        name="place",
    )(me, own, other)


def widen_kernel(in_ref, out_ref):
    out_ref[...] = in_ref[...].astype(F32)


def widen(x):
    parts, rows, cols = x.shape
    steps = 2
    block = pl.BlockSpec((parts, rows // steps, cols), lambda i: (0, i, 0))
    return pl.pallas_call(
        widen_kernel,
        grid=(steps,),
        in_specs=[block],
        out_specs=block,
        out_shape=pltpu.HBM(x.shape, F32),
        compiler_params=params(8),
        name="widen",
    )(x)


def swap(x, axis, mask):
    n = lax.axis_size(axis)
    return lax.ppermute(x, axis, [(i, i ^ mask) for i in range(n)])


def cross(x):
    pairs = []
    for i in range(lax.axis_size("freq") // 2):
        for core in range(2):
            for g in range(2):
                pairs.append(((2 * i + core) * 2 + g, (2 * i + g) * 2 + core))
    return lax.ppermute(x, WIDE, pairs)


def body(
    voltages,
    prior_gains,
    station_flags,
    ingest_map,
    station_coords,
    pointing,
    corr_channels,
    beam_channels,
):
    n_freq = lax.axis_size("freq")
    n_time = lax.axis_size("tm")
    n_group = lax.axis_size("grp")
    freq_index = lax.axis_index("freq")
    group_index = lax.axis_index("grp")
    slots, _, rows, samples = voltages.shape
    stations = ingest_map.shape[0]
    inputs = 2 * stations
    total = samples * n_time

    me = jnp.stack([freq_index, group_index, lax.axis_index("tm")]).astype(jnp.int32)
    base = ((freq_index * n_group + group_index) * rows).astype(jnp.int32).reshape(1)

    corr_send = ingest(
        voltages, corr_channels, ingest_map, station_flags, base, n_group,
        lambda slot, g: (slot // 2 * 2 + g, slot % 2), 16,
    )
    corr_y = lax.all_to_all(corr_send, WIDE, split_axis=0, concat_axis=0, tiled=True)
    beam_send = ingest(
        voltages, beam_channels, ingest_map, station_flags, base, n_group,
        lambda slot, g: (slot, g), 16,
    )
    my_beam = lax.dynamic_slice_in_dim(beam_channels, freq_index, 1, 0)[0]
    ratio = 0.875 + 0.25 * (my_beam.astype(F32) + 0.5) / slots
    slot_coords = jnp.take(station_coords, ingest_map, axis=1, mode="clip")
    east = (pointing[0].astype(F32) + 0.5) / GRID_CELLS - 0.5
    north = (pointing[1].astype(F32) + 0.5) / GRID_CELLS - 0.5
    phase = (2.0 * math.pi * ratio) * (
        east[:, None] * slot_coords[0][None, :] + north[:, None] * slot_coords[1][None, :]
    )
    cosine, sine = jnp.cos(phase), jnp.sin(phase)

    z = cross(prior_gains[0])
    slot = lax.broadcasted_iota(jnp.int32, (slots, slots), 1)
    same = corr_channels[None, :] == beam_channels[:, None]
    source = jnp.sum(jnp.where(same, slot, 0), axis=1)
    beam_send, corr_y, z, cosine, sine, source, me = lax.optimization_barrier(
        (beam_send, corr_y, z, cosine, sine, source, me)
    )
    part = begin(corr_y, z)
    beam_y = lax.all_to_all(beam_send, WIDE, split_axis=0, concat_axis=0, tiled=True)

    scale = float(inputs) / total
    part = part + swap(part, "freq", 1)
    part, late = lax.optimization_barrier((part, corr_y))
    ys = [corr_y, swap(late, "freq", 1)]
    pieces = {}
    for step in range(ITERS):
        if step:
            part, z = apply_visibilities(ys, z, sums, scale)
        near = swap(part, "tm", 1)
        if step == 2:
            part, *late = lax.optimization_barrier((part, *ys))
            near, pieces[0] = lax.optimization_barrier(
                (near, correlate(late, me, 1.0 / total, 0, n_time))
            )
        part = part + near
        far = swap(part, "tm", 3)
        if step:
            part, *late = lax.optimization_barrier((part, *ys))
            far, pieces[step] = lax.optimization_barrier(
                (far, correlate(late, me, 1.0 / total, step, n_time))
            )
        sums = (part, far)
    depth = slots // 4
    part, far, piece = lax.optimization_barrier((*sums, pieces[2]))
    pieces[2] = swap(piece, "tm", 2)
    z = finish(z, (part, far), scale)
    reach = [(0, 0), (0, 1), (1, 0), (1, 1)]
    half_ring = slots // 2 * n_group
    vectors = [z] + [swap(z, WIDE, high * half_ring + low) for high, low in reach[1:]]
    copies, solved = choose(source, me, vectors, reach, depth)
    copies, beam_y, *bulk = lax.optimization_barrier(
        (copies, beam_y, pieces[1], pieces[3])
    )
    pieces[1], pieces[3] = swap(bulk[0], "tm", 1), swap(bulk[1], "tm", 3)
    pieces = [pieces[m] for m in range(n_time)]
    copies, beam_y = lax.optimization_barrier((copies, beam_y))
    groups = [
        [high * 2 * depth + 2 * i + c for i in range(depth)]
        for high in range(2)
        for c in range(2)
    ]
    line = lax.all_to_all(
        copies, "freq", split_axis=0, concat_axis=0, axis_index_groups=groups, tiled=True
    )

    line, pieces[2] = lax.optimization_barrier((line, pieces[2]))
    away = beamform(1, source, me, line, cosine, sine, beam_y, n_group)
    other = swap(away, "grp", 1)
    late, *pieces = lax.optimization_barrier((line, *pieces))
    visibilities = widen(cross(gather(pieces)))
    own = beamform(0, source, me, late, cosine, sine, beam_y, n_group)
    beams = place(me, own, other)
    return visibilities[None], solved[None], beams[None]


def solution(mesh):
    return jax.shard_map(
        body,
        mesh=mesh,
        in_specs=(
            P(None, None, ("freq", "grp"), "tm"),
            P("freq", None, None),
            P(),
            P(),
            P(),
            P(),
            P(),
            P(),
        ),
        out_specs=(
            P("freq", None, "grp", "tm"),
            P("freq", None, None),
            P("freq", None, None, "grp", "tm"),
        ),
        check_vma=False,
    )
```

```python
import functools
import math

import jax
import jax.numpy as jnp
from jax import lax
from jax.experimental import pallas as pl
from jax.experimental.pallas import tpu as pltpu
from jax.sharding import PartitionSpec as P

ITERS = 4
GRID_CELLS = 64.0
F32 = jnp.float32
BF16 = jnp.bfloat16
WIDE = ("freq", "grp")
TEAM = ("tm", "grp")
VMEM = pltpu.VMEM
SMEM = pltpu.SMEM
LONG = pl.CostEstimate(flops=40 << 30, bytes_accessed=64 << 20, transcendentals=0)


def whole(space=VMEM):
    return pl.BlockSpec(memory_space=space)


def params(mib=48):
    return pltpu.CompilerParams(vmem_limit_bytes=mib << 20)


def ingest_kernel(
    stations,
    pick,
    base_ref,
    chan_hbm,
    map_hbm,
    flag_hbm,
    volts_hbm,
    out_hbm,
    chan_ref,
    map_ref,
    flag_ref,
    volts_ref,
    out_ref,
    table_sem,
    volts_sem,
    out_sem,
):
    slots, groups, _, rows, half = out_ref.shape
    steps = out_sem.shape[0]
    per_step = slots // steps
    load = pltpu.make_async_copy(volts_hbm, volts_ref, volts_sem)
    load.start()
    tables = [
        pltpu.make_async_copy(source, target, table_sem.at[i])
        for i, (source, target) in enumerate(
            ((chan_hbm, chan_ref), (map_hbm, map_ref), (flag_hbm, flag_ref))
        )
    ]
    for copy in tables:
        copy.start()
    for copy in tables:
        copy.wait()
    line = lax.broadcasted_iota(jnp.int32, (rows, half), 0)
    keep = jnp.zeros((rows, half), F32)
    for row in range(rows):
        slot = lax.rem(base_ref[0] + row, stations)
        good = (1 - flag_ref[map_ref[slot]]).astype(F32)
        keep = jnp.where(line == row, good, keep)
    keep = keep.astype(BF16)
    load.wait()
    stores = []
    for step in range(steps):
        for slot in range(step * per_step, (step + 1) * per_step):
            for g in range(groups):
                index, cut = pick(slot, g)
                channel = chan_ref[index]
                for part in range(2):
                    piece = volts_ref[channel, part, :, cut * half : (cut + 1) * half]
                    out_ref[slot, g, part] = piece * keep
        span = pl.ds(step * per_step, per_step)
        store = pltpu.make_async_copy(out_ref.at[span], out_hbm.at[span], out_sem.at[step])
        store.start()
        stores.append(store)
    for store in stores:
        store.wait()


def ingest(voltages, channels, ingest_map, station_flags, base, groups, pick, grant):
    slots, parts, rows, samples = voltages.shape
    stations = ingest_map.shape[0]
    half = samples // 2
    shape = (slots, groups, parts, rows, half)
    steps = 8
    out = pl.pallas_call(
        functools.partial(ingest_kernel, stations, pick),
        in_specs=[whole(SMEM)] + [whole(pltpu.HBM)] * 4,
        out_specs=whole(pltpu.HBM),
        out_shape=pltpu.HBM(shape, BF16),
        scratch_shapes=[
            SMEM(channels.shape, jnp.int32),
            SMEM(ingest_map.shape, jnp.int32),
            SMEM(station_flags.shape, jnp.int32),
            VMEM(voltages.shape, BF16),
            VMEM(shape, BF16),
            pltpu.SemaphoreType.DMA((3,)),
            pltpu.SemaphoreType.DMA,
            pltpu.SemaphoreType.DMA((steps,)),
        ],
        compiler_params=params(grant),
        name="ingest",
    )(
        base,
        *(
            pltpu.with_memory_space_constraint(x, pltpu.HBM)
            for x in (channels, ingest_map, station_flags, voltages)
        ),
    )
    return out.reshape(slots * groups, parts, rows, half)


def load_part(ref, part):
    blocks, _, rows, samples = ref.shape
    return ref[:, part].reshape(blocks * rows, samples)


def nt_dot(a, b):
    return lax.dot_general(a, b, (((1,), (1,)), ((), ())), preferred_element_type=F32)


def correlate_kernel(scale, mask, me_ref, *refs):
    *y_refs, out_ref = refs
    blocks = y_refs[0].shape[0]
    _, height, width = out_ref.shape
    rows = blocks * height // (height * 2)
    cols = blocks * width // (height * 2)
    high = pl.ds(pl.multiple_of((me_ref[0] % 2) * rows, rows), rows)
    wide = pl.ds(pl.multiple_of((me_ref[2] ^ mask) * cols, cols), cols)
    samples = y_refs[0].shape[3]
    real, imag = 0.0, 0.0
    for y_ref in y_refs:
        left_r = y_ref[high, 0].reshape(height, samples)
        left_i = y_ref[high, 1].reshape(height, samples)
        right_r = y_ref[wide, 0].reshape(width, samples)
        right_i = y_ref[wide, 1].reshape(width, samples)
        real = real + nt_dot(left_r, right_r) + nt_dot(left_i, right_i)
        imag = imag + nt_dot(left_i, right_r) + nt_dot(-left_r, right_i)
    out_ref[0] = (real * scale).astype(BF16)
    out_ref[1] = (imag * scale).astype(BF16)


def correlate(ys, me, scale, mask, n_time):
    blocks, _, rows, samples = ys[0].shape
    inputs = blocks * rows
    return pl.pallas_call(
        functools.partial(correlate_kernel, scale, mask),
        in_specs=[whole(SMEM)] + [whole(VMEM)] * len(ys),
        out_specs=whole(VMEM),
        out_shape=pltpu.HBM((2, inputs // 2, inputs // n_time), BF16),
        compiler_params=params(16),
        name="correlate",
    )(me, *ys)


def gather_kernel(*refs):
    *part_refs, out_ref = refs
    pieces = [ref[...].astype(F32) for ref in part_refs]
    out_ref[...] = ((pieces[0] + pieces[1]) + (pieces[2] + pieces[3])).astype(BF16)


def gather(pieces):
    parts, rows, cols = pieces[0].shape
    steps = 2
    block = pl.BlockSpec((parts, rows // steps, cols), lambda i: (0, i, 0))
    pieces = [pltpu.with_memory_space_constraint(pieces[0], pltpu.HBM), *pieces[1:]]
    return pl.pallas_call(
        gather_kernel,
        grid=(steps,),
        in_specs=[block] * len(pieces),
        out_specs=block,
        out_shape=jax.ShapeDtypeStruct((parts, rows, cols), BF16),
        compiler_params=params(16),
        name="gather",
    )(*pieces)


def in_terms(x):
    high = x.astype(BF16).astype(F32)
    rest = x - high
    mid = rest.astype(BF16).astype(F32)
    low = rest - mid
    pad = jnp.zeros_like(x)
    return jnp.concatenate([high, mid, low, pad], axis=0).astype(BF16)


def add_terms(x):
    return x[0:2] + x[2:4] + x[4:6]


def advance(scale, z, update):
    power = jnp.sum(z * z) + 1e-06
    return 0.5 * (z + scale * update / power)


def apply_half(terms, y_ref):
    real, imag = load_part(y_ref, 0), load_part(y_ref, 1)
    a = add_terms(jnp.dot(terms, real, preferred_element_type=F32))
    b = add_terms(jnp.dot(terms, imag, preferred_element_type=F32))
    w = jnp.concatenate([a[0:1] + b[1:2], a[1:2] - b[0:1]], axis=0)
    terms = in_terms(w)
    c = add_terms(nt_dot(terms, real))
    d = add_terms(nt_dot(terms, imag))
    return jnp.concatenate([c[0:1] - d[1:2], c[1:2] + d[0:1]], axis=0)


def apply_kernel(scale, mine_ref, other_ref, z_ref, near_ref, far_ref, out_ref, fresh_ref):
    z = advance(scale, z_ref[...], near_ref[...] + far_ref[...])
    fresh_ref[...] = z
    terms = in_terms(z)
    out_ref[...] = apply_half(terms, mine_ref) + apply_half(terms, other_ref)


def apply_visibilities(ys, z, sums, scale):
    return pl.pallas_call(
        functools.partial(apply_kernel, scale),
        in_specs=[whole(VMEM)] * 5,
        out_specs=[whole(VMEM)] * 2,
        out_shape=[jax.ShapeDtypeStruct(z.shape, F32)] * 2,
        compiler_params=params(16),
        name="apply",
    )(*ys, z, *sums)


def begin_kernel(y_ref, z_ref, out_ref):
    out_ref[...] = apply_half(in_terms(z_ref[...]), y_ref)


def begin(y, z):
    return pl.pallas_call(
        begin_kernel,
        in_specs=[whole(VMEM)] * 2,
        out_specs=whole(VMEM),
        out_shape=jax.ShapeDtypeStruct(z.shape, F32),
        compiler_params=params(16),
        name="begin",
    )(y, z)


def finish_kernel(scale, z_ref, near_ref, far_ref, fresh_ref):
    fresh_ref[...] = advance(scale, z_ref[...], near_ref[...] + far_ref[...])


def finish(z, sums, scale):
    return pl.pallas_call(
        functools.partial(finish_kernel, scale),
        in_specs=[whole(VMEM)] * 3,
        out_specs=whole(VMEM),
        out_shape=jax.ShapeDtypeStruct(z.shape, F32),
        compiler_params=params(8),
        name="finish",
    )(z, *sums)


def choose_kernel(reach, source_ref, me_ref, *refs):
    *z_refs, copies_ref, solved_ref, table_ref = refs
    depth = copies_ref.shape[0]
    chip, grp = me_ref[0], me_ref[1]
    core, high_half = chip % 2, chip // (2 * depth)
    for (high, low), z_ref in zip(reach, z_refs):
        table_ref[2 * high + low] = z_ref[...]
    solved_ref[...] = table_ref[core ^ grp]
    for i in range(depth):
        slot = source_ref[high_half * 2 * depth + 2 * i + core]
        far, side = (slot // (2 * depth)) ^ high_half, (slot % 2) ^ grp
        copies_ref[i] = table_ref[2 * far + side]


def choose(source, me, vectors, reach, depth):
    shape = vectors[0].shape
    return pl.pallas_call(
        functools.partial(choose_kernel, reach),
        in_specs=[whole(SMEM)] * 2 + [whole(VMEM)] * len(reach),
        out_specs=[whole(VMEM)] * 2,
        out_shape=[
            jax.ShapeDtypeStruct((depth,) + shape, F32),
            jax.ShapeDtypeStruct(shape, F32),
        ],
        scratch_shapes=[VMEM((len(reach),) + shape, F32)],
        compiler_params=params(8),
        name="choose",
    )(source, me, *vectors)


def beam_kernel(turn, source_ref, me_ref, line_ref, cos_ref, sin_ref, y_ref, *refs):
    out_ref = refs[0] if turn else refs[1]
    slot = source_ref[me_ref[0]]
    gains = line_ref[(slot // 2) % line_ref.shape[0]]
    blocks, _, rows, samples = y_ref.shape
    stations = blocks // 2 * rows
    beams = out_ref.shape[2]
    factor = 1.0 / math.sqrt(stations)
    half = pl.ds(pl.multiple_of((me_ref[1] ^ turn) * beams, beams), beams)
    cosine, sine = cos_ref[half, :], sin_ref[half, :]
    span = pl.ds(pl.multiple_of(me_ref[1] * samples, samples), samples)
    dot = functools.partial(jnp.dot, preferred_element_type=F32)
    stores = []
    for pol in range(2):
        gain_r = gains[0:1, pol * stations : (pol + 1) * stations]
        gain_i = gains[1:2, pol * stations : (pol + 1) * stations]
        denom = jnp.maximum(gain_r * gain_r + gain_i * gain_i, 0.5)
        along_r, along_i = gain_r / denom, gain_i / denom
        y_r = y_ref[pol * blocks // 2 : (pol + 1) * blocks // 2, 0].reshape(stations, samples)
        y_i = y_ref[pol * blocks // 2 : (pol + 1) * blocks // 2, 1].reshape(stations, samples)
        w_r = ((cosine * along_r - sine * along_i) * factor).astype(BF16)
        w_i = (-(cosine * along_i + sine * along_r) * factor).astype(BF16)
        out_ref[pol, 0] = (dot(w_r, y_r) - dot(w_i, y_i)).astype(BF16)
        out_ref[pol, 1] = (dot(w_i, y_r) + dot(w_r, y_i)).astype(BF16)
        if not turn:
            store = pltpu.make_async_copy(
                out_ref.at[pol], refs[0].at[pol, :, :, span], refs[2].at[pol]
            )
            store.start()
            stores.append(store)
    for store in stores:
        store.wait()


def beamform(turn, source, me, line, cosine, sine, y, groups):
    samples = y.shape[3]
    beams = cosine.shape[0] // groups
    shape = (2, 2, beams, samples)
    if turn:
        out_spec, out_shape, scratch = whole(VMEM), jax.ShapeDtypeStruct(shape, BF16), []
    else:
        out_spec = whole(pltpu.HBM)
        out_shape = pltpu.HBM((2, 2, beams, groups * samples), BF16)
        scratch = [VMEM(shape, BF16), pltpu.SemaphoreType.DMA((2,))]
    return pl.pallas_call(
        functools.partial(beam_kernel, turn),
        in_specs=[whole(SMEM)] * 2 + [whole(VMEM)] * 4,
        out_specs=out_spec,
        out_shape=out_shape,
        scratch_shapes=scratch,
        compiler_params=params(16),
        name="beamform",
    )(source, me, line, cosine, sine, y)


def place_kernel(me_ref, own_hbm, other_ref, out_hbm, sem):
    samples = other_ref.shape[3]
    span = pl.ds(pl.multiple_of((1 - me_ref[1]) * samples, samples), samples)
    store = pltpu.make_async_copy(other_ref, out_hbm.at[:, :, :, span], sem)
    store.start()
    store.wait()


def place(me, own, other):
    return pl.pallas_call(
        place_kernel,
        in_specs=[whole(SMEM), whole(pltpu.HBM), whole(pl.ANY)],
        out_specs=whole(pltpu.HBM),
        out_shape=pltpu.HBM(own.shape, BF16),
        scratch_shapes=[pltpu.SemaphoreType.DMA],
        input_output_aliases={1: 0},
        compiler_params=params(8),
        name="place",
    )(me, own, other)


def widen_kernel(in_ref, out_ref):
    out_ref[...] = in_ref[...].astype(F32)


def widen(x):
    parts, rows, cols = x.shape
    steps = 2
    block = pl.BlockSpec((parts, rows // steps, cols), lambda i: (0, i, 0))
    return pl.pallas_call(
        widen_kernel,
        grid=(steps,),
        in_specs=[block],
        out_specs=block,
        out_shape=pltpu.HBM(x.shape, F32),
        compiler_params=params(8),
        name="widen",
    )(x)


def swap(x, axis, mask):
    n = lax.axis_size(axis)
    return lax.ppermute(x, axis, [(i, i ^ mask) for i in range(n)])


def cross(x):
    pairs = []
    for i in range(lax.axis_size("freq") // 2):
        for core in range(2):
            for g in range(2):
                pairs.append(((2 * i + core) * 2 + g, (2 * i + g) * 2 + core))
    return lax.ppermute(x, WIDE, pairs)


def body(
    voltages,
    prior_gains,
    station_flags,
    ingest_map,
    station_coords,
    pointing,
    corr_channels,
    beam_channels,
):
    n_freq = lax.axis_size("freq")
    n_time = lax.axis_size("tm")
    n_group = lax.axis_size("grp")
    freq_index = lax.axis_index("freq")
    group_index = lax.axis_index("grp")
    slots, _, rows, samples = voltages.shape
    stations = ingest_map.shape[0]
    inputs = 2 * stations
    total = samples * n_time

    me = jnp.stack([freq_index, group_index, lax.axis_index("tm")]).astype(jnp.int32)
    base = ((freq_index * n_group + group_index) * rows).astype(jnp.int32).reshape(1)

    corr_send = ingest(
        voltages, corr_channels, ingest_map, station_flags, base, n_group,
        lambda slot, g: (slot // 2 * 2 + g, slot % 2), 16,
    )
    corr_y = lax.all_to_all(corr_send, WIDE, split_axis=0, concat_axis=0, tiled=True)
    beam_send = ingest(
        voltages, beam_channels, ingest_map, station_flags, base, n_group,
        lambda slot, g: (slot, g), 16,
    )
    my_beam = lax.dynamic_slice_in_dim(beam_channels, freq_index, 1, 0)[0]
    ratio = 0.875 + 0.25 * (my_beam.astype(F32) + 0.5) / slots
    slot_coords = jnp.take(station_coords, ingest_map, axis=1, mode="clip")
    east = (pointing[0].astype(F32) + 0.5) / GRID_CELLS - 0.5
    north = (pointing[1].astype(F32) + 0.5) / GRID_CELLS - 0.5
    phase = (2.0 * math.pi * ratio) * (
        east[:, None] * slot_coords[0][None, :] + north[:, None] * slot_coords[1][None, :]
    )
    cosine, sine = jnp.cos(phase), jnp.sin(phase)

    z = cross(prior_gains[0])
    slot = lax.broadcasted_iota(jnp.int32, (slots, slots), 1)
    same = corr_channels[None, :] == beam_channels[:, None]
    source = jnp.sum(jnp.where(same, slot, 0), axis=1)
    beam_send, corr_y, z, cosine, sine, source, me = lax.optimization_barrier(
        (beam_send, corr_y, z, cosine, sine, source, me)
    )
    part = begin(corr_y, z)
    beam_y = lax.all_to_all(beam_send, WIDE, split_axis=0, concat_axis=0, tiled=True)

    scale = float(inputs) / total
    part = part + swap(part, "freq", 1)
    part, late = lax.optimization_barrier((part, corr_y))
    ys = [corr_y, swap(late, "freq", 1)]
    pieces = {}
    for step in range(ITERS):
        if step:
            part, z = apply_visibilities(ys, z, sums, scale)
        near = swap(part, "tm", 1)
        if step == 2:
            part, *late = lax.optimization_barrier((part, *ys))
            near, pieces[0] = lax.optimization_barrier(
                (near, correlate(late, me, 1.0 / total, 0, n_time))
            )
        part = part + near
        far = swap(part, "tm", 3)
        if step:
            part, *late = lax.optimization_barrier((part, *ys))
            far, pieces[step] = lax.optimization_barrier(
                (far, correlate(late, me, 1.0 / total, step, n_time))
            )
        sums = (part, far)
    depth = slots // 4
    part, far, piece = lax.optimization_barrier((*sums, pieces[2]))
    pieces[2] = swap(piece, "tm", 2)
    z = finish(z, (part, far), scale)
    reach = [(0, 0), (0, 1), (1, 0), (1, 1)]
    half_ring = slots // 2 * n_group
    vectors = [z] + [swap(z, WIDE, high * half_ring + low) for high, low in reach[1:]]
    copies, solved = choose(source, me, vectors, reach, depth)
    copies, *bulk = lax.optimization_barrier((copies, pieces[1], pieces[3]))
    pieces[1], pieces[3] = swap(bulk[0], "tm", 1), swap(bulk[1], "tm", 3)
    pieces = [pieces[m] for m in range(n_time)]
    copies, beam_y = lax.optimization_barrier((copies, beam_y))
    groups = [
        [high * 2 * depth + 2 * i + c for i in range(depth)]
        for high in range(2)
        for c in range(2)
    ]
    line = lax.all_to_all(
        copies, "freq", split_axis=0, concat_axis=0, axis_index_groups=groups, tiled=True
    )

    away = beamform(1, source, me, line, cosine, sine, beam_y, n_group)
    other = swap(away, "grp", 1)
    visibilities = widen(cross(gather(pieces)))
    own = beamform(0, source, me, line, cosine, sine, beam_y, n_group)
    beams = place(me, own, other)
    return visibilities[None], solved[None], beams[None]


def solution(mesh):
    return jax.shard_map(
        body,
        mesh=mesh,
        in_specs=(
            P(None, None, ("freq", "grp"), "tm"),
            P("freq", None, None),
            P(),
            P(),
            P(),
            P(),
            P(),
            P(),
        ),
        out_specs=(
            P("freq", None, "grp", "tm"),
            P("freq", None, None),
            P("freq", None, None, "grp", "tm"),
        ),
        check_vma=False,
    )
```

```python
import functools
import math

import jax
import jax.numpy as jnp
from jax import lax
from jax.experimental import pallas as pl
from jax.experimental.pallas import tpu as pltpu
from jax.sharding import PartitionSpec as P

ITERS = 4
GRID_CELLS = 64.0
F32 = jnp.float32
BF16 = jnp.bfloat16
WIDE = ("freq", "grp")
TEAM = ("tm", "grp")
VMEM = pltpu.VMEM
SMEM = pltpu.SMEM
LONG = pl.CostEstimate(flops=40 << 30, bytes_accessed=64 << 20, transcendentals=0)


def whole(space=VMEM):
    return pl.BlockSpec(memory_space=space)


def params(mib=48):
    return pltpu.CompilerParams(vmem_limit_bytes=mib << 20)


def ingest_kernel(
    stations,
    pick,
    base_ref,
    chan_hbm,
    map_hbm,
    flag_hbm,
    volts_hbm,
    out_hbm,
    chan_ref,
    map_ref,
    flag_ref,
    volts_ref,
    out_ref,
    table_sem,
    volts_sem,
    out_sem,
):
    slots, groups, _, rows, half = out_ref.shape
    steps = out_sem.shape[0]
    per_step = slots // steps
    load = pltpu.make_async_copy(volts_hbm, volts_ref, volts_sem)
    load.start()
    tables = [
        pltpu.make_async_copy(source, target, table_sem.at[i])
        for i, (source, target) in enumerate(
            ((chan_hbm, chan_ref), (map_hbm, map_ref), (flag_hbm, flag_ref))
        )
    ]
    for copy in tables:
        copy.start()
    for copy in tables:
        copy.wait()
    line = lax.broadcasted_iota(jnp.int32, (rows, half), 0)
    keep = jnp.zeros((rows, half), F32)
    for row in range(rows):
        slot = lax.rem(base_ref[0] + row, stations)
        good = (1 - flag_ref[map_ref[slot]]).astype(F32)
        keep = jnp.where(line == row, good, keep)
    keep = keep.astype(BF16)
    load.wait()
    stores = []
    for step in range(steps):
        for slot in range(step * per_step, (step + 1) * per_step):
            for g in range(groups):
                index, cut = pick(slot, g)
                channel = chan_ref[index]
                for part in range(2):
                    piece = volts_ref[channel, part, :, cut * half : (cut + 1) * half]
                    out_ref[slot, g, part] = piece * keep
        span = pl.ds(step * per_step, per_step)
        store = pltpu.make_async_copy(out_ref.at[span], out_hbm.at[span], out_sem.at[step])
        store.start()
        stores.append(store)
    for store in stores:
        store.wait()


def ingest(voltages, channels, ingest_map, station_flags, base, groups, pick, grant):
    slots, parts, rows, samples = voltages.shape
    stations = ingest_map.shape[0]
    half = samples // 2
    shape = (slots, groups, parts, rows, half)
    steps = 8
    out = pl.pallas_call(
        functools.partial(ingest_kernel, stations, pick),
        in_specs=[whole(SMEM)] + [whole(pltpu.HBM)] * 4,
        out_specs=whole(pltpu.HBM),
        out_shape=pltpu.HBM(shape, BF16),
        scratch_shapes=[
            SMEM(channels.shape, jnp.int32),
            SMEM(ingest_map.shape, jnp.int32),
            SMEM(station_flags.shape, jnp.int32),
            VMEM(voltages.shape, BF16),
            VMEM(shape, BF16),
            pltpu.SemaphoreType.DMA((3,)),
            pltpu.SemaphoreType.DMA,
            pltpu.SemaphoreType.DMA((steps,)),
        ],
        compiler_params=params(grant),
        name="ingest",
    )(
        base,
        *(
            pltpu.with_memory_space_constraint(x, pltpu.HBM)
            for x in (channels, ingest_map, station_flags, voltages)
        ),
    )
    return out.reshape(slots * groups, parts, rows, half)


def load_part(ref, part):
    blocks, _, rows, samples = ref.shape
    return ref[:, part].reshape(blocks * rows, samples)


def nt_dot(a, b):
    return lax.dot_general(a, b, (((1,), (1,)), ((), ())), preferred_element_type=F32)


def correlate_kernel(scale, mask, me_ref, *refs):
    *y_refs, out_ref = refs
    blocks = y_refs[0].shape[0]
    _, height, width = out_ref.shape
    rows = blocks * height // (height * 2)
    cols = blocks * width // (height * 2)
    high = pl.ds(pl.multiple_of((me_ref[0] % 2) * rows, rows), rows)
    wide = pl.ds(pl.multiple_of((me_ref[2] ^ mask) * cols, cols), cols)
    samples = y_refs[0].shape[3]
    real, imag = 0.0, 0.0
    for y_ref in y_refs:
        left_r = y_ref[high, 0].reshape(height, samples)
        left_i = y_ref[high, 1].reshape(height, samples)
        right_r = y_ref[wide, 0].reshape(width, samples)
        right_i = y_ref[wide, 1].reshape(width, samples)
        real = real + nt_dot(left_r, right_r) + nt_dot(left_i, right_i)
        imag = imag + nt_dot(left_i, right_r) + nt_dot(-left_r, right_i)
    out_ref[0] = (real * scale).astype(BF16)
    out_ref[1] = (imag * scale).astype(BF16)


def correlate(ys, me, scale, mask, n_time):
    blocks, _, rows, samples = ys[0].shape
    inputs = blocks * rows
    return pl.pallas_call(
        functools.partial(correlate_kernel, scale, mask),
        in_specs=[whole(SMEM)] + [whole(VMEM)] * len(ys),
        out_specs=whole(VMEM),
        out_shape=pltpu.HBM((2, inputs // 2, inputs // n_time), BF16),
        compiler_params=params(16),
        name="correlate",
    )(me, *ys)


def gather_kernel(*refs):
    *part_refs, out_ref = refs
    pieces = [ref[...].astype(F32) for ref in part_refs]
    out_ref[...] = ((pieces[0] + pieces[1]) + (pieces[2] + pieces[3])).astype(BF16)


def gather(pieces):
    parts, rows, cols = pieces[0].shape
    steps = 2
    block = pl.BlockSpec((parts, rows // steps, cols), lambda i: (0, i, 0))
    pieces = [pltpu.with_memory_space_constraint(pieces[0], pltpu.HBM), *pieces[1:]]
    return pl.pallas_call(
        gather_kernel,
        grid=(steps,),
        in_specs=[block] * len(pieces),
        out_specs=block,
        out_shape=jax.ShapeDtypeStruct((parts, rows, cols), BF16),
        compiler_params=params(16),
        name="gather",
    )(*pieces)


def in_terms(x):
    high = x.astype(BF16).astype(F32)
    rest = x - high
    mid = rest.astype(BF16).astype(F32)
    low = rest - mid
    pad = jnp.zeros_like(x)
    return jnp.concatenate([high, mid, low, pad], axis=0).astype(BF16)


def add_terms(x):
    return x[0:2] + x[2:4] + x[4:6]


def advance(scale, z, update):
    power = jnp.sum(z * z) + 1e-06
    return 0.5 * (z + scale * update / power)


def apply_half(terms, y_ref):
    real, imag = load_part(y_ref, 0), load_part(y_ref, 1)
    a = add_terms(jnp.dot(terms, real, preferred_element_type=F32))
    b = add_terms(jnp.dot(terms, imag, preferred_element_type=F32))
    w = jnp.concatenate([a[0:1] + b[1:2], a[1:2] - b[0:1]], axis=0)
    terms = in_terms(w)
    c = add_terms(nt_dot(terms, real))
    d = add_terms(nt_dot(terms, imag))
    return jnp.concatenate([c[0:1] - d[1:2], c[1:2] + d[0:1]], axis=0)


def apply_kernel(scale, mine_ref, other_ref, z_ref, near_ref, far_ref, out_ref, fresh_ref):
    z = advance(scale, z_ref[...], near_ref[...] + far_ref[...])
    fresh_ref[...] = z
    terms = in_terms(z)
    out_ref[...] = apply_half(terms, mine_ref) + apply_half(terms, other_ref)


def apply_visibilities(ys, z, sums, scale):
    return pl.pallas_call(
        functools.partial(apply_kernel, scale),
        in_specs=[whole(VMEM)] * 5,
        out_specs=[whole(VMEM)] * 2,
        out_shape=[jax.ShapeDtypeStruct(z.shape, F32)] * 2,
        compiler_params=params(16),
        name="apply",
    )(*ys, z, *sums)


def begin_kernel(y_ref, z_ref, out_ref):
    out_ref[...] = apply_half(in_terms(z_ref[...]), y_ref)


def begin(y, z):
    return pl.pallas_call(
        begin_kernel,
        in_specs=[whole(VMEM)] * 2,
        out_specs=whole(VMEM),
        out_shape=jax.ShapeDtypeStruct(z.shape, F32),
        compiler_params=params(16),
        name="begin",
    )(y, z)


def finish_kernel(scale, z_ref, near_ref, far_ref, fresh_ref):
    fresh_ref[...] = advance(scale, z_ref[...], near_ref[...] + far_ref[...])


def finish(z, sums, scale):
    return pl.pallas_call(
        functools.partial(finish_kernel, scale),
        in_specs=[whole(VMEM)] * 3,
        out_specs=whole(VMEM),
        out_shape=jax.ShapeDtypeStruct(z.shape, F32),
        compiler_params=params(8),
        name="finish",
    )(z, *sums)


def choose_kernel(reach, source_ref, me_ref, *refs):
    *z_refs, copies_ref, solved_ref, table_ref = refs
    depth = copies_ref.shape[0]
    chip, grp = me_ref[0], me_ref[1]
    core, high_half = chip % 2, chip // (2 * depth)
    for (high, low), z_ref in zip(reach, z_refs):
        table_ref[2 * high + low] = z_ref[...]
    solved_ref[...] = table_ref[core ^ grp]
    for i in range(depth):
        slot = source_ref[high_half * 2 * depth + 2 * i + core]
        far, side = (slot // (2 * depth)) ^ high_half, (slot % 2) ^ grp
        copies_ref[i] = table_ref[2 * far + side]


def choose(source, me, vectors, reach, depth):
    shape = vectors[0].shape
    return pl.pallas_call(
        functools.partial(choose_kernel, reach),
        in_specs=[whole(SMEM)] * 2 + [whole(VMEM)] * len(reach),
        out_specs=[whole(VMEM)] * 2,
        out_shape=[
            jax.ShapeDtypeStruct((depth,) + shape, F32),
            jax.ShapeDtypeStruct(shape, F32),
        ],
        scratch_shapes=[VMEM((len(reach),) + shape, F32)],
        compiler_params=params(8),
        name="choose",
    )(source, me, *vectors)


def beam_kernel(turn, source_ref, me_ref, line_ref, cos_ref, sin_ref, y_ref, *refs):
    out_ref = refs[0] if turn else refs[1]
    slot = source_ref[me_ref[0]]
    gains = line_ref[(slot // 2) % line_ref.shape[0]]
    blocks, _, rows, samples = y_ref.shape
    stations = blocks // 2 * rows
    beams = out_ref.shape[2]
    factor = 1.0 / math.sqrt(stations)
    half = pl.ds(pl.multiple_of((me_ref[1] ^ turn) * beams, beams), beams)
    cosine, sine = cos_ref[half, :], sin_ref[half, :]
    span = pl.ds(pl.multiple_of(me_ref[1] * samples, samples), samples)
    dot = functools.partial(jnp.dot, preferred_element_type=F32)
    stores = []
    for pol in range(2):
        gain_r = gains[0:1, pol * stations : (pol + 1) * stations]
        gain_i = gains[1:2, pol * stations : (pol + 1) * stations]
        denom = jnp.maximum(gain_r * gain_r + gain_i * gain_i, 0.5)
        along_r, along_i = gain_r / denom, gain_i / denom
        y_r = y_ref[pol * blocks // 2 : (pol + 1) * blocks // 2, 0].reshape(stations, samples)
        y_i = y_ref[pol * blocks // 2 : (pol + 1) * blocks // 2, 1].reshape(stations, samples)
        w_r = ((cosine * along_r - sine * along_i) * factor).astype(BF16)
        w_i = (-(cosine * along_i + sine * along_r) * factor).astype(BF16)
        out_ref[pol, 0] = (dot(w_r, y_r) - dot(w_i, y_i)).astype(BF16)
        out_ref[pol, 1] = (dot(w_i, y_r) + dot(w_r, y_i)).astype(BF16)
        if not turn:
            store = pltpu.make_async_copy(
                out_ref.at[pol], refs[0].at[pol, :, :, span], refs[2].at[pol]
            )
            store.start()
            stores.append(store)
    for store in stores:
        store.wait()


def beamform(turn, source, me, line, cosine, sine, y, groups):
    samples = y.shape[3]
    beams = cosine.shape[0] // groups
    shape = (2, 2, beams, samples)
    if turn:
        out_spec, out_shape, scratch = whole(VMEM), jax.ShapeDtypeStruct(shape, BF16), []
    else:
        out_spec = whole(pltpu.HBM)
        out_shape = pltpu.HBM((2, 2, beams, groups * samples), BF16)
        scratch = [VMEM(shape, BF16), pltpu.SemaphoreType.DMA((2,))]
    return pl.pallas_call(
        functools.partial(beam_kernel, turn),
        in_specs=[whole(SMEM)] * 2 + [whole(VMEM)] * 4,
        out_specs=out_spec,
        out_shape=out_shape,
        scratch_shapes=scratch,
        compiler_params=params(16),
        cost_estimate=LONG,
        name="beamform",
    )(
        source,
        me,
        line,
        pltpu.with_memory_space_constraint(cosine, pltpu.HBM),
        pltpu.with_memory_space_constraint(sine, pltpu.HBM),
        y,
    )


def place_kernel(me_ref, own_hbm, other_ref, out_hbm, sem):
    samples = other_ref.shape[3]
    span = pl.ds(pl.multiple_of((1 - me_ref[1]) * samples, samples), samples)
    store = pltpu.make_async_copy(other_ref, out_hbm.at[:, :, :, span], sem)
    store.start()
    store.wait()


def place(me, own, other):
    return pl.pallas_call(
        place_kernel,
        in_specs=[whole(SMEM), whole(pltpu.HBM), whole(pl.ANY)],
        out_specs=whole(pltpu.HBM),
        out_shape=pltpu.HBM(own.shape, BF16),
        scratch_shapes=[pltpu.SemaphoreType.DMA],
        input_output_aliases={1: 0},
        compiler_params=params(8),
        name="place",
    )(me, own, other)


def stage_kernel(in_ref, out_ref):
    out_ref[...] = in_ref[...]


def stage(y):
    blocks = y.shape[0]
    steps = 4
    spec = pl.BlockSpec((blocks // steps,) + y.shape[1:], lambda i: (i, 0, 0, 0))
    return pl.pallas_call(
        stage_kernel,
        grid=(steps,),
        in_specs=[spec],
        out_specs=spec,
        out_shape=pltpu.VMEM(y.shape, BF16),
        compiler_params=params(8),
        name="stage",
    )(y)


def widen_kernel(in_ref, out_ref):
    out_ref[...] = in_ref[...].astype(F32)


def widen(x):
    parts, rows, cols = x.shape
    steps = 2
    block = pl.BlockSpec((parts, rows // steps, cols), lambda i: (0, i, 0))
    return pl.pallas_call(
        widen_kernel,
        grid=(steps,),
        in_specs=[block],
        out_specs=block,
        out_shape=pltpu.HBM(x.shape, F32),
        compiler_params=params(8),
        name="widen",
    )(x)


def swap(x, axis, mask):
    n = lax.axis_size(axis)
    return lax.ppermute(x, axis, [(i, i ^ mask) for i in range(n)])


def cross(x):
    pairs = []
    for i in range(lax.axis_size("freq") // 2):
        for core in range(2):
            for g in range(2):
                pairs.append(((2 * i + core) * 2 + g, (2 * i + g) * 2 + core))
    return lax.ppermute(x, WIDE, pairs)


def body(
    voltages,
    prior_gains,
    station_flags,
    ingest_map,
    station_coords,
    pointing,
    corr_channels,
    beam_channels,
):
    n_freq = lax.axis_size("freq")
    n_time = lax.axis_size("tm")
    n_group = lax.axis_size("grp")
    freq_index = lax.axis_index("freq")
    group_index = lax.axis_index("grp")
    slots, _, rows, samples = voltages.shape
    stations = ingest_map.shape[0]
    inputs = 2 * stations
    total = samples * n_time

    me = jnp.stack([freq_index, group_index, lax.axis_index("tm")]).astype(jnp.int32)
    base = ((freq_index * n_group + group_index) * rows).astype(jnp.int32).reshape(1)

    corr_send = ingest(
        voltages, corr_channels, ingest_map, station_flags, base, n_group,
        lambda slot, g: (slot // 2 * 2 + g, slot % 2), 16,
    )
    corr_y = lax.all_to_all(corr_send, WIDE, split_axis=0, concat_axis=0, tiled=True)
    beam_send = ingest(
        voltages, beam_channels, ingest_map, station_flags, base, n_group,
        lambda slot, g: (slot, g), 16,
    )
    my_beam = lax.dynamic_slice_in_dim(beam_channels, freq_index, 1, 0)[0]
    ratio = 0.875 + 0.25 * (my_beam.astype(F32) + 0.5) / slots
    slot_coords = jnp.take(station_coords, ingest_map, axis=1, mode="clip")
    east = (pointing[0].astype(F32) + 0.5) / GRID_CELLS - 0.5
    north = (pointing[1].astype(F32) + 0.5) / GRID_CELLS - 0.5
    phase = (2.0 * math.pi * ratio) * (
        east[:, None] * slot_coords[0][None, :] + north[:, None] * slot_coords[1][None, :]
    )
    cosine, sine = jnp.cos(phase), jnp.sin(phase)

    z = cross(prior_gains[0])
    slot = lax.broadcasted_iota(jnp.int32, (slots, slots), 1)
    same = corr_channels[None, :] == beam_channels[:, None]
    source = jnp.sum(jnp.where(same, slot, 0), axis=1)
    beam_send, corr_y, z, cosine, sine, source, me = lax.optimization_barrier(
        (beam_send, corr_y, z, cosine, sine, source, me)
    )
    part = begin(corr_y, z)
    beam_y = lax.all_to_all(beam_send, WIDE, split_axis=0, concat_axis=0, tiled=True)

    scale = float(inputs) / total
    part = part + swap(part, "freq", 1)
    part, late = lax.optimization_barrier((part, corr_y))
    ys = [corr_y, swap(late, "freq", 1)]
    pieces = {}
    for step in range(ITERS):
        if step:
            part, z = apply_visibilities(ys, z, sums, scale)
        near = swap(part, "tm", 1)
        if step == 2:
            part, *late = lax.optimization_barrier((part, *ys))
            near, pieces[0] = lax.optimization_barrier(
                (near, correlate(late, me, 1.0 / total, 0, n_time))
            )
        part = part + near
        far = swap(part, "tm", 3)
        if step:
            part, *late = lax.optimization_barrier((part, *ys))
            far, pieces[step] = lax.optimization_barrier(
                (far, correlate(late, me, 1.0 / total, step, n_time))
            )
        sums = (part, far)
    depth = slots // 4
    part, far, piece = lax.optimization_barrier((*sums, pieces[2]))
    pieces[2] = swap(piece, "tm", 2)
    z = finish(z, (part, far), scale)
    reach = [(0, 0), (0, 1), (1, 0), (1, 1)]
    half_ring = slots // 2 * n_group
    vectors = [z] + [swap(z, WIDE, high * half_ring + low) for high, low in reach[1:]]
    copies, solved = choose(source, me, vectors, reach, depth)
    copies, beam_y, *bulk = lax.optimization_barrier(
        (copies, beam_y, pieces[1], pieces[3])
    )
    pieces[1], pieces[3] = swap(bulk[0], "tm", 1), swap(bulk[1], "tm", 3)
    pieces = [pieces[m] for m in range(n_time)]
    copies, beam_y = lax.optimization_barrier((copies, beam_y))
    groups = [
        [high * 2 * depth + 2 * i + c for i in range(depth)]
        for high in range(2)
        for c in range(2)
    ]
    line = lax.all_to_all(
        copies, "freq", split_axis=0, concat_axis=0, axis_index_groups=groups, tiled=True
    )

    beam_y = stage(beam_y)
    line, pieces[2], beam_y = lax.optimization_barrier((line, pieces[2], beam_y))
    away = beamform(1, source, me, line, cosine, sine, beam_y, n_group)
    other = swap(away, "grp", 1)
    late, *pieces = lax.optimization_barrier((line, *pieces))
    visibilities = widen(cross(gather(pieces)))
    own = beamform(0, source, me, late, cosine, sine, beam_y, n_group)
    beams = place(me, own, other)
    return visibilities[None], solved[None], beams[None]


def solution(mesh):
    return jax.shard_map(
        body,
        mesh=mesh,
        in_specs=(
            P(None, None, ("freq", "grp"), "tm"),
            P("freq", None, None),
            P(),
            P(),
            P(),
            P(),
            P(),
            P(),
        ),
        out_specs=(
            P("freq", None, "grp", "tm"),
            P("freq", None, None),
            P("freq", None, None, "grp", "tm"),
        ),
        check_vma=False,
    )
```
